256 devices in a mesh: seq: 64 (over y, z_lo, x), tp: 4 (over z_hi, core).
Axes of the slice: x: 4, y: 4, z: 8 (z_hi: 2, z_lo: 4; z = z_hi * 4 + z_lo), core: 2. Of those that a mesh axis runs over, the one named last changes fastest.
Arguments:
- tokens: bfloat16 [32768, 5376], P(('seq', 'tp')), may hold values from -180 to 180
- in_gain: float32 [5376], replicated, may hold values from 0.5 to 1.5
- raw_queries: bfloat16 [32768, 2048], P('seq', 'tp'), may hold values from -6 to 6
- w_key: bfloat16 [5376, 1024], P(None, 'tp'), may hold values from -0.078125 to 0.078125
- w_value: bfloat16 [5376, 1024], P(None, 'tp'), may hold values from -0.078125 to 0.078125
- q_gain: float32 [128], replicated, may hold values from 0.5 to 1.5
- k_gain: float32 [128], replicated, may hold values from 0.5 to 1.5
- doc_lengths: int32 [32], replicated, may hold values from 1 to 4096, as said below
- out_grad: bfloat16 [32768, 2048], P('seq', 'tp'), may hold values from -60 to 60
Outputs:
- grad_x: bfloat16 [32768, 5376], P(('seq', 'tp'))
- grad_queries: bfloat16 [32768, 2048], P('seq', 'tp')
- grad_wk: float32 [5376, 1024], P('seq', 'tp')
- grad_wv: float32 [5376, 1024], P('seq', 'tp')
The draws below stay inside these ranges and needn't reach their ends.
Inputs may be any that keep to these rules, and one draw needn't show every extreme that they name: `doc_lengths`: the 32 lengths sum to 32768; the last rollout is the longest, exactly 4096 tokens.
All inputs are finite; a program needn't handle non-finite values.
Results may differ from the reference program's by a relative error of at most 0.014.
Values may be sent and summed in bfloat16 or wider, within the bound.
A program may use at most 128 MiB of HBM per device.

```python
import math
import jax
import jax.numpy as jnp
from jax import lax

D = 5376
HD = 128
QH = 16
KVH = 8
WINDOW = 1024
TOK_DEV = 512
TOKENS = 32768
NDOCS = 32
MAXDOC = 4096
N_TP = 4


def draw_tokens(key, part):
    key_base, key_rows, key_cols = jax.random.split(key, 3)
    row_scale = jnp.exp(jax.random.uniform(key_rows, (TOKENS, 1), jnp.float32, 0.0, math.log(10.0)))
    col_scale = jnp.exp(jax.random.uniform(key_cols, (1, D), jnp.float32, math.log(0.3), math.log(3.0)))
    base = jnp.clip(jax.random.normal(key_base, (TOKENS, D), jnp.float32), -6.0, 6.0)
    return (base * row_scale * col_scale).astype(jnp.bfloat16)


def draw_doc_lengths(key, part):
    other_count = NDOCS - 1
    remaining = TOKENS - MAXDOC
    even_length = remaining // other_count
    leftover = remaining % other_count
    key_moves, key_order = jax.random.split(jax.random.fold_in(key, 7), 2)
    order_index = jnp.arange(other_count, dtype=jnp.int32)
    lengths = even_length + (order_index < leftover).astype(jnp.int32)
    moves = jax.random.randint(key_moves, (other_count,), 0, even_length, jnp.int32)
    pair_moves = jnp.take(moves, order_index // 2)
    paired = order_index // 2 * 2 + 1 < other_count
    signs = jnp.where(order_index % 2 == 0, 1, -1).astype(jnp.int32)
    lengths = lengths + jnp.where(paired, signs * pair_moves, jnp.zeros_like(pair_moves))
    shuffled = jax.random.permutation(key_order, other_count)
    lengths = jnp.take(lengths, shuffled)
    return jnp.concatenate([lengths, jnp.full((1,), MAXDOC, jnp.int32)]).astype(jnp.int32)


def steps_of(rng, shape, cuts, low, top_value):
    factor_of = 1.0
    for dim, shards_of in cuts:
        heights = jax.random.uniform(jax.random.fold_in(jax.random.fold_in(rng, 6), dim), (shards_of,), jnp.float32, low / len(cuts), top_value / len(cuts))
        factor_of = factor_of * jnp.repeat(jnp.exp(heights), shape[dim] // shards_of).reshape((-1,) + (1,) * (len(shape) - 1 - dim))
    return factor_of


def gaussian(own_key, dims, deviation, most, pieces=(), held_as=jnp.bfloat16):
    loudness = steps_of(own_key, dims, pieces, -0.22, 0.18) if pieces else 1.0
    result = jax.random.normal(own_key, dims, jnp.float32) * deviation * loudness
    return jnp.minimum(jnp.maximum(result, -most), most).astype(held_as)


def setup_inputs(seed: int = 0) -> dict:
    arg_keys = jax.random.split(jax.random.key(seed), 10)
    tokens = draw_tokens(jax.random.fold_in(arg_keys[9], 71), 0)
    in_gain = jnp.clip(1.0 + 0.1 * jax.random.normal(arg_keys[1], (D,), jnp.float32), 0.5, 1.5)
    raw_queries = gaussian(arg_keys[2], (TOKENS, QH * HD), 1.0, 6.0, ((0, 64), (1, 4)))
    w_key = gaussian(arg_keys[3], (D, KVH * HD), D ** -0.5, 0.078125, ((1, 4),))
    w_value = gaussian(arg_keys[4], (D, KVH * HD), D ** -0.5, 0.078125, ((1, 4),))
    q_gain = jnp.clip(1.0 + 0.1 * jax.random.normal(arg_keys[5], (HD,), jnp.float32), 0.5, 1.5)
    k_gain = jnp.clip(1.0 + 0.1 * jax.random.normal(arg_keys[6], (HD,), jnp.float32), 0.5, 1.5)
    doc_lengths = draw_doc_lengths(jax.random.fold_in(arg_keys[9], 71), 0)
    out_grad = gaussian(arg_keys[8], (TOKENS, QH * HD), 10.0, 60.0, ((0, 64), (1, 4)))
    return {"tokens": tokens, "in_gain": in_gain, "raw_queries": raw_queries, "w_key": w_key, "w_value": w_value, "q_gain": q_gain, "k_gain": k_gain, "doc_lengths": doc_lengths, "out_grad": out_grad}


EPSILON = 1e-06
QUERY_SCALE = 168.0 ** (-0.5)
ROPE_BASE = 10000.0

def doc_begin(doc_lengths, positions):
    endings = jnp.cumsum(doc_lengths, dtype=jnp.int32)
    starts = endings - doc_lengths
    inside = starts[None, :] <= positions[:, None]
    return lax.optimization_barrier(jnp.max(jnp.where(inside, starts[None, :], jnp.zeros_like(starts)[None, :]), axis=1))

def input_norm(values, gain):
    return values * lax.rsqrt(lax.optimization_barrier(jnp.mean(values * values, axis=1, keepdims=True)) + EPSILON) * gain

def head_norm(values, gain):
    return values * lax.rsqrt(lax.optimization_barrier(jnp.mean(values * values, axis=-1, keepdims=True)) + EPSILON) * gain

def rotate(values, positions):
    half_size = values.shape[-1] // 2
    powers = jnp.arange(half_size, dtype=jnp.float32) * (2.0 / values.shape[-1])
    frequency = ROPE_BASE ** (-powers)
    angles = positions.astype(jnp.float32)[:, None] * frequency[None, :]
    cosine = jnp.cos(angles)[:, None, :]
    sine = jnp.sin(angles)[:, None, :]
    first = values[..., :half_size]
    second = values[..., half_size:]
    return jnp.concatenate([first * cosine - second * sine, second * cosine + first * sine], axis=-1)

def contract_last(left, right):
    return lax.dot_general(left, right, (((1,), (1,)), ((), ())), preferred_element_type=jnp.float32)

def contract_first(left, right):
    return lax.dot_general(left, right, (((0,), (0,)), ((), ())), preferred_element_type=jnp.float32)

def attend(queries, key_rows, value_rows, grads, lowest, positions, key_positions):
    query_float = queries.astype(jnp.float32)
    key_float = key_rows.astype(jnp.float32)
    value_float = value_rows.astype(jnp.float32)
    grad_float = grads.astype(jnp.float32)
    scores = jnp.einsum('qkgd,skd->kgqs', query_float, key_float)
    allowed = (key_positions[None, :] >= lowest[:, None]) & (key_positions[None, :] <= positions[:, None])
    exps = jnp.where(allowed[None, None], jnp.exp(scores), jnp.zeros_like(scores))
    totals = lax.optimization_barrier(jnp.sum(exps, axis=-1, keepdims=True))
    probs = exps / totals
    rounded = lax.optimization_barrier(probs.astype(jnp.bfloat16)).astype(jnp.float32)
    outputs = jnp.einsum('kgqs,skd->qkgd', rounded, value_float)
    deltas = lax.optimization_barrier(jnp.sum(grad_float * outputs, axis=-1))
    along = jnp.einsum('qkgd,skd->kgqs', grad_float, value_float)
    slopes = probs * (along - jnp.transpose(deltas, (1, 2, 0))[..., None])
    slopes = lax.optimization_barrier(slopes.astype(jnp.bfloat16)).astype(jnp.float32)
    query_grad = jnp.einsum('kgqs,skd->qkgd', slopes, key_float)
    key_grad = jnp.einsum('kgqs,qkgd->skd', slopes, query_float)
    value_grad = jnp.einsum('kgqs,qkgd->skd', rounded, grad_float)
    return (query_grad, key_grad, value_grad)

def reference(tokens, in_gain, raw_queries, w_key, w_value, q_gain, k_gain, doc_lengths, out_grad):
    head_size = q_gain.shape[0]
    kv_heads = w_key.shape[1] // head_size
    group_size = raw_queries.shape[1] // w_key.shape[1]
    total_rows = tokens.shape[0]
    reach_count = (WINDOW - 2) // TOK_DEV + 1
    x_float = tokens.astype(jnp.float32)
    normed_rows = input_norm(x_float, in_gain).astype(jnp.bfloat16)
    positions = jnp.arange(total_rows, dtype=jnp.int32)
    begins = doc_begin(doc_lengths, positions)
    offsets = positions - begins
    lowest = jnp.maximum(begins, positions - (WINDOW - 1))
    queries = raw_queries.astype(jnp.float32).reshape(total_rows, -1, head_size)
    keys_raw = jnp.dot(normed_rows, w_key, preferred_element_type=jnp.float32).reshape(total_rows, -1, head_size)
    values_raw = jnp.dot(normed_rows, w_value, preferred_element_type=jnp.float32).reshape(total_rows, -1, head_size)

    def query_map(values):
        return rotate(head_norm(values, q_gain), offsets) * QUERY_SCALE

    def key_map(values):
        return rotate(head_norm(values, k_gain), offsets)
    query_rot, query_back = jax.vjp(query_map, queries)
    key_rot, key_back = jax.vjp(key_map, keys_raw)
    query_rows = query_rot.astype(jnp.bfloat16).reshape(total_rows, kv_heads, group_size, head_size)
    key_rows = key_rot.astype(jnp.bfloat16)
    value_rows = values_raw.astype(jnp.bfloat16)
    grad_rows = out_grad.reshape(total_rows, kv_heads, group_size, head_size)
    margin = reach_count * TOK_DEV
    window_rows = margin + TOK_DEV
    key_padded = jnp.concatenate([jnp.zeros((margin, kv_heads, head_size), jnp.bfloat16), key_rows], axis=0)
    value_padded = jnp.concatenate([jnp.zeros((margin, kv_heads, head_size), jnp.bfloat16), value_rows], axis=0)

    def block_step(carry, block_index):
        key_accum, value_accum = carry
        start = (block_index * TOK_DEV).astype(jnp.int32)
        query_block = lax.dynamic_slice_in_dim(query_rows, start, TOK_DEV, 0)
        grad_block = lax.dynamic_slice_in_dim(grad_rows, start, TOK_DEV, 0)
        key_block = lax.dynamic_slice_in_dim(key_padded, start, window_rows, 0)
        value_block = lax.dynamic_slice_in_dim(value_padded, start, window_rows, 0)
        block_positions = lax.dynamic_slice_in_dim(positions, start, TOK_DEV, 0)
        block_lowest = lax.dynamic_slice_in_dim(lowest, start, TOK_DEV, 0)
        key_positions = start - margin + jnp.arange(window_rows, dtype=jnp.int32)
        query_grad, key_grad, value_grad = attend(query_block, key_block, value_block, grad_block, block_lowest, block_positions, key_positions)
        key_accum = lax.dynamic_update_slice_in_dim(key_accum, lax.dynamic_slice_in_dim(key_accum, start, window_rows, 0) + key_grad, start, 0)
        value_accum = lax.dynamic_update_slice_in_dim(value_accum, lax.dynamic_slice_in_dim(value_accum, start, window_rows, 0) + value_grad, start, 0)
        return ((key_accum, value_accum), query_grad)
    empty = jnp.zeros((total_rows + margin, kv_heads, head_size), jnp.float32)
    (key_accum, value_accum), query_grads = lax.scan(block_step, (empty, empty), jnp.arange(total_rows // TOK_DEV, dtype=jnp.int32))
    query_grad = query_grads.reshape(total_rows, kv_heads * group_size, head_size)
    key_grad = key_accum[margin:]
    value_grad = value_accum[margin:]
    grad_queries = query_back(query_grad)[0].reshape(total_rows, -1).astype(jnp.bfloat16)
    grad_k = key_back(key_grad)[0].reshape(total_rows, -1).astype(jnp.bfloat16)
    grad_v = value_grad.reshape(total_rows, -1).astype(jnp.bfloat16)
    kv_cols = w_key.shape[1] // N_TP
    summed = jnp.zeros(tokens.shape, jnp.float32)
    for member in range(N_TP):
        k_lo = member * kv_cols
        partial_sum = contract_last(grad_k[:, k_lo:k_lo + kv_cols], w_key[:, k_lo:k_lo + kv_cols])
        partial_sum = partial_sum + contract_last(grad_v[:, k_lo:k_lo + kv_cols], w_value[:, k_lo:k_lo + kv_cols])
        summed = summed + lax.optimization_barrier(partial_sum.astype(jnp.bfloat16)).astype(jnp.float32)

    def norm_map(values):
        return input_norm(values, in_gain)
    unused_rows, norm_back = jax.vjp(norm_map, x_float)
    grad_x = norm_back(summed)[0].astype(jnp.bfloat16)
    grad_wk = contract_first(normed_rows, grad_k)
    grad_wv = contract_first(normed_rows, grad_v)
    return (grad_x, grad_queries, grad_wk, grad_wv)
```

```python
import jax
import jax.numpy as jnp
from jax import lax
from jax.experimental import pallas as pl
from jax.experimental.pallas import tpu as pltpu
from jax.sharding import PartitionSpec as P

WINDOW = 1024


EPSILON = 1e-06
QUERY_SCALE = 168.0 ** (-0.5)
ROPE_BASE = 10000.0


def from_behind(array, axis, by):
    size = lax.axis_size(axis)
    pairs = [(i, i + by) for i in range(size) if 0 <= i + by < size]
    return lax.ppermute(array, axis, pairs)


def doc_begin(doc_lengths, positions):
    endings = jnp.cumsum(doc_lengths, dtype=jnp.int32)
    starts = endings - doc_lengths
    inside = starts[None, :] <= positions[:, None]
    return jnp.max(jnp.where(inside, starts[None, :], jnp.zeros_like(starts)[None, :]), axis=1)


def input_norm(values, gain):
    return values * lax.rsqrt(jnp.mean(values * values, axis=1, keepdims=True) + EPSILON) * gain


def head_norm(values, gain):
    return values * lax.rsqrt(jnp.mean(values * values, axis=-1, keepdims=True) + EPSILON) * gain


def rotate(values, positions):
    half_size = values.shape[-1] // 2
    powers = jnp.arange(half_size, dtype=jnp.float32) * (2.0 / values.shape[-1])
    frequency = ROPE_BASE ** (-powers)
    angles = positions.astype(jnp.float32)[:, None] * frequency[None, :]
    cosine = jnp.cos(angles)[:, None, :]
    sine = jnp.sin(angles)[:, None, :]
    first = values[..., :half_size]
    second = values[..., half_size:]
    return jnp.concatenate(
        [first * cosine - second * sine, second * cosine + first * sine], axis=-1
    )


def contract_last(left, right):
    return lax.dot_general(
        left, right, (((1,), (1,)), ((), ())), preferred_element_type=jnp.float32
    )


def contract_first(left, right):
    return lax.dot_general(
        left, right, (((0,), (0,)), ((), ())), preferred_element_type=jnp.float32
    )


def attend(queries, key_rows, value_rows, grads, lowest, positions, key_positions):
    scores = jnp.einsum("qkgd,skd->kgqs", queries, key_rows, preferred_element_type=jnp.float32)
    allowed = (key_positions[None, :] >= lowest[:, None]) & (
        key_positions[None, :] <= positions[:, None]
    )
    exps = jnp.where(allowed[None, None], jnp.exp(scores), jnp.zeros_like(scores))
    totals = jnp.sum(exps, axis=-1, keepdims=True)
    probs = exps / totals
    rounded = probs.astype(jnp.bfloat16)
    outputs = jnp.einsum("kgqs,skd->qkgd", rounded, value_rows, preferred_element_type=jnp.float32)
    deltas = jnp.sum(grads.astype(jnp.float32) * outputs, axis=-1)
    along = jnp.einsum("qkgd,skd->kgqs", grads, value_rows, preferred_element_type=jnp.float32)
    slopes = (probs * (along - jnp.transpose(deltas, (1, 2, 0))[..., None])).astype(jnp.bfloat16)
    query_grad = jnp.einsum("kgqs,skd->qkgd", slopes, key_rows, preferred_element_type=jnp.float32)
    key_grad = jnp.einsum("kgqs,qkgd->skd", slopes, queries, preferred_element_type=jnp.float32)
    value_grad = jnp.einsum("kgqs,qkgd->skd", rounded, grads, preferred_element_type=jnp.float32)
    return (query_grad, key_grad, value_grad)


MESH_IDS = pl.DeviceIdType.MESH


def ring_sum(piece, size, split, pos, up, down, bufs, sems, finish):
    half_up, half_down, mixed_up, mixed_down, full_up, full_down = bufs
    send_sem, recv_sem = sems
    far = lax.rem(pos + 2, 4)
    after = lax.rem(pos + 1, 4)
    before = lax.rem(pos + 3, 4)
    low = pl.ds(0, split)
    high = pl.ds(split, size - split)

    def copy(index, source, target, device):
        return pltpu.make_async_remote_copy(
            src_ref=source,
            dst_ref=target,
            send_sem=send_sem.at[index],
            recv_sem=recv_sem.at[index],
            device_id=device,
            device_id_type=MESH_IDS,
        )

    first = [
        copy(0, piece(far).at[low], half_up, up),
        copy(1, piece(far).at[high], half_down, down),
        copy(2, piece(after).at[high], full_up.at[high], up),
        copy(3, piece(before).at[low], full_down.at[low], down),
    ]
    for one in first:
        one.start()

    def second():
        first[0].wait_recv()
        mixed_up[...] = (
            piece(after)[low, :].astype(jnp.float32) + half_up[...].astype(jnp.float32)
        ).astype(jnp.bfloat16)
        last_up = copy(4, mixed_up, full_up.at[low], up)
        last_up.start()
        first[1].wait_recv()
        mixed_down[...] = (
            piece(before)[high, :].astype(jnp.float32) + half_down[...].astype(jnp.float32)
        ).astype(jnp.bfloat16)
        last_down = copy(5, mixed_down, full_down.at[high], down)
        last_down.start()

        def third():
            first[2].wait_recv()
            first[3].wait_recv()
            last_up.wait_recv()
            last_down.wait_recv()
            finish(
                lambda rows: piece(pos)[rows, :].astype(jnp.float32)
                + full_up[rows, :].astype(jnp.float32)
                + full_down[rows, :].astype(jnp.float32)
            )

            def drain():
                for one in first + [last_up, last_down]:
                    one.wait_send()

            return drain

        return third

    return second


def weight_sum_kernel(
    key_ref, value_ref, key_out, value_out,
    key_send, order, value_total, key_next, value_next, last_send, last_recv,
    *rest,
):
    bufs_a, bufs_b, bufs_c, bufs_d = rest[0:6], rest[6:12], rest[12:18], rest[18:24]
    sems = rest[24:]
    rows = key_out.shape[0]
    cols = key_out.shape[1]
    big, mid = 16 * rows, 4 * rows
    split_big = big // 2
    split_mid = mid // 2 + mid // 2 % 16
    place = lax.axis_index("seq")
    member = lax.axis_index("tp")
    x = lax.rem(place, 4)
    z = lax.rem(place // 4, 4)
    y = place // 16

    def device(ys, zs, xs):
        return ((ys * 4 + zs) * 4 + xs, member)

    x_up, x_down = device(y, z, lax.rem(x + 1, 4)), device(y, z, lax.rem(x + 3, 4))
    y_up, y_down = device(lax.rem(y + 1, 4), z, x), device(lax.rem(y + 3, 4), z, x)
    z_others = [device(y, lax.rem(z + d, 4), x) for d in (1, 2, 3)]
    barrier = pltpu.get_barrier_semaphore()
    for other in [x_up, x_down, y_up, y_down] + z_others:
        pl.semaphore_signal(barrier, inc=1, device_id=other, device_id_type=MESH_IDS)

    pl.semaphore_wait(barrier, 7)

    def finish_b1(total):
        for part in range(4):
            at = pl.ds(part * mid, mid)
            value_total[at, :] = total(at)
        for xs in range(4):
            for zs in range(4):
                order[zs * rows : zs * rows + rows, :] = value_total[
                    zs * mid + xs * rows : zs * mid + xs * rows + rows, :
                ]
            value_next[xs] = order[...].astype(jnp.bfloat16)

    second_b = ring_sum(
        lambda t: value_ref.at[pl.ds(pl.multiple_of(t * big, 16), big)],
        big, split_big, y, y_up, y_down, bufs_b, sems[2:4], finish_b1,
    )

    for ys in range(4):
        for xs in range(4):
            for zs in range(4):
                begin = ((ys * 4 + zs) * 4 + xs) * rows
                order[zs * rows : zs * rows + rows, :] = key_ref[begin : begin + rows, :]
            key_send[xs, ys * mid : ys * mid + mid, :] = order[...].astype(jnp.bfloat16)

    def finish_a1(total):
        for part in range(4):
            at = pl.ds(part * mid, mid)
            key_next[part] = total(at).astype(jnp.bfloat16)

    second_a = ring_sum(
        lambda t: key_send.at[t],
        big, split_big, x, x_up, x_down, bufs_a, sems[0:2], finish_a1,
    )
    third_b = second_b()
    third_a = second_a()
    drain_b = third_b()

    def finish_last(at):
        def finish(total):
            order[...] = total(pl.ds(0, mid))
            for zs in range(4):
                last_send[zs, 0:rows, at : at + cols] = order[
                    zs * rows : zs * rows + rows, :
                ].astype(jnp.bfloat16)
                last_send[zs, rows:, at : at + cols] = jnp.zeros(
                    (last_send.shape[1] - rows, cols), jnp.bfloat16
                )

        return finish

    second_d = ring_sum(
        lambda t: value_next.at[t],
        mid, split_mid, x, x_up, x_down, bufs_d, sems[6:8], finish_last(cols),
    )
    drain_a = third_a()
    second_c = ring_sum(
        lambda t: key_next.at[t],
        mid, split_mid, y, y_up, y_down, bufs_c, sems[4:6], finish_last(0),
    )
    third_d = second_d()
    third_c = second_c()
    drain_d = third_d()
    drain_c = third_c()
    copies = []
    for d in (1, 2, 3):
        one = pltpu.make_async_remote_copy(
            src_ref=last_send.at[lax.rem(z + d, 4)],
            dst_ref=last_recv.at[d - 1],
            send_sem=sems[8].at[d - 1],
            recv_sem=sems[9].at[d - 1],
            device_id=z_others[d - 1],
            device_id_type=MESH_IDS,
        )
        one.start()
        copies.append(one)
    for one in copies:
        one.wait_recv()
    total = last_send[z, 0:rows, :].astype(jnp.float32)
    for d in range(3):
        total = total + last_recv[d, 0:rows, :].astype(jnp.float32)
    key_out[...] = total[:, 0:cols]
    value_out[...] = total[:, cols:]
    for one in copies:
        one.wait_send()
    for drain in (drain_a, drain_b, drain_c, drain_d):
        drain()


def weight_sum(key_term, value_term):
    depth, cols = key_term.shape
    rows = depth // 64
    big, mid = 16 * rows, 4 * rows
    split_big = big // 2
    split_mid = mid // 2 + mid // 2 % 16
    padded = (rows + 15) // 16 * 16
    bf = jnp.bfloat16

    def bufs(size, split):
        return [
            pltpu.VMEM((split, cols), bf),
            pltpu.VMEM((size - split, cols), bf),
            pltpu.VMEM((split, cols), bf),
            pltpu.VMEM((size - split, cols), bf),
            pltpu.VMEM((size, cols), bf),
            pltpu.VMEM((size, cols), bf),
        ]

    return pl.pallas_call(
        weight_sum_kernel,
        out_shape=[jax.ShapeDtypeStruct((rows, cols), jnp.float32)] * 2,
        in_specs=[pl.BlockSpec(memory_space=pltpu.VMEM)] * 2,
        out_specs=[pl.BlockSpec(memory_space=pltpu.VMEM)] * 2,
        scratch_shapes=[
            pltpu.VMEM((4, big, cols), bf),
            pltpu.VMEM((mid, cols), jnp.float32),
            pltpu.VMEM((big, cols), jnp.float32),
            pltpu.VMEM((4, mid, cols), bf),
            pltpu.VMEM((4, mid, cols), bf),
            pltpu.VMEM((4, padded, 2 * cols), bf),
            pltpu.VMEM((3, padded, 2 * cols), bf),
        ]
        + bufs(big, split_big)
        + bufs(big, split_big)
        + bufs(mid, split_mid)
        + bufs(mid, split_mid)
        + [pltpu.SemaphoreType.DMA((6,))] * 8
        + [pltpu.SemaphoreType.DMA((3,))] * 2,
        compiler_params=pltpu.CompilerParams(
            collective_id=1, has_side_effects=True, vmem_limit_bytes=40 * 1024 * 1024
        ),
        cost_estimate=pl.CostEstimate(
            flops=100_000_000, bytes_accessed=150_000_000, transcendentals=0
        ),
        name="weight_sum",
    )(key_term, value_term)


def shards(tokens, in_gain, raw_queries, w_key, w_value, q_gain, k_gain, doc_lengths, out_grad):
    tp_count = lax.axis_size("tp")
    head_size = q_gain.shape[0]
    kv_heads = w_key.shape[1] // head_size
    group_size = raw_queries.shape[1] // w_key.shape[1]
    shard_rows = tokens.shape[0] * tp_count
    reach_count = (WINDOW - 2) // shard_rows + 1
    x_float = tokens.astype(jnp.float32)
    normed_rows = input_norm(x_float, in_gain).astype(jnp.bfloat16)
    gathered = lax.all_gather(normed_rows, "tp", axis=0, tiled=True)
    first_row = lax.axis_index("seq") * shard_rows
    positions = first_row + jnp.arange(shard_rows, dtype=jnp.int32)
    begins = doc_begin(doc_lengths, positions)
    offsets = positions - begins
    lowest = jnp.maximum(begins, positions - (WINDOW - 1))
    queries = raw_queries.astype(jnp.float32).reshape(shard_rows, -1, head_size)
    keys_raw = jnp.dot(gathered, w_key, preferred_element_type=jnp.float32).reshape(
        shard_rows, -1, head_size
    )
    values_raw = jnp.dot(gathered, w_value, preferred_element_type=jnp.float32).reshape(
        shard_rows, -1, head_size
    )

    def query_map(values):
        return rotate(head_norm(values, q_gain), offsets) * QUERY_SCALE

    def key_map(values):
        return rotate(head_norm(values, k_gain), offsets)

    query_rot, query_back = jax.vjp(query_map, queries)
    key_rot, key_back = jax.vjp(key_map, keys_raw)
    query_rows = query_rot.astype(jnp.bfloat16).reshape(shard_rows, kv_heads, group_size, head_size)
    key_rows = key_rot.astype(jnp.bfloat16)
    value_rows = values_raw.astype(jnp.bfloat16)
    grad_rows = out_grad.reshape(shard_rows, kv_heads, group_size, head_size)
    rim_keys = []
    rim_values = []
    for distance in range(reach_count, 0, -1):
        far_keys, far_values = from_behind((key_rows, value_rows), "seq", distance)
        rim_keys.append(far_keys)
        rim_values.append(far_values)
    key_window = jnp.concatenate(rim_keys + [key_rows], axis=0)
    value_window = jnp.concatenate(rim_values + [value_rows], axis=0)
    key_positions = (
        first_row
        - reach_count * shard_rows
        + jnp.arange((reach_count + 1) * shard_rows, dtype=jnp.int32)
    )
    query_grad, key_grad_all, value_grad_all = attend(
        query_rows, key_window, value_window, grad_rows, lowest, positions, key_positions
    )
    own_start = reach_count * shard_rows
    key_grad = key_grad_all[own_start:]
    value_grad = value_grad_all[own_start:]
    for distance in range(1, reach_count + 1):
        lower_row = (reach_count - distance) * shard_rows
        back_keys, back_values = (
            from_behind(
                key_grad_all[lower_row : lower_row + shard_rows].astype(jnp.bfloat16),
                "seq",
                -distance,
            ).astype(jnp.float32),
            from_behind(
                value_grad_all[lower_row : lower_row + shard_rows].astype(jnp.bfloat16),
                "seq",
                -distance,
            ).astype(jnp.float32),
        )
        key_grad = key_grad + back_keys
        value_grad = value_grad + back_values
    query_grad = query_grad.reshape(shard_rows, kv_heads * group_size, head_size)
    grad_queries = query_back(query_grad)[0].reshape(shard_rows, -1).astype(jnp.bfloat16)
    grad_k = key_back(key_grad)[0].reshape(shard_rows, -1).astype(jnp.bfloat16)
    grad_v = value_grad.reshape(shard_rows, -1).astype(jnp.bfloat16)
    partial_sum = contract_last(grad_k, w_key) + contract_last(grad_v, w_value)
    normed_grad = lax.psum_scatter(
        partial_sum.astype(jnp.bfloat16), "tp", scatter_dimension=0, tiled=True
    ).astype(jnp.float32)

    def norm_map(values):
        return input_norm(values, in_gain)

    unused_rows, norm_back = jax.vjp(norm_map, x_float)
    grad_x = norm_back(normed_grad)[0].astype(jnp.bfloat16)
    key_term = contract_first(gathered, grad_k)
    value_term = contract_first(gathered, grad_v).astype(jnp.bfloat16)
    grad_wk, grad_wv = weight_sum(key_term, value_term)
    return (grad_x, grad_queries, grad_wk, grad_wv)


def solution(mesh):
    placed = (
        P(("seq", "tp"), None),
        P(),
        P("seq", "tp"),
        P(None, "tp"),
        P(None, "tp"),
        P(),
        P(),
        P(),
        P("seq", "tp"),
    )
    return jax.shard_map(
        shards,
        mesh=mesh,
        in_specs=placed,
        out_specs=(P(("seq", "tp"), None), P("seq", "tp"), P("seq", "tp"), P("seq", "tp")),
        check_vma=False,
    )
```

```python
import jax
import jax.numpy as jnp
from jax import lax
from jax.experimental import pallas as pl
from jax.experimental.pallas import tpu as pltpu
from jax.sharding import PartitionSpec as P

WINDOW = 1024
WIDE = 4


EPSILON = 1e-06
QUERY_SCALE = 168.0 ** (-0.5)
ROPE_BASE = 10000.0


def doc_begin(doc_lengths, positions):
    endings = jnp.cumsum(doc_lengths, dtype=jnp.int32)
    starts = endings - doc_lengths
    inside = starts[None, :] <= positions[:, None]
    return jnp.max(jnp.where(inside, starts[None, :], jnp.zeros_like(starts)[None, :]), axis=1)


def input_norm(values, gain):
    return values * lax.rsqrt(jnp.mean(values * values, axis=1, keepdims=True) + EPSILON) * gain


def angle_tables(positions, head_size):
    half_size = head_size // 2
    powers = jnp.arange(half_size, dtype=jnp.float32) * (2.0 / head_size)
    frequency = ROPE_BASE ** (-powers)
    angles = positions.astype(jnp.float32)[:, None] * frequency[None, :]
    cosine = jnp.cos(angles)
    sine = jnp.sin(angles)
    return jnp.concatenate([cosine, cosine], axis=1), jnp.concatenate([-sine, sine], axis=1)


def contract_last(left, right):
    return lax.dot_general(
        left, right, (((1,), (1,)), ((), ())), preferred_element_type=jnp.float32
    )


def contract_first(left, right):
    return lax.dot_general(
        left, right, (((0,), (0,)), ((), ())), preferred_element_type=jnp.float32
    )


MESH_IDS = pl.DeviceIdType.MESH


def ring_sum(piece, size, split, pos, up, down, bufs, sems, finish):
    half_up, half_down, mixed_up, mixed_down, full_up, full_down = bufs
    send_sem, recv_sem = sems
    far = lax.rem(pos + 2, 4)
    after = lax.rem(pos + 1, 4)
    before = lax.rem(pos + 3, 4)
    low = pl.ds(0, split)
    high = pl.ds(split, size - split)

    def copy(index, source, target, device):
        return pltpu.make_async_remote_copy(
            src_ref=source,
            dst_ref=target,
            send_sem=send_sem.at[index],
            recv_sem=recv_sem.at[index],
            device_id=device,
            device_id_type=MESH_IDS,
        )

    first = [
        copy(0, piece(far).at[low], half_up, up),
        copy(1, piece(far).at[high], half_down, down),
        copy(2, piece(after).at[high], full_up.at[high], up),
        copy(3, piece(before).at[low], full_down.at[low], down),
    ]
    for one in first:
        one.start()

    def second():
        first[0].wait_recv()
        mixed_up[...] = (
            piece(after)[low, :].astype(jnp.float32) + half_up[...].astype(jnp.float32)
        ).astype(jnp.bfloat16)
        last_up = copy(4, mixed_up, full_up.at[low], up)
        last_up.start()
        first[1].wait_recv()
        mixed_down[...] = (
            piece(before)[high, :].astype(jnp.float32) + half_down[...].astype(jnp.float32)
        ).astype(jnp.bfloat16)
        last_down = copy(5, mixed_down, full_down.at[high], down)
        last_down.start()

        def third():
            first[2].wait_recv()
            first[3].wait_recv()
            last_up.wait_recv()
            last_down.wait_recv()
            finish(
                lambda rows: piece(pos)[rows, :].astype(jnp.float32)
                + full_up[rows, :].astype(jnp.float32)
                + full_down[rows, :].astype(jnp.float32)
            )

            def drain():
                for one in first + [last_up, last_down]:
                    one.wait_send()

            return drain

        return third

    return second


def weight_sum_kernel(
    key_ref, value_ref, key_out, value_out,
    key_send, order, value_total, key_next, value_next, last_send, last_recv,
    *rest,
):
    bufs_a, bufs_b, bufs_c, bufs_d = rest[0:6], rest[6:12], rest[12:18], rest[18:24]
    sems = rest[24:]
    rows = key_out.shape[0]
    cols = key_out.shape[1]
    big, mid = 16 * rows, 4 * rows
    split_big = big // 2
    split_mid = mid // 2 + mid // 2 % 16
    place = lax.axis_index("seq")
    member = lax.axis_index("tp")
    x = lax.rem(place, 4)
    z = lax.rem(place // 4, 4)
    y = place // 16

    def device(ys, zs, xs):
        return ((ys * 4 + zs) * 4 + xs, member)

    x_up, x_down = device(y, z, lax.rem(x + 1, 4)), device(y, z, lax.rem(x + 3, 4))
    y_up, y_down = device(lax.rem(y + 1, 4), z, x), device(lax.rem(y + 3, 4), z, x)
    z_others = [device(y, lax.rem(z + d, 4), x) for d in (1, 2, 3)]
    barrier = pltpu.get_barrier_semaphore()
    for other in [x_up, x_down, y_up, y_down] + z_others:
        pl.semaphore_signal(barrier, inc=1, device_id=other, device_id_type=MESH_IDS)

    pl.semaphore_wait(barrier, 7)

    def finish_b1(total):
        for part in range(4):
            at = pl.ds(part * mid, mid)
            value_total[at, :] = total(at)
        for xs in range(4):
            for zs in range(4):
                order[zs * rows : zs * rows + rows, :] = value_total[
                    zs * mid + xs * rows : zs * mid + xs * rows + rows, :
                ]
            value_next[xs] = order[...].astype(jnp.bfloat16)

    second_b = ring_sum(
        lambda t: value_ref.at[pl.ds(pl.multiple_of(t * big, 16), big)],
        big, split_big, y, y_up, y_down, bufs_b, sems[2:4], finish_b1,
    )

    for ys in range(4):
        for xs in range(4):
            for zs in range(4):
                begin = ((ys * 4 + zs) * 4 + xs) * rows
                order[zs * rows : zs * rows + rows, :] = key_ref[begin : begin + rows, :]
            key_send[xs, ys * mid : ys * mid + mid, :] = order[...].astype(jnp.bfloat16)

    def finish_a1(total):
        for part in range(4):
            at = pl.ds(part * mid, mid)
            key_next[part] = total(at).astype(jnp.bfloat16)

    second_a = ring_sum(
        lambda t: key_send.at[t],
        big, split_big, x, x_up, x_down, bufs_a, sems[0:2], finish_a1,
    )
    third_b = second_b()
    third_a = second_a()
    drain_b = third_b()

    def finish_last(at):
        def finish(total):
            order[...] = total(pl.ds(0, mid))
            for zs in range(4):
                last_send[zs, 0:rows, at : at + cols] = order[
                    zs * rows : zs * rows + rows, :
                ].astype(jnp.bfloat16)
                last_send[zs, rows:, at : at + cols] = jnp.zeros(
                    (last_send.shape[1] - rows, cols), jnp.bfloat16
                )

        return finish

    second_d = ring_sum(
        lambda t: value_next.at[t],
        mid, split_mid, x, x_up, x_down, bufs_d, sems[6:8], finish_last(cols),
    )
    drain_a = third_a()
    second_c = ring_sum(
        lambda t: key_next.at[t],
        mid, split_mid, y, y_up, y_down, bufs_c, sems[4:6], finish_last(0),
    )
    third_d = second_d()
    third_c = second_c()
    drain_d = third_d()
    drain_c = third_c()
    copies = []
    for d in (1, 2, 3):
        one = pltpu.make_async_remote_copy(
            src_ref=last_send.at[lax.rem(z + d, 4)],
            dst_ref=last_recv.at[d - 1],
            send_sem=sems[8].at[d - 1],
            recv_sem=sems[9].at[d - 1],
            device_id=z_others[d - 1],
            device_id_type=MESH_IDS,
        )
        one.start()
        copies.append(one)
    for one in copies:
        one.wait_recv()
    total = last_send[z, 0:rows, :].astype(jnp.float32)
    for d in range(3):
        total = total + last_recv[d, 0:rows, :].astype(jnp.float32)
    key_out[...] = total[:, 0:cols]
    value_out[...] = total[:, cols:]
    for one in copies:
        one.wait_send()
    for drain in (drain_a, drain_b, drain_c, drain_d):
        drain()


def weight_sum(key_term, value_term):
    depth, cols = key_term.shape
    rows = depth // 64
    big, mid = 16 * rows, 4 * rows
    split_big = big // 2
    split_mid = mid // 2 + mid // 2 % 16
    padded = (rows + 15) // 16 * 16
    bf = jnp.bfloat16

    def bufs(size, split):
        return [
            pltpu.VMEM((split, cols), bf),
            pltpu.VMEM((size - split, cols), bf),
            pltpu.VMEM((split, cols), bf),
            pltpu.VMEM((size - split, cols), bf),
            pltpu.VMEM((size, cols), bf),
            pltpu.VMEM((size, cols), bf),
        ]

    return pl.pallas_call(
        weight_sum_kernel,
        out_shape=[jax.ShapeDtypeStruct((rows, cols), jnp.float32)] * 2,
        in_specs=[pl.BlockSpec(memory_space=pltpu.VMEM)] * 2,
        out_specs=[pl.BlockSpec(memory_space=pltpu.VMEM)] * 2,
        scratch_shapes=[
            pltpu.VMEM((4, big, cols), bf),
            pltpu.VMEM((mid, cols), jnp.float32),
            pltpu.VMEM((big, cols), jnp.float32),
            pltpu.VMEM((4, mid, cols), bf),
            pltpu.VMEM((4, mid, cols), bf),
            pltpu.VMEM((4, padded, 2 * cols), bf),
            pltpu.VMEM((3, padded, 2 * cols), bf),
        ]
        + bufs(big, split_big)
        + bufs(big, split_big)
        + bufs(mid, split_mid)
        + bufs(mid, split_mid)
        + [pltpu.SemaphoreType.DMA((6,))] * 8
        + [pltpu.SemaphoreType.DMA((3,))] * 2,
        compiler_params=pltpu.CompilerParams(
            collective_id=1, has_side_effects=True, vmem_limit_bytes=40 * 1024 * 1024
        ),
        cost_estimate=pl.CostEstimate(
            flops=100_000_000, bytes_accessed=150_000_000, transcendentals=0
        ),
        name="weight_sum",
    )(key_term, value_term)


def turn(values, cosine, sine):
    return values * cosine + pltpu.roll(values, values.shape[-1] // 2, 1) * sine


def gather_kernel(
    tokens_ref, gain_ref, raw_ref, q_gain_ref, k_gain_ref, cos_ref, sin_ref, w_key_ref, w_value_ref,
    gathered_ref, query_ref, raw_key_ref, window_ref,
    held, relay_up, relay_down, weights, window,
    weight_sem, out_sem, window_sem, relay_send, relay_recv, cross_send, cross_recv,
    pair_send, pair_recv, chunk_send, chunk_recv, halo_send, halo_recv,
):
    rows = tokens_ref.shape[0]
    half = rows // 2
    piece = half // 4
    cols = w_key_ref.shape[1]
    head_size = k_gain_ref.shape[1]
    place = lax.axis_index("seq")
    member = lax.axis_index("tp")
    count = lax.axis_size("seq")
    core = lax.rem(member, 2)
    upper = member // 2
    x = lax.rem(place, WIDE)
    z = upper * 4 + lax.rem(place // WIDE, 4)
    y = place // (4 * WIDE)

    def along_z(by):
        other = lax.rem(z + by, 8)
        return ((y * 4 + lax.rem(other, 4)) * WIDE + x, other // 4 * 2 + core)

    z_up, z_down = along_z(2), along_z(6)
    partner = (place, upper * 2 + 1 - core)
    later = [(lax.rem(place + by, count), member) for by in (1, 2)]
    earlier = [(lax.rem(place + count - by, count), member) for by in (1, 2)]

    def remote(source, target, send_sem, recv_sem, device):
        return pltpu.make_async_remote_copy(
            src_ref=source,
            dst_ref=target,
            send_sem=send_sem,
            recv_sem=recv_sem,
            device_id=device,
            device_id_type=MESH_IDS,
        )

    loads = [
        pltpu.make_async_copy(w_key_ref, weights.at[:, pl.ds(0, cols)], weight_sem.at[0]),
        pltpu.make_async_copy(w_value_ref, weights.at[:, pl.ds(cols, cols)], weight_sem.at[1]),
    ]
    for one in loads:
        one.start()
    barrier = pltpu.get_barrier_semaphore()
    for other in [z_up, z_down, partner] + later + earlier:
        pl.semaphore_signal(barrier, inc=1, device_id=other, device_id_type=MESH_IDS)

    own = pl.multiple_of(member * rows, rows)
    beside = pl.multiple_of((upper * 2 + 1 - core) * rows, rows)
    across = pl.multiple_of(((1 - upper) * 2 + core) * rows, rows)
    corner = pl.multiple_of(((1 - upper) * 2 + 1 - core) * rows, rows)

    def norm_rows(step, carry):
        at = pl.ds(pl.multiple_of(step * 16, 16), 16)
        values = tokens_ref[at, :].astype(jnp.float32)
        scale = lax.rsqrt(jnp.mean(values * values, axis=1, keepdims=True) + EPSILON)
        held[pl.ds(pl.multiple_of(own + step * 16, 16), 16), :] = (
            values * scale * gain_ref[...]
        ).astype(jnp.bfloat16)
        return carry

    lax.fori_loop(0, rows // 16, norm_rows, 0)
    pl.semaphore_wait(barrier, 7)

    to_partner = remote(
        held.at[pl.ds(own, rows)], held.at[pl.ds(own, rows)], pair_send.at[0], pair_recv.at[0], partner
    )
    to_partner.start()

    def first_up(step):
        return remote(
            held.at[pl.ds(pl.multiple_of(own + step * piece, piece), piece)],
            relay_up.at[pl.ds(pl.multiple_of(step * piece, piece), piece)],
            relay_send.at[0, step], relay_recv.at[0, step], z_up,
        )

    def first_down(step):
        return remote(
            held.at[pl.ds(pl.multiple_of(own + half + step * piece, piece), piece)],
            relay_down.at[pl.ds(pl.multiple_of(step * piece, piece), piece)],
            relay_send.at[1, step], relay_recv.at[1, step], z_down,
        )

    def second_up(step):
        target = pl.multiple_of(((1 - lax.rem(z + 2, 8) // 4) * 2 + core) * rows + step * piece, piece)
        return remote(
            relay_up.at[pl.ds(pl.multiple_of(step * piece, piece), piece)],
            held.at[pl.ds(target, piece)],
            cross_send.at[0, step], cross_recv.at[0, step], z_up,
        )

    def second_down(step):
        target = pl.multiple_of(
            ((1 - lax.rem(z + 6, 8) // 4) * 2 + core) * rows + half + step * piece, piece
        )
        return remote(
            relay_down.at[pl.ds(pl.multiple_of(step * piece, piece), piece)],
            held.at[pl.ds(target, piece)],
            cross_send.at[1, step], cross_recv.at[1, step], z_down,
        )

    def pass_on(side, step):
        at = pl.ds(pl.multiple_of(across + side * half + step * piece, piece), piece)
        return remote(held.at[at], held.at[at], chunk_send.at[side, step], chunk_recv.at[side, step], partner)

    for step in range(4):
        first_up(step).start()
        first_down(step).start()

    def halo(by, index, begin, size):
        return remote(
            window.at[2, pl.ds(begin, size)],
            window.at[2 - by, pl.ds(begin, size)],
            halo_send.at[by - 1, index], halo_recv.at[by - 1, index], later[by - 1],
        )

    def project(parts):
        block = [held[pl.ds(begin, size), :] for begin, size in parts]
        block = block[0] if len(block) == 1 else jnp.concatenate(block, axis=0)
        result = jnp.dot(block, weights[...], preferred_element_type=jnp.float32)
        at = 0
        for begin, size in parts:
            mine = result[at : at + size]
            at += size
            where = pl.ds(begin, size)
            raw_key_ref[where, :] = mine[:, :cols]
            window[2, where, cols:] = mine[:, cols:].astype(jnp.bfloat16)
            for head in range(cols // head_size):
                lanes = slice(head * head_size, (head + 1) * head_size)
                values = mine[:, lanes]
                scale = lax.rsqrt(jnp.mean(values * values, axis=1, keepdims=True) + EPSILON)
                values = values * scale * k_gain_ref[...]
                window[2, where, lanes] = turn(values, cos_ref[where, :], sin_ref[where, :]).astype(
                    jnp.bfloat16
                )

    out_own = pltpu.make_async_copy(
        held.at[pl.ds(own, rows)], gathered_ref.at[pl.ds(own, rows)], out_sem.at[0]
    )
    out_own.start()
    for one in loads:
        one.wait()
    project([(own, rows)])
    halo(1, 0, own, rows).start()
    halo(2, 0, own, rows).start()
    to_partner.wait_recv()
    out_beside = pltpu.make_async_copy(
        held.at[pl.ds(beside, rows)], gathered_ref.at[pl.ds(beside, rows)], out_sem.at[1]
    )
    out_beside.start()
    project([(beside, rows)])
    halo(1, 1, beside, rows).start()
    halo(2, 1, beside, rows).start()

    for head in range(raw_ref.shape[1] // head_size):
        lanes = slice(head * head_size, (head + 1) * head_size)
        values = raw_ref[:, lanes].astype(jnp.float32)
        scale = lax.rsqrt(jnp.mean(values * values, axis=1, keepdims=True) + EPSILON)
        values = values * scale * q_gain_ref[...]
        query_ref[:, lanes] = (turn(values, cos_ref[...], sin_ref[...]) * QUERY_SCALE).astype(
            jnp.bfloat16
        )

    for step in range(4):
        first_up(step).wait_recv()
        second_up(step).start()
        first_down(step).wait_recv()
        second_down(step).start()

    def groups(step):
        return [
            (pl.multiple_of(base + side * half + step * piece, piece), piece)
            for base in (across, corner)
            for side in (0, 1)
        ]

    def arrive(step, carry):
        for side, copy in ((0, second_up(step)), (1, second_down(step))):
            copy.wait_recv()
            pass_on(side, step).start()
        for side in (0, 1):
            pass_on(side, step).wait_recv()
        project(groups(step))
        for index, (begin, size) in enumerate(groups(step)):
            halo(1, 2 + step * 4 + index, begin, size).start()
            halo(2, 2 + step * 4 + index, begin, size).start()
        return carry

    lax.fori_loop(0, 4, arrive, 0)
    out_across = pltpu.make_async_copy(
        held.at[pl.ds(across, rows)], gathered_ref.at[pl.ds(across, rows)], out_sem.at[2]
    )
    out_corner = pltpu.make_async_copy(
        held.at[pl.ds(corner, rows)], gathered_ref.at[pl.ds(corner, rows)], out_sem.at[3]
    )
    out_across.start()
    out_corner.start()

    def each_halo(act):
        for by in (1, 2):
            act(halo(by, 0, own, rows))
            act(halo(by, 1, beside, rows))

            def inner(step, carry):
                for index, (begin, size) in enumerate(groups(step)):
                    act(halo(by, 2 + step * 4 + index, begin, size))
                return carry

            lax.fori_loop(0, 4, inner, 0)

    each_halo(lambda copy: copy.wait_recv())
    out_window = pltpu.make_async_copy(window, window_ref, window_sem.at[0])
    out_window.start()
    each_halo(lambda copy: copy.wait_send())
    to_partner.wait_send()
    for step in range(4):
        first_up(step).wait_send()
        first_down(step).wait_send()
        second_up(step).wait_send()
        second_down(step).wait_send()
        pass_on(0, step).wait_send()
        pass_on(1, step).wait_send()
    for one in (out_own, out_beside, out_across, out_corner, out_window):
        one.wait()


def gather_and_project(tokens, in_gain, raw_queries, w_key, w_value, q_gain, k_gain, cosine, sine):
    rows, depth = tokens.shape
    shard = rows * 4
    cols = w_key.shape[1]
    bf = jnp.bfloat16
    vmem = pl.BlockSpec(memory_space=pltpu.VMEM)
    anywhere = pl.BlockSpec(memory_space=pl.ANY)
    dma = pltpu.SemaphoreType.DMA
    return pl.pallas_call(
        gather_kernel,
        out_shape=[
            jax.ShapeDtypeStruct((shard, depth), bf),
            jax.ShapeDtypeStruct(raw_queries.shape, bf),
            jax.ShapeDtypeStruct((shard, cols), jnp.float32),
            jax.ShapeDtypeStruct((3, shard, 2 * cols), bf),
        ],
        in_specs=[vmem] * 7 + [anywhere] * 2,
        out_specs=[anywhere, vmem, vmem, anywhere],
        scratch_shapes=[
            pltpu.VMEM((shard, depth), bf),
            pltpu.VMEM((rows // 2, depth), bf),
            pltpu.VMEM((rows // 2, depth), bf),
            pltpu.VMEM((depth, 2 * cols), bf),
            pltpu.VMEM((3, shard, 2 * cols), bf),
            dma((2,)),
            dma((4,)),
            dma((1,)),
            dma((2, 4)),
            dma((2, 4)),
            dma((2, 4)),
            dma((2, 4)),
            dma((1,)),
            dma((1,)),
            dma((2, 4)),
            dma((2, 4)),
            dma((2, 18)),
            dma((2, 18)),
        ],
        compiler_params=pltpu.CompilerParams(
            collective_id=2, has_side_effects=True, vmem_limit_bytes=40 * 1024 * 1024
        ),
        cost_estimate=pl.CostEstimate(
            flops=3_000_000_000, bytes_accessed=150_000_000, transcendentals=0
        ),
        name="gather_and_project",
    )(tokens, in_gain[None, :], raw_queries, q_gain[None, :], k_gain[None, :], cosine, sine, w_key, w_value)


def unturn(values, cosine, sine):
    return values * cosine - pltpu.roll(values, values.shape[-1] // 2, 1) * sine


def norm_back(grad, values, gain):
    scale = lax.rsqrt(jnp.mean(values * values, axis=1, keepdims=True) + EPSILON)
    unit = values * scale
    inner = grad * gain
    return scale * (inner - unit * jnp.mean(inner * unit, axis=1, keepdims=True))


def attend_kernel(
    query_ref, window_ref, out_grad_ref, low_ref, raw_ref, raw_key_ref, cos_ref, sin_ref, q_gain_ref, k_gain_ref,
    grad_query_ref, grad_kv_ref,
    exps, along, totals, query_total, parts, returned,
    send_sem, recv_sem,
):
    shard = query_ref.shape[0]
    head_size = q_gain_ref.shape[1]
    kv_heads = raw_key_ref.shape[1] // head_size
    group_size = query_ref.shape[1] // raw_key_ref.shape[1]
    tile = shard // 2
    reach = 2 * shard
    place = lax.axis_index("seq")
    member = lax.axis_index("tp")
    count = lax.axis_size("seq")
    later = [(lax.rem(place + by, count), member) for by in (2, 1)]
    earlier = [(lax.rem(place + count - by, count), member) for by in (2, 1)]
    barrier = pltpu.get_barrier_semaphore()
    for other in later + earlier:
        pl.semaphore_signal(barrier, inc=1, device_id=other, device_id_type=MESH_IDS)

    totals[...] = jnp.zeros_like(totals)

    def across(left, right):
        return lax.dot_general(left, right, (((1,), (1,)), ((), ())), preferred_element_type=jnp.float32)

    def back(window, head):
        return pltpu.make_async_remote_copy(
            src_ref=parts.at[window, head],
            dst_ref=returned.at[window, head],
            send_sem=send_sem.at[window, head],
            recv_sem=recv_sem.at[window, head],
            device_id=earlier[window],
            device_id_type=MESH_IDS,
        )

    for head in range(kv_heads):
        key_lanes = slice(head * head_size, (head + 1) * head_size)
        value_lanes = slice((kv_heads + head) * head_size, (kv_heads + head + 1) * head_size)
        lanes = [
            slice((head * group_size + member_of) * head_size, (head * group_size + member_of + 1) * head_size)
            for member_of in range(group_size)
        ]

        def half(step, carry):
            begin = pl.multiple_of(step * tile, tile)
            rows = pl.ds(begin, tile)
            queries = jnp.concatenate([query_ref[rows, at] for at in lanes], axis=0)
            grads = jnp.concatenate([out_grad_ref[rows, at] for at in lanes], axis=0)
            low = low_ref[step]
            low = jnp.concatenate([low] * group_size, axis=1)
            width = group_size * tile
            high = lax.broadcasted_iota(jnp.int32, (1, tile), 1) + (reach + begin)
            high = jnp.concatenate([high] * group_size, axis=1)

            def scores(index, stats):
                total, delta = stats
                first = pl.multiple_of(begin + index * tile, tile)
                key_rows = pl.ds(first, tile)
                score = across(window_ref[key_rows, key_lanes], queries)
                partial = across(window_ref[key_rows, value_lanes], grads)
                key = lax.broadcasted_iota(jnp.int32, (tile, width), 0) + first
                value = jnp.where((key >= low) & (key <= high), jnp.exp(score), 0.0)
                at = pl.ds(pl.multiple_of(index * tile, tile), tile)
                exps[at, :] = value
                along[at, :] = partial
                total = total + jnp.sum(value, axis=0, keepdims=True)
                delta = delta + jnp.sum(value * partial, axis=0, keepdims=True)
                return total, delta

            nothing = jnp.zeros((1, width), jnp.float32)
            total, delta = lax.fori_loop(0, reach // tile + 1, scores, (nothing, nothing))
            inverse = 1.0 / total
            delta = delta * inverse
            query_total[...] = jnp.zeros_like(query_total)

            def slopes(index, carry):
                key_rows = pl.ds(pl.multiple_of(begin + index * tile, tile), tile)
                at = pl.ds(pl.multiple_of(index * tile, tile), tile)
                probs = exps[at, :] * inverse
                slope = (probs * (along[at, :] - delta)).astype(jnp.bfloat16)
                query_total[...] += contract_first(window_ref[key_rows, key_lanes], slope)
                totals[key_rows, key_lanes] += jnp.dot(slope, queries, preferred_element_type=jnp.float32)
                totals[key_rows, value_lanes] += jnp.dot(
                    probs.astype(jnp.bfloat16), grads, preferred_element_type=jnp.float32
                )
                return carry

            lax.fori_loop(0, reach // tile + 1, slopes, 0)
            flipped = query_total[...].T
            for member_of, at in enumerate(lanes):
                grad = flipped[member_of * tile : (member_of + 1) * tile] * QUERY_SCALE
                grad = unturn(grad, cos_ref[rows, :], sin_ref[rows, :])
                values = raw_ref[rows, at].astype(jnp.float32)
                grad_query_ref[rows, at] = norm_back(grad, values, q_gain_ref[...]).astype(jnp.bfloat16)
            return carry

        lax.fori_loop(0, 2, half, 0)
        for window in range(2):
            rows = slice(window * shard, (window + 1) * shard)
            parts[window, head, :, :head_size] = totals[rows, key_lanes].astype(jnp.bfloat16)
            parts[window, head, :, head_size:] = totals[rows, value_lanes].astype(jnp.bfloat16)
        if head == 0:
            pl.semaphore_wait(barrier, 4)
        for window in range(2):
            back(window, head).start()

    own = slice(reach, reach + shard)
    for head in range(kv_heads):
        key_lanes = slice(head * head_size, (head + 1) * head_size)
        value_lanes = slice((kv_heads + head) * head_size, (kv_heads + head + 1) * head_size)
        for window in range(2):
            back(window, head).wait_recv()
        key_grad = totals[own, key_lanes]
        value_grad = totals[own, value_lanes]
        for window in (1, 0):
            key_grad = key_grad + returned[window, head, :, :head_size].astype(jnp.float32)
            value_grad = value_grad + returned[window, head, :, head_size:].astype(jnp.float32)
        grad_kv_ref[:, value_lanes] = value_grad.astype(jnp.bfloat16)
        key_grad = unturn(key_grad, cos_ref[...], sin_ref[...])
        grad_kv_ref[:, key_lanes] = norm_back(key_grad, raw_key_ref[:, key_lanes], k_gain_ref[...]).astype(
            jnp.bfloat16
        )
    for head in range(kv_heads):
        for window in range(2):
            back(window, head).wait_send()


def attend_back(query_rot, window, out_grad, low, raw_queries, raw_keys, cosine, sine, q_gain, k_gain):
    shard = query_rot.shape[0]
    head_size = q_gain.shape[0]
    kv_heads = raw_keys.shape[1] // head_size
    group_size = query_rot.shape[1] // raw_keys.shape[1]
    tile = shard // 2
    width = group_size * tile
    vmem = pl.BlockSpec(memory_space=pltpu.VMEM)
    return pl.pallas_call(
        attend_kernel,
        out_shape=[
            jax.ShapeDtypeStruct(query_rot.shape, jnp.bfloat16),
            jax.ShapeDtypeStruct((shard, 2 * raw_keys.shape[1]), jnp.bfloat16),
        ],
        in_specs=[vmem] * 10,
        out_specs=[vmem] * 2,
        scratch_shapes=[
            pltpu.VMEM((2 * shard + tile, width), jnp.float32),
            pltpu.VMEM((2 * shard + tile, width), jnp.float32),
            pltpu.VMEM((3 * shard, 2 * raw_keys.shape[1]), jnp.float32),
            pltpu.VMEM((head_size, width), jnp.float32),
            pltpu.VMEM((2, kv_heads, shard, 2 * head_size), jnp.bfloat16),
            pltpu.VMEM((2, kv_heads, shard, 2 * head_size), jnp.bfloat16),
            pltpu.SemaphoreType.DMA((2, kv_heads)),
            pltpu.SemaphoreType.DMA((2, kv_heads)),
        ],
        compiler_params=pltpu.CompilerParams(
            collective_id=3, has_side_effects=True, vmem_limit_bytes=40 * 1024 * 1024
        ),
        cost_estimate=pl.CostEstimate(
            flops=8_000_000_000, bytes_accessed=100_000_000, transcendentals=3_000_000
        ),
        name="attend_back",
    )(
        query_rot, window.reshape(3 * shard, window.shape[2]), out_grad, low, raw_queries, raw_keys,
        cosine, sine, q_gain[None, :], k_gain[None, :],
    )


def shards(tokens, in_gain, raw_queries, w_key, w_value, q_gain, k_gain, doc_lengths, out_grad):
    head_size = q_gain.shape[0]
    shard_rows = tokens.shape[0] * lax.axis_size("tp")
    reach = 2 * shard_rows
    x_float = tokens.astype(jnp.float32)
    first_row = lax.axis_index("seq") * shard_rows
    positions = first_row + jnp.arange(shard_rows, dtype=jnp.int32)
    begins = doc_begin(doc_lengths, positions)
    lowest = jnp.maximum(begins, positions - (WINDOW - 1))
    low = (lowest - (first_row - reach)).reshape(2, 1, shard_rows // 2)
    cosine, sine = angle_tables(positions - begins, head_size)
    gathered, query_rot, raw_keys, window = gather_and_project(
        tokens, in_gain, raw_queries, w_key, w_value, q_gain, k_gain, cosine, sine
    )
    grad_queries, grad_kv = attend_back(
        query_rot, window, out_grad, low, raw_queries, raw_keys, cosine, sine, q_gain, k_gain
    )
    kv_cols = w_key.shape[1]
    grad_k = grad_kv[:, :kv_cols]
    grad_v = grad_kv[:, kv_cols:]
    partial_sum = contract_last(grad_k, w_key) + contract_last(grad_v, w_value)
    normed_grad = lax.psum_scatter(
        partial_sum.astype(jnp.bfloat16), "tp", scatter_dimension=0, tiled=True
    ).astype(jnp.float32)

    def norm_map(values):
        return input_norm(values, in_gain)

    unused_rows, input_back = jax.vjp(norm_map, x_float)
    grad_x = input_back(normed_grad)[0].astype(jnp.bfloat16)
    key_term = contract_first(gathered, grad_k)
    value_term = contract_first(gathered, grad_v).astype(jnp.bfloat16)
    grad_wk, grad_wv = weight_sum(key_term, value_term)
    return (grad_x, grad_queries, grad_wk, grad_wv)


def solution(mesh):
    placed = (
        P(("seq", "tp"), None),
        P(),
        P("seq", "tp"),
        P(None, "tp"),
        P(None, "tp"),
        P(),
        P(),
        P(),
        P("seq", "tp"),
    )
    return jax.shard_map(
        shards,
        mesh=mesh,
        in_specs=placed,
        out_specs=(P(("seq", "tp"), None), P("seq", "tp"), P("seq", "tp"), P("seq", "tp")),
        check_vma=False,
    )
```

```python
import functools

import jax
import jax.numpy as jnp
from jax import lax
from jax.experimental import pallas as pl
from jax.experimental.pallas import tpu as pltpu
from jax.sharding import PartitionSpec as P

WINDOW = 1024
WIDE = 4


EPSILON = 1e-06
QUERY_SCALE = 168.0 ** (-0.5)
ROPE_BASE = 10000.0


def doc_begin(doc_lengths, positions):
    endings = jnp.cumsum(doc_lengths, dtype=jnp.int32)
    starts = endings - doc_lengths
    inside = starts[None, :] <= positions[:, None]
    return jnp.max(jnp.where(inside, starts[None, :], jnp.zeros_like(starts)[None, :]), axis=1)


def angle_tables(positions, head_size):
    half_size = head_size // 2
    powers = jnp.arange(half_size, dtype=jnp.float32) * (2.0 / head_size)
    frequency = ROPE_BASE ** (-powers)
    angles = positions.astype(jnp.float32)[:, None] * frequency[None, :]
    cosine = jnp.cos(angles)
    sine = jnp.sin(angles)
    return jnp.concatenate([cosine, cosine], axis=1), jnp.concatenate([-sine, sine], axis=1)


def contract_last(left, right):
    return lax.dot_general(
        left, right, (((1,), (1,)), ((), ())), preferred_element_type=jnp.float32
    )


def contract_first(left, right):
    return lax.dot_general(
        left, right, (((0,), (0,)), ((), ())), preferred_element_type=jnp.float32
    )


MESH_IDS = pl.DeviceIdType.MESH


def ring_sum(piece, size, split, pos, up, down, bufs, sems, finish):
    half_up, half_down, mixed_up, mixed_down, full_up, full_down = bufs
    send_sem, recv_sem = sems
    far = lax.rem(pos + 2, 4)
    after = lax.rem(pos + 1, 4)
    before = lax.rem(pos + 3, 4)
    low = pl.ds(0, split)
    high = pl.ds(split, size - split)

    def copy(index, source, target, device):
        return pltpu.make_async_remote_copy(
            src_ref=source,
            dst_ref=target,
            send_sem=send_sem.at[index],
            recv_sem=recv_sem.at[index],
            device_id=device,
            device_id_type=MESH_IDS,
        )

    first = [
        copy(0, piece(far).at[low], half_up, up),
        copy(1, piece(far).at[high], half_down, down),
        copy(2, piece(after).at[high], full_up.at[high], up),
        copy(3, piece(before).at[low], full_down.at[low], down),
    ]
    for one in first:
        one.start()

    def second():
        first[0].wait_recv()
        mixed_up[...] = (
            piece(after)[low, :].astype(jnp.float32) + half_up[...].astype(jnp.float32)
        ).astype(jnp.bfloat16)
        last_up = copy(4, mixed_up, full_up.at[low], up)
        last_up.start()
        first[1].wait_recv()
        mixed_down[...] = (
            piece(before)[high, :].astype(jnp.float32) + half_down[...].astype(jnp.float32)
        ).astype(jnp.bfloat16)
        last_down = copy(5, mixed_down, full_down.at[high], down)
        last_down.start()

        def third():
            first[2].wait_recv()
            first[3].wait_recv()
            last_up.wait_recv()
            last_down.wait_recv()
            finish(
                lambda rows: piece(pos)[rows, :].astype(jnp.float32)
                + full_up[rows, :].astype(jnp.float32)
                + full_down[rows, :].astype(jnp.float32)
            )

            def drain():
                for one in first + [last_up, last_down]:
                    one.wait_send()

            return drain

        return third

    return second


def turn(values, cosine, sine):
    return values * cosine + pltpu.roll(values, values.shape[-1] // 2, 1) * sine


def gather_kernel(
    tokens_hbm, gain_ref, raw_hbm, q_gain_ref, k_gain_ref, cos_ref, sin_ref, w_key_ref, w_value_ref,
    gathered_ref, query_ref, raw_key_ref, window_ref,
    held, relay_up, relay_down, weights, window, tokens_ref, raw_ref, passing,
    weight_sem, out_sem, window_sem, relay_send, relay_recv, cross_send, cross_recv,
    pair_send, pair_recv, chunk_send, chunk_recv, halo_send, halo_recv, middle_send, middle_recv,
):
    rows = tokens_ref.shape[0]
    half = rows // 2
    piece = half // 4
    cols = w_key_ref.shape[1]
    head_size = k_gain_ref.shape[1]
    place = lax.axis_index("seq")
    member = lax.axis_index("tp")
    count = lax.axis_size("seq")
    core = lax.rem(member, 2)
    upper = member // 2
    x = lax.rem(place, WIDE)
    z = upper * 4 + lax.rem(place // WIDE, 4)
    y = place // (4 * WIDE)

    def along_z(by):
        other = lax.rem(z + by, 8)
        return ((y * 4 + lax.rem(other, 4)) * WIDE + x, other // 4 * 2 + core)

    z_up, z_down = along_z(2), along_z(6)
    partner = (place, upper * 2 + 1 - core)
    later = (lax.rem(place + 1, count), member)
    earlier = (lax.rem(place + count - 1, count), member)

    def in_row(of, xs):
        return (of // WIDE * WIDE + xs, member)

    left, right = lax.rem(x + WIDE - 1, WIDE), lax.rem(x + 1, WIDE)
    middle_to = in_row(lax.rem(place + 2, count), left)
    middle_from = (lax.rem(place // WIDE * WIDE + left + count - 2, count), member)
    row_left, row_right = in_row(place, left), in_row(place, right)

    def remote(source, target, send_sem, recv_sem, device):
        return pltpu.make_async_remote_copy(
            src_ref=source,
            dst_ref=target,
            send_sem=send_sem,
            recv_sem=recv_sem,
            device_id=device,
            device_id_type=MESH_IDS,
        )

    load_tokens = pltpu.make_async_copy(tokens_hbm, tokens_ref, weight_sem.at[2])
    load_tokens.start()
    load_raw = pltpu.make_async_copy(raw_hbm, raw_ref, weight_sem.at[3])
    load_raw.start()
    loads = [
        pltpu.make_async_copy(w_key_ref, weights.at[:, pl.ds(0, cols)], weight_sem.at[0]),
        pltpu.make_async_copy(w_value_ref, weights.at[:, pl.ds(cols, cols)], weight_sem.at[1]),
    ]
    for one in loads:
        one.start()
    barrier = pltpu.get_barrier_semaphore()
    for other in [z_up, z_down, partner, later, earlier, middle_to, middle_from, row_left, row_right]:
        pl.semaphore_signal(barrier, inc=1, device_id=other, device_id_type=MESH_IDS)

    own = pl.multiple_of(member * rows, rows)
    beside = pl.multiple_of((upper * 2 + 1 - core) * rows, rows)
    across = pl.multiple_of(((1 - upper) * 2 + core) * rows, rows)
    corner = pl.multiple_of(((1 - upper) * 2 + 1 - core) * rows, rows)

    def norm_rows(step, carry):
        at = pl.ds(pl.multiple_of(step * 16, 16), 16)
        values = tokens_ref[at, :].astype(jnp.float32)
        scale = lax.rsqrt(jnp.mean(values * values, axis=1, keepdims=True) + EPSILON)
        held[pl.ds(pl.multiple_of(own + step * 16, 16), 16), :] = (
            values * scale * gain_ref[...]
        ).astype(jnp.bfloat16)
        return carry

    load_tokens.wait()
    lax.fori_loop(0, rows // 16, norm_rows, 0)
    pl.semaphore_wait(barrier, 9)

    to_partner = remote(
        held.at[pl.ds(own, rows)], held.at[pl.ds(own, rows)], pair_send.at[0], pair_recv.at[0], partner
    )
    to_partner.start()

    def first_up(step):
        return remote(
            held.at[pl.ds(pl.multiple_of(own + step * piece, piece), piece)],
            relay_up.at[pl.ds(pl.multiple_of(step * piece, piece), piece)],
            relay_send.at[0, step], relay_recv.at[0, step], z_up,
        )

    def first_down(step):
        return remote(
            held.at[pl.ds(pl.multiple_of(own + half + step * piece, piece), piece)],
            relay_down.at[pl.ds(pl.multiple_of(step * piece, piece), piece)],
            relay_send.at[1, step], relay_recv.at[1, step], z_down,
        )

    def second_up(step):
        target = pl.multiple_of(((1 - lax.rem(z + 2, 8) // 4) * 2 + core) * rows + step * piece, piece)
        return remote(
            relay_up.at[pl.ds(pl.multiple_of(step * piece, piece), piece)],
            held.at[pl.ds(target, piece)],
            cross_send.at[0, step], cross_recv.at[0, step], z_up,
        )

    def second_down(step):
        target = pl.multiple_of(
            ((1 - lax.rem(z + 6, 8) // 4) * 2 + core) * rows + half + step * piece, piece
        )
        return remote(
            relay_down.at[pl.ds(pl.multiple_of(step * piece, piece), piece)],
            held.at[pl.ds(target, piece)],
            cross_send.at[1, step], cross_recv.at[1, step], z_down,
        )

    def pass_on(side, step):
        at = pl.ds(pl.multiple_of(across + side * half + step * piece, piece), piece)
        return remote(held.at[at], held.at[at], chunk_send.at[side, step], chunk_recv.at[side, step], partner)

    for step in range(4):
        first_up(step).start()
        first_down(step).start()

    def halo(by, index, begin, size):
        at = pl.ds(begin, size)
        return remote(
            window.at[2, at] if by == 1 else passing.at[at],
            window.at[2 - by, at],
            halo_send.at[by - 1, index], halo_recv.at[by - 1, index], later if by == 1 else row_left,
        )

    def middle(index, begin, size):
        at = pl.ds(begin, size)
        return remote(
            window.at[2, at], passing.at[at], middle_send.at[index], middle_recv.at[index], middle_to
        )

    def hand_on(index, begin, size):
        middle(index, begin, size).wait_recv()
        halo(2, index, begin, size).start()

    def project(parts):
        block = [held[pl.ds(begin, size), :] for begin, size in parts]
        block = block[0] if len(block) == 1 else jnp.concatenate(block, axis=0)
        result = jnp.dot(block, weights[...], preferred_element_type=jnp.float32)
        at = 0
        for begin, size in parts:
            mine = result[at : at + size]
            at += size
            where = pl.ds(begin, size)
            raw_key_ref[where, :] = mine[:, :cols]
            window[2, where, cols:] = mine[:, cols:].astype(jnp.bfloat16)
            for head in range(cols // head_size):
                lanes = slice(head * head_size, (head + 1) * head_size)
                values = mine[:, lanes]
                scale = lax.rsqrt(jnp.mean(values * values, axis=1, keepdims=True) + EPSILON)
                values = values * scale * k_gain_ref[...]
                window[2, where, lanes] = turn(values, cos_ref[where, :], sin_ref[where, :]).astype(
                    jnp.bfloat16
                )

    out_own = pltpu.make_async_copy(
        held.at[pl.ds(own, rows)], gathered_ref.at[pl.ds(own, rows)], out_sem.at[0]
    )
    out_own.start()
    for one in loads:
        one.wait()
    project([(own, rows)])
    halo(1, 0, own, rows).start()
    middle(0, own, rows).start()
    to_partner.wait_recv()
    out_beside = pltpu.make_async_copy(
        held.at[pl.ds(beside, rows)], gathered_ref.at[pl.ds(beside, rows)], out_sem.at[1]
    )
    out_beside.start()
    project([(beside, rows)])
    halo(1, 1, beside, rows).start()
    middle(1, beside, rows).start()

    load_raw.wait()
    for head in range(raw_ref.shape[1] // head_size):
        lanes = slice(head * head_size, (head + 1) * head_size)
        values = raw_ref[:, lanes].astype(jnp.float32)
        scale = lax.rsqrt(jnp.mean(values * values, axis=1, keepdims=True) + EPSILON)
        values = values * scale * q_gain_ref[...]
        query_ref[:, lanes] = (turn(values, cos_ref[...], sin_ref[...]) * QUERY_SCALE).astype(
            jnp.bfloat16
        )

    for step in range(4):
        first_up(step).wait_recv()
        second_up(step).start()
        first_down(step).wait_recv()
        second_down(step).start()
        if step == 1:
            hand_on(0, own, rows)
            hand_on(1, beside, rows)

    def groups(step):
        return [
            (pl.multiple_of(base + side * half + step * piece, piece), piece)
            for base in (across, corner)
            for side in (0, 1)
        ]

    def arrive(step, carry):
        for side, copy in ((0, second_up(step)), (1, second_down(step))):
            copy.wait_recv()
            pass_on(side, step).start()
        for side in (0, 1):
            pass_on(side, step).wait_recv()
        project(groups(step))
        for index, (begin, size) in enumerate(groups(step)):
            halo(1, 2 + step * 4 + index, begin, size).start()
            middle(2 + step * 4 + index, begin, size).start()

        @pl.when(step > 0)
        def before():
            for index, (begin, size) in enumerate(groups(step - 1)):
                hand_on(2 + (step - 1) * 4 + index, begin, size)

        return carry

    lax.fori_loop(0, 4, arrive, 0)
    for index, (begin, size) in enumerate(groups(3)):
        hand_on(14 + index, begin, size)
    out_across = pltpu.make_async_copy(
        held.at[pl.ds(across, rows)], gathered_ref.at[pl.ds(across, rows)], out_sem.at[2]
    )
    out_corner = pltpu.make_async_copy(
        held.at[pl.ds(corner, rows)], gathered_ref.at[pl.ds(corner, rows)], out_sem.at[3]
    )
    out_across.start()
    out_corner.start()

    def each_halo(kinds, act):
        for kind in kinds:
            act(kind(0, own, rows))
            act(kind(1, beside, rows))

            def inner(step, carry):
                for index, (begin, size) in enumerate(groups(step)):
                    act(kind(2 + step * 4 + index, begin, size))
                return carry

            lax.fori_loop(0, 4, inner, 0)

    halos = [functools.partial(halo, 1), functools.partial(halo, 2)]
    each_halo(halos, lambda copy: copy.wait_recv())
    out_window = pltpu.make_async_copy(window, window_ref, window_sem.at[0])
    out_window.start()
    each_halo(halos + [middle], lambda copy: copy.wait_send())
    to_partner.wait_send()
    for step in range(4):
        first_up(step).wait_send()
        first_down(step).wait_send()
        second_up(step).wait_send()
        second_down(step).wait_send()
        pass_on(0, step).wait_send()
        pass_on(1, step).wait_send()
    for one in (out_own, out_beside, out_across, out_corner, out_window):
        one.wait()


def gather_and_project(tokens, in_gain, raw_queries, w_key, w_value, q_gain, k_gain, cosine, sine):
    rows, depth = tokens.shape
    shard = rows * 4
    cols = w_key.shape[1]
    bf = jnp.bfloat16
    vmem = pl.BlockSpec(memory_space=pltpu.VMEM)
    anywhere = pl.BlockSpec(memory_space=pl.ANY)
    outside = pl.BlockSpec(memory_space=pltpu.HBM)
    dma = pltpu.SemaphoreType.DMA
    return pl.pallas_call(
        gather_kernel,
        out_shape=[
            jax.ShapeDtypeStruct((shard, depth), bf),
            jax.ShapeDtypeStruct(raw_queries.shape, bf),
            jax.ShapeDtypeStruct((shard, cols), jnp.float32),
            jax.ShapeDtypeStruct((3, shard, 2 * cols), bf),
        ],
        in_specs=[outside, vmem, outside] + [vmem] * 4 + [outside] * 2,
        out_specs=[anywhere, vmem, vmem, anywhere],
        scratch_shapes=[
            pltpu.VMEM((shard, depth), bf),
            pltpu.VMEM((rows // 2, depth), bf),
            pltpu.VMEM((rows // 2, depth), bf),
            pltpu.VMEM((depth, 2 * cols), bf),
            pltpu.VMEM((3, shard, 2 * cols), bf),
            pltpu.VMEM((rows, depth), bf),
            pltpu.VMEM(raw_queries.shape, bf),
            pltpu.VMEM((shard, 2 * cols), bf),
            dma((4,)),
            dma((4,)),
            dma((1,)),
            dma((2, 4)),
            dma((2, 4)),
            dma((2, 4)),
            dma((2, 4)),
            dma((1,)),
            dma((1,)),
            dma((2, 4)),
            dma((2, 4)),
            dma((2, 18)),
            dma((2, 18)),
            dma((18,)),
            dma((18,)),
        ],
        compiler_params=pltpu.CompilerParams(
            collective_id=2, has_side_effects=True, vmem_limit_bytes=60 * 1024 * 1024
        ),
        cost_estimate=pl.CostEstimate(
            flops=3_000_000_000, bytes_accessed=150_000_000, transcendentals=0
        ),
        name="gather_and_project",
    )(tokens, in_gain[None, :], raw_queries, q_gain[None, :], k_gain[None, :], cosine, sine, w_key, w_value)


def unturn(values, cosine, sine):
    return values * cosine - pltpu.roll(values, values.shape[-1] // 2, 1) * sine


def norm_back(grad, values, gain):
    scale = lax.rsqrt(jnp.mean(values * values, axis=1, keepdims=True) + EPSILON)
    unit = values * scale
    inner = grad * gain
    return scale * (inner - unit * jnp.mean(inner * unit, axis=1, keepdims=True))


def attend_kernel(
    query_ref, window_ref, out_grad_hbm, low_ref, raw_hbm, raw_key_ref, cos_ref, sin_ref, q_gain_ref, k_gain_ref,
    grad_query_ref, grad_kv_ref,
    exps, along, totals, query_total, parts, returned, out_grad_ref, raw_ref, passing,
    send_sem, recv_sem, middle_send, middle_recv, load_sem,
):
    shard = query_ref.shape[0]
    head_size = q_gain_ref.shape[1]
    kv_heads = raw_key_ref.shape[1] // head_size
    group_size = query_ref.shape[1] // raw_key_ref.shape[1]
    tile = shard // 2
    reach = 2 * shard
    place = lax.axis_index("seq")
    member = lax.axis_index("tp")
    count = lax.axis_size("seq")
    x = lax.rem(place, WIDE)

    def in_row(of, xs):
        return (of // WIDE * WIDE + xs, member)

    left, right = lax.rem(x + WIDE - 1, WIDE), lax.rem(x + 1, WIDE)
    later = (lax.rem(place + 1, count), member)
    earlier = (lax.rem(place + count - 1, count), member)
    middle_to = in_row(lax.rem(place + count - 2, count), right)
    middle_from = (lax.rem(place // WIDE * WIDE + right + 2, count), member)
    row_left, row_right = in_row(place, left), in_row(place, right)
    load_grads = pltpu.make_async_copy(out_grad_hbm, out_grad_ref, load_sem.at[0])
    load_grads.start()
    load_raw = pltpu.make_async_copy(raw_hbm, raw_ref, load_sem.at[1])
    load_raw.start()
    barrier = pltpu.get_barrier_semaphore()
    for other in [later, earlier, middle_to, middle_from, row_left, row_right]:
        pl.semaphore_signal(barrier, inc=1, device_id=other, device_id_type=MESH_IDS)

    totals[...] = jnp.zeros_like(totals)

    def across(left, right):
        return lax.dot_general(left, right, (((1,), (1,)), ((), ())), preferred_element_type=jnp.float32)

    def back(window, head):
        return pltpu.make_async_remote_copy(
            src_ref=parts.at[window, head] if window == 1 else passing.at[head],
            dst_ref=returned.at[window, head],
            send_sem=send_sem.at[window, head],
            recv_sem=recv_sem.at[window, head],
            device_id=earlier if window == 1 else row_right,
            device_id_type=MESH_IDS,
        )

    def middle(head):
        return pltpu.make_async_remote_copy(
            src_ref=parts.at[0, head],
            dst_ref=passing.at[head],
            send_sem=middle_send.at[head],
            recv_sem=middle_recv.at[head],
            device_id=middle_to,
            device_id_type=MESH_IDS,
        )

    load_grads.wait()
    load_raw.wait()
    for head in range(kv_heads):
        key_lanes = slice(head * head_size, (head + 1) * head_size)
        value_lanes = slice((kv_heads + head) * head_size, (kv_heads + head + 1) * head_size)
        lanes = [
            slice((head * group_size + member_of) * head_size, (head * group_size + member_of + 1) * head_size)
            for member_of in range(group_size)
        ]

        def half(step, carry):
            begin = pl.multiple_of(step * tile, tile)
            rows = pl.ds(begin, tile)
            queries = jnp.concatenate([query_ref[rows, at] for at in lanes], axis=0)
            grads = jnp.concatenate([out_grad_ref[rows, at] for at in lanes], axis=0)
            low = low_ref[step]
            low = jnp.concatenate([low] * group_size, axis=1)
            width = group_size * tile
            high = lax.broadcasted_iota(jnp.int32, (1, tile), 1) + (reach + begin)
            high = jnp.concatenate([high] * group_size, axis=1)

            def scores(index, stats):
                total, delta = stats
                first = pl.multiple_of(begin + index * tile, tile)
                key_rows = pl.ds(first, tile)
                score = across(window_ref[key_rows, key_lanes], queries)
                partial = across(window_ref[key_rows, value_lanes], grads)
                key = lax.broadcasted_iota(jnp.int32, (tile, width), 0) + first
                value = jnp.where((key >= low) & (key <= high), jnp.exp(score), 0.0)
                at = pl.ds(pl.multiple_of(index * tile, tile), tile)
                exps[at, :] = value
                along[at, :] = partial
                total = total + jnp.sum(value, axis=0, keepdims=True)
                delta = delta + jnp.sum(value * partial, axis=0, keepdims=True)
                return total, delta

            nothing = jnp.zeros((1, width), jnp.float32)
            total, delta = lax.fori_loop(0, reach // tile + 1, scores, (nothing, nothing))
            inverse = 1.0 / total
            delta = delta * inverse
            query_total[...] = jnp.zeros_like(query_total)

            def slopes(index, carry):
                key_rows = pl.ds(pl.multiple_of(begin + index * tile, tile), tile)
                at = pl.ds(pl.multiple_of(index * tile, tile), tile)
                probs = exps[at, :] * inverse
                slope = (probs * (along[at, :] - delta)).astype(jnp.bfloat16)
                query_total[...] += contract_first(window_ref[key_rows, key_lanes], slope)
                totals[key_rows, key_lanes] += jnp.dot(slope, queries, preferred_element_type=jnp.float32)
                totals[key_rows, value_lanes] += jnp.dot(
                    probs.astype(jnp.bfloat16), grads, preferred_element_type=jnp.float32
                )
                return carry

            lax.fori_loop(0, reach // tile + 1, slopes, 0)
            flipped = query_total[...].T
            for member_of, at in enumerate(lanes):
                grad = flipped[member_of * tile : (member_of + 1) * tile] * QUERY_SCALE
                grad = unturn(grad, cos_ref[rows, :], sin_ref[rows, :])
                values = raw_ref[rows, at].astype(jnp.float32)
                grad_query_ref[rows, at] = norm_back(grad, values, q_gain_ref[...]).astype(jnp.bfloat16)
            return carry

        lax.fori_loop(0, 2, half, 0)
        for window in range(2):
            rows = slice(window * shard, (window + 1) * shard)
            parts[window, head, :, :head_size] = totals[rows, key_lanes].astype(jnp.bfloat16)
            parts[window, head, :, head_size:] = totals[rows, value_lanes].astype(jnp.bfloat16)
        if head == 0:
            pl.semaphore_wait(barrier, 6)
        middle(head).start()
        back(1, head).start()

    for head in range(kv_heads):
        middle(head).wait_recv()
        back(0, head).start()
    own = slice(reach, reach + shard)
    for head in range(kv_heads):
        key_lanes = slice(head * head_size, (head + 1) * head_size)
        value_lanes = slice((kv_heads + head) * head_size, (kv_heads + head + 1) * head_size)
        for window in range(2):
            back(window, head).wait_recv()
        key_grad = totals[own, key_lanes]
        value_grad = totals[own, value_lanes]
        for window in (1, 0):
            key_grad = key_grad + returned[window, head, :, :head_size].astype(jnp.float32)
            value_grad = value_grad + returned[window, head, :, head_size:].astype(jnp.float32)
        grad_kv_ref[:, value_lanes] = value_grad.astype(jnp.bfloat16)
        key_grad = unturn(key_grad, cos_ref[...], sin_ref[...])
        grad_kv_ref[:, key_lanes] = norm_back(key_grad, raw_key_ref[:, key_lanes], k_gain_ref[...]).astype(
            jnp.bfloat16
        )
    for head in range(kv_heads):
        middle(head).wait_send()
        for window in range(2):
            back(window, head).wait_send()


def attend_back(query_rot, window, out_grad, low, raw_queries, raw_keys, cosine, sine, q_gain, k_gain):
    shard = query_rot.shape[0]
    head_size = q_gain.shape[0]
    kv_heads = raw_keys.shape[1] // head_size
    group_size = query_rot.shape[1] // raw_keys.shape[1]
    tile = shard // 2
    width = group_size * tile
    vmem = pl.BlockSpec(memory_space=pltpu.VMEM)
    outside = pl.BlockSpec(memory_space=pltpu.HBM)
    return pl.pallas_call(
        attend_kernel,
        out_shape=[
            jax.ShapeDtypeStruct(query_rot.shape, jnp.bfloat16),
            jax.ShapeDtypeStruct((shard, 2 * raw_keys.shape[1]), jnp.bfloat16),
        ],
        in_specs=[vmem, vmem, outside, vmem, outside] + [vmem] * 5,
        out_specs=[vmem] * 2,
        scratch_shapes=[
            pltpu.VMEM((2 * shard + tile, width), jnp.float32),
            pltpu.VMEM((2 * shard + tile, width), jnp.float32),
            pltpu.VMEM((3 * shard, 2 * raw_keys.shape[1]), jnp.float32),
            pltpu.VMEM((head_size, width), jnp.float32),
            pltpu.VMEM((2, kv_heads, shard, 2 * head_size), jnp.bfloat16),
            pltpu.VMEM((2, kv_heads, shard, 2 * head_size), jnp.bfloat16),
            pltpu.VMEM(query_rot.shape, jnp.bfloat16),
            pltpu.VMEM(query_rot.shape, jnp.bfloat16),
            pltpu.VMEM((kv_heads, shard, 2 * head_size), jnp.bfloat16),
            pltpu.SemaphoreType.DMA((2, kv_heads)),
            pltpu.SemaphoreType.DMA((2, kv_heads)),
            pltpu.SemaphoreType.DMA((kv_heads,)),
            pltpu.SemaphoreType.DMA((kv_heads,)),
            pltpu.SemaphoreType.DMA((2,)),
        ],
        compiler_params=pltpu.CompilerParams(
            collective_id=3, has_side_effects=True, vmem_limit_bytes=60 * 1024 * 1024
        ),
        cost_estimate=pl.CostEstimate(
            flops=8_000_000_000, bytes_accessed=100_000_000, transcendentals=3_000_000
        ),
        name="attend_back",
    )(
        query_rot, window.reshape(3 * shard, window.shape[2]), out_grad, low, raw_queries, raw_keys,
        cosine, sine, q_gain[None, :], k_gain[None, :],
    )


def finish_kernel(
    gathered_ref, grad_ref, w_key_ref, w_value_ref, tokens_ref, gain_ref,
    key_out, value_out, grad_x_ref,
    held, weights, tokens, total_own, corner_out, corner_in, beside_out, beside_in, cross_out, cross_in,
    relay_up, relay_down,
    key_term, value_term, key_send, order, value_total, key_next, value_next, last_send, last_recv,
    *rest,
):
    bufs_a, bufs_b, bufs_c, bufs_d = rest[0:6], rest[6:12], rest[12:18], rest[18:24]
    sems = rest[24:34]
    load_sem, weight_sem, pair_send, pair_recv, relay_send, relay_recv, cross_send, cross_recv = rest[34:]
    depth = gain_ref.shape[1]
    block = tokens_ref.shape[0]
    rows = key_out.shape[0]
    cols = key_out.shape[1]
    half = block // 2
    piece = half // 4
    big, mid = 16 * rows, 4 * rows
    split_big = big // 2
    split_mid = mid // 2 + mid // 2 % 16
    slab = 768 if depth % 768 == 0 else 128
    strip = 384 if depth % 384 == 0 else 128
    place = lax.axis_index("seq")
    member = lax.axis_index("tp")
    core = lax.rem(member, 2)
    upper = member // 2
    x = lax.rem(place, 4)
    z = lax.rem(place // 4, 4)
    y = place // 16
    height = upper * 4 + z

    def device(ys, zs, xs):
        return ((ys * 4 + zs) * 4 + xs, member)

    def along_z(by):
        other = lax.rem(height + by, 8)
        return ((y * 4 + lax.rem(other, 4)) * 4 + x, other // 4 * 2 + core)

    def remote(source, target, send_sem, recv_sem, to):
        return pltpu.make_async_remote_copy(
            src_ref=source,
            dst_ref=target,
            send_sem=send_sem,
            recv_sem=recv_sem,
            device_id=to,
            device_id_type=MESH_IDS,
        )

    def weight_load(step):
        at = pl.ds(pl.multiple_of(step * slab, slab), slab)
        return (
            pltpu.make_async_copy(w_key_ref.at[at], weights.at[at, pl.ds(0, cols)], weight_sem.at[0, step]),
            pltpu.make_async_copy(w_value_ref.at[at], weights.at[at, pl.ds(cols, cols)], weight_sem.at[1, step]),
        )

    for step in range(depth // slab):
        for one in weight_load(step):
            one.start()
    load_held = pltpu.make_async_copy(gathered_ref, held, load_sem.at[0])
    load_held.start()
    load_tokens = pltpu.make_async_copy(tokens_ref, tokens, load_sem.at[1])
    load_tokens.start()

    z_up, z_down = along_z(2), along_z(6)
    partner = (place, upper * 2 + 1 - core)
    x_up, x_down = device(y, z, lax.rem(x + 1, 4)), device(y, z, lax.rem(x + 3, 4))
    y_up, y_down = device(lax.rem(y + 1, 4), z, x), device(lax.rem(y + 3, 4), z, x)
    z_others = [device(y, lax.rem(z + d, 4), x) for d in (1, 2, 3)]
    barrier = pltpu.get_barrier_semaphore()
    for other in [z_up, z_down, partner, x_up, x_down, y_up, y_down] + z_others:
        pl.semaphore_signal(barrier, inc=1, device_id=other, device_id_type=MESH_IDS)

    own = pl.multiple_of(member * block, block)
    beside = pl.multiple_of((upper * 2 + 1 - core) * block, block)
    across = pl.multiple_of(((1 - upper) * 2 + core) * block, block)
    corner = pl.multiple_of(((1 - upper) * 2 + 1 - core) * block, block)

    def part(begin, store, first=False):
        grads = grad_ref[pl.ds(begin, block), :]

        def one_slab(step, carry):
            if first:
                for one in weight_load(step):
                    one.wait()
            at = pl.ds(pl.multiple_of(step * slab, slab), slab)
            store(at, contract_last(grads, weights[at, :]))
            return carry

        lax.fori_loop(0, depth // slab, one_slab, 0)

    def store_corner(at, value):
        corner_out[:, at] = value.astype(jnp.bfloat16)

    part(corner, store_corner, first=True)
    pl.semaphore_wait(barrier, 10)
    send_corner = remote(corner_out, corner_in, pair_send.at[0], pair_recv.at[0], partner)
    send_corner.start()

    def store_total(at, value):
        total_own[:, at] = value

    part(across, store_total)
    send_corner.wait_recv()

    def join(step, carry):
        at = pl.ds(pl.multiple_of(step * 16, 16), 16)
        cross_out[at, :] = (total_own[at, :] + corner_in[at, :].astype(jnp.float32)).astype(jnp.bfloat16)
        return carry

    lax.fori_loop(0, block // 16, join, 0)

    def rows_at(side, step):
        return pl.ds(side * half + step * piece, piece)

    def small(step):
        return pl.ds(step * piece, piece)

    first = [
        [
            remote(cross_out.at[rows_at(0, step)], relay_up.at[small(step)], relay_send.at[0, step], relay_recv.at[0, step], z_up),
            remote(cross_out.at[rows_at(1, step)], relay_down.at[small(step)], relay_send.at[1, step], relay_recv.at[1, step], z_down),
        ]
        for step in range(4)
    ]
    second = [
        [
            remote(relay_up.at[small(step)], cross_in.at[rows_at(0, step)], cross_send.at[0, step], cross_recv.at[0, step], z_up),
            remote(relay_down.at[small(step)], cross_in.at[rows_at(1, step)], cross_send.at[1, step], cross_recv.at[1, step], z_down),
        ]
        for step in range(4)
    ]
    for pair in first:
        for one in pair:
            one.start()

    def relay(step):
        for side in (0, 1):
            first[step][side].wait_recv()
            second[step][side].start()

    load_held.wait()

    def strips(step, carry):
        at = pl.ds(pl.multiple_of(step * strip, strip), strip)
        result = contract_first(held[:, at], grad_ref[...])
        key_term[at, :] = result[:, :cols]
        value_term[at, :] = result[:, cols:].astype(jnp.bfloat16)
        return carry

    lax.fori_loop(0, depth // strip, strips, 0)

    def finish_b1(total):
        for quarter in range(4):
            at = pl.ds(quarter * mid, mid)
            value_total[at, :] = total(at)
        for xs in range(4):
            for zs in range(4):
                order[zs * rows : zs * rows + rows, :] = value_total[
                    zs * mid + xs * rows : zs * mid + xs * rows + rows, :
                ]
            value_next[xs] = order[...].astype(jnp.bfloat16)

    second_b = ring_sum(
        lambda t: value_term.at[pl.ds(pl.multiple_of(t * big, 16), big)],
        big, split_big, y, y_up, y_down, bufs_b, sems[2:4], finish_b1,
    )

    for ys in range(4):
        for xs in range(4):
            for zs in range(4):
                begin = ((ys * 4 + zs) * 4 + xs) * rows
                order[zs * rows : zs * rows + rows, :] = key_term[begin : begin + rows, :]
            key_send[xs, ys * mid : ys * mid + mid, :] = order[...].astype(jnp.bfloat16)

    def finish_a1(total):
        for quarter in range(4):
            at = pl.ds(quarter * mid, mid)
            key_next[quarter] = total(at).astype(jnp.bfloat16)

    second_a = ring_sum(
        lambda t: key_send.at[t],
        big, split_big, x, x_up, x_down, bufs_a, sems[0:2], finish_a1,
    )
    relay(0)

    def store_beside(at, value):
        beside_out[:, at] = value.astype(jnp.bfloat16)

    part(beside, store_beside)
    send_beside = remote(beside_out, beside_in, pair_send.at[1], pair_recv.at[1], partner)
    send_beside.start()
    part(own, store_total)
    relay(1)
    third_b = second_b()
    third_a = second_a()
    relay(2)
    drain_b = third_b()

    def finish_last(at):
        def finish(total):
            order[...] = total(pl.ds(0, mid))
            for zs in range(4):
                last_send[zs, 0:rows, at : at + cols] = order[
                    zs * rows : zs * rows + rows, :
                ].astype(jnp.bfloat16)
                last_send[zs, rows:, at : at + cols] = jnp.zeros(
                    (last_send.shape[1] - rows, cols), jnp.bfloat16
                )

        return finish

    second_d = ring_sum(
        lambda t: value_next.at[t],
        mid, split_mid, x, x_up, x_down, bufs_d, sems[6:8], finish_last(cols),
    )
    relay(3)
    drain_a = third_a()
    second_c = ring_sum(
        lambda t: key_next.at[t],
        mid, split_mid, y, y_up, y_down, bufs_c, sems[4:6], finish_last(0),
    )
    third_d = second_d()
    third_c = second_c()
    drain_d = third_d()
    drain_c = third_c()
    copies = []
    for d in (1, 2, 3):
        one = remote(
            last_send.at[lax.rem(z + d, 4)], last_recv.at[d - 1], sems[8].at[d - 1], sems[9].at[d - 1], z_others[d - 1]
        )
        one.start()
        copies.append(one)

    load_tokens.wait()
    send_beside.wait_recv()
    for step in range(4):
        for side in (0, 1):
            second[step][side].wait_recv()
            at = rows_at(side, step)
            grad = (
                total_own[at, :] + beside_in[at, :].astype(jnp.float32) + cross_in[at, :].astype(jnp.float32)
            )
            grad_x_ref[at, :] = norm_back(grad, tokens[at, :].astype(jnp.float32), gain_ref[...]).astype(
                jnp.bfloat16
            )

    for one in copies:
        one.wait_recv()
    total = last_send[z, 0:rows, :].astype(jnp.float32)
    for d in range(3):
        total = total + last_recv[d, 0:rows, :].astype(jnp.float32)
    key_out[...] = total[:, 0:cols]
    value_out[...] = total[:, cols:]
    for one in copies:
        one.wait_send()
    for drain in (drain_a, drain_b, drain_c, drain_d):
        drain()
    send_corner.wait_send()
    send_beside.wait_send()
    for pair in first + second:
        for one in pair:
            one.wait_send()


def finish(gathered, grad_kv, w_key, w_value, tokens, in_gain):
    shard, depth = gathered.shape
    block = tokens.shape[0]
    cols = w_key.shape[1]
    rows = depth // 64
    big, mid = 16 * rows, 4 * rows
    split_big = big // 2
    split_mid = mid // 2 + mid // 2 % 16
    padded = (rows + 15) // 16 * 16
    slabs = depth // (768 if depth % 768 == 0 else 128)
    bf = jnp.bfloat16
    dma = pltpu.SemaphoreType.DMA
    vmem = pl.BlockSpec(memory_space=pltpu.VMEM)
    outside = pl.BlockSpec(memory_space=pltpu.HBM)

    def bufs(size, split):
        return [
            pltpu.VMEM((split, cols), bf),
            pltpu.VMEM((size - split, cols), bf),
            pltpu.VMEM((split, cols), bf),
            pltpu.VMEM((size - split, cols), bf),
            pltpu.VMEM((size, cols), bf),
            pltpu.VMEM((size, cols), bf),
        ]

    return pl.pallas_call(
        finish_kernel,
        out_shape=[
            jax.ShapeDtypeStruct((rows, cols), jnp.float32),
            jax.ShapeDtypeStruct((rows, cols), jnp.float32),
            jax.ShapeDtypeStruct((block, depth), bf),
        ],
        in_specs=[outside, vmem, outside, outside, outside, vmem],
        out_specs=[vmem] * 3,
        scratch_shapes=[
            pltpu.VMEM((shard, depth), bf),
            pltpu.VMEM((depth, 2 * cols), bf),
            pltpu.VMEM((block, depth), bf),
            pltpu.VMEM((block, depth), jnp.float32),
        ]
        + [pltpu.VMEM((block, depth), bf)] * 6
        + [pltpu.VMEM((block // 2, depth), bf)] * 2
        + [
            pltpu.VMEM((depth, cols), jnp.float32),
            pltpu.VMEM((depth, cols), bf),
            pltpu.VMEM((4, big, cols), bf),
            pltpu.VMEM((mid, cols), jnp.float32),
            pltpu.VMEM((big, cols), jnp.float32),
            pltpu.VMEM((4, mid, cols), bf),
            pltpu.VMEM((4, mid, cols), bf),
            pltpu.VMEM((4, padded, 2 * cols), bf),
            pltpu.VMEM((3, padded, 2 * cols), bf),
        ]
        + bufs(big, split_big)
        + bufs(big, split_big)
        + bufs(mid, split_mid)
        + bufs(mid, split_mid)
        + [dma((6,))] * 8
        + [dma((3,))] * 2
        + [dma((2,)), dma((2, slabs)), dma((2,)), dma((2,))]
        + [dma((2, 4))] * 4,
        compiler_params=pltpu.CompilerParams(
            collective_id=1, has_side_effects=True, vmem_limit_bytes=60 * 1024 * 1024
        ),
        cost_estimate=pl.CostEstimate(
            flops=6_000_000_000, bytes_accessed=150_000_000, transcendentals=0
        ),
        name="finish",
    )(gathered, grad_kv, w_key, w_value, tokens, in_gain[None, :])


def shards(tokens, in_gain, raw_queries, w_key, w_value, q_gain, k_gain, doc_lengths, out_grad):
    head_size = q_gain.shape[0]
    shard_rows = tokens.shape[0] * lax.axis_size("tp")
    reach = 2 * shard_rows
    first_row = lax.axis_index("seq") * shard_rows
    positions = first_row + jnp.arange(shard_rows, dtype=jnp.int32)
    begins = doc_begin(doc_lengths, positions)
    lowest = jnp.maximum(begins, positions - (WINDOW - 1))
    low = (lowest - (first_row - reach)).reshape(2, 1, shard_rows // 2)
    cosine, sine = angle_tables(positions - begins, head_size)
    gathered, query_rot, raw_keys, window = gather_and_project(
        tokens, in_gain, raw_queries, w_key, w_value, q_gain, k_gain, cosine, sine
    )
    grad_queries, grad_kv = attend_back(
        query_rot, window, out_grad, low, raw_queries, raw_keys, cosine, sine, q_gain, k_gain
    )
    grad_wk, grad_wv, grad_x = finish(gathered, grad_kv, w_key, w_value, tokens, in_gain)
    return (grad_x, grad_queries, grad_wk, grad_wv)


def solution(mesh):
    placed = (
        P(("seq", "tp"), None),
        P(),
        P("seq", "tp"),
        P(None, "tp"),
        P(None, "tp"),
        P(),
        P(),
        P(),
        P("seq", "tp"),
    )
    return jax.shard_map(
        shards,
        mesh=mesh,
        in_specs=placed,
        out_specs=(P(("seq", "tp"), None), P("seq", "tp"), P("seq", "tp"), P("seq", "tp")),
        check_vma=False,
    )
```

```python
import functools

import jax
import jax.numpy as jnp
from jax import lax
from jax.experimental import pallas as pl
from jax.experimental.pallas import tpu as pltpu
from jax.sharding import PartitionSpec as P

WINDOW = 1024
WIDE = 4


EPSILON = 1e-06
QUERY_SCALE = 168.0 ** (-0.5)
ROPE_BASE = 10000.0


def doc_begin(doc_lengths, positions):
    endings = jnp.cumsum(doc_lengths, dtype=jnp.int32)
    starts = endings - doc_lengths
    inside = starts[None, :] <= positions[:, None]
    return jnp.max(jnp.where(inside, starts[None, :], jnp.zeros_like(starts)[None, :]), axis=1)


def angle_tables(positions, head_size):
    half_size = head_size // 2
    powers = jnp.arange(half_size, dtype=jnp.float32) * (2.0 / head_size)
    frequency = ROPE_BASE ** (-powers)
    angles = positions.astype(jnp.float32)[:, None] * frequency[None, :]
    cosine = jnp.cos(angles)
    sine = jnp.sin(angles)
    return jnp.concatenate([cosine, cosine], axis=1), jnp.concatenate([-sine, sine], axis=1)


def contract_last(left, right):
    return lax.dot_general(
        left, right, (((1,), (1,)), ((), ())), preferred_element_type=jnp.float32
    )


def contract_first(left, right):
    return lax.dot_general(
        left, right, (((0,), (0,)), ((), ())), preferred_element_type=jnp.float32
    )


MESH_IDS = pl.DeviceIdType.MESH


def ring_sum(piece, size, split, pos, up, down, bufs, sems, finish):
    half_up, half_down, mixed_up, mixed_down, full_up, full_down = bufs
    send_sem, recv_sem = sems
    far = lax.rem(pos + 2, 4)
    after = lax.rem(pos + 1, 4)
    before = lax.rem(pos + 3, 4)
    low = pl.ds(0, split)
    high = pl.ds(split, size - split)

    def copy(index, source, target, device):
        return pltpu.make_async_remote_copy(
            src_ref=source,
            dst_ref=target,
            send_sem=send_sem.at[index],
            recv_sem=recv_sem.at[index],
            device_id=device,
            device_id_type=MESH_IDS,
        )

    first = [
        copy(0, piece(far).at[low], half_up, up),
        copy(1, piece(far).at[high], half_down, down),
        copy(2, piece(after).at[high], full_up.at[high], up),
        copy(3, piece(before).at[low], full_down.at[low], down),
    ]
    for one in first:
        one.start()

    def second():
        first[0].wait_recv()
        mixed_up[...] = (
            piece(after)[low, :].astype(jnp.float32) + half_up[...].astype(jnp.float32)
        ).astype(jnp.bfloat16)
        last_up = copy(4, mixed_up, full_up.at[low], up)
        last_up.start()
        first[1].wait_recv()
        mixed_down[...] = (
            piece(before)[high, :].astype(jnp.float32) + half_down[...].astype(jnp.float32)
        ).astype(jnp.bfloat16)
        last_down = copy(5, mixed_down, full_down.at[high], down)
        last_down.start()

        def third():
            first[2].wait_recv()
            first[3].wait_recv()
            last_up.wait_recv()
            last_down.wait_recv()
            finish(
                lambda rows: piece(pos)[rows, :].astype(jnp.float32)
                + full_up[rows, :].astype(jnp.float32)
                + full_down[rows, :].astype(jnp.float32)
            )

            def drain():
                for one in first + [last_up, last_down]:
                    one.wait_send()

            return drain

        return third

    return second


def turn(values, cosine, sine):
    return values * cosine + pltpu.roll(values, values.shape[-1] // 2, 1) * sine


def gather_kernel(
    tokens_hbm, gain_ref, raw_hbm, q_gain_ref, k_gain_ref, cos_ref, sin_ref, w_key_ref, w_value_ref,
    gathered_ref, query_ref, raw_key_ref, window_ref,
    held, relay_up, relay_down, weights, window, tokens_ref, raw_ref, passing,
    weight_sem, out_sem, window_sem, relay_send, relay_recv, cross_send, cross_recv,
    pair_send, pair_recv, chunk_send, chunk_recv, halo_send, halo_recv, middle_send, middle_recv,
):
    rows = tokens_ref.shape[0]
    half = rows // 2
    piece = half // 4
    cols = w_key_ref.shape[1]
    head_size = k_gain_ref.shape[1]
    place = lax.axis_index("seq")
    member = lax.axis_index("tp")
    count = lax.axis_size("seq")
    core = lax.rem(member, 2)
    upper = member // 2
    x = lax.rem(place, WIDE)
    z = upper * 4 + lax.rem(place // WIDE, 4)
    y = place // (4 * WIDE)

    def along_z(by):
        other = lax.rem(z + by, 8)
        return ((y * 4 + lax.rem(other, 4)) * WIDE + x, other // 4 * 2 + core)

    z_up, z_down = along_z(2), along_z(6)
    partner = (place, upper * 2 + 1 - core)
    later = (lax.rem(place + 1, count), member)
    earlier = (lax.rem(place + count - 1, count), member)

    def in_row(of, xs):
        return (of // WIDE * WIDE + xs, member)

    left, right = lax.rem(x + WIDE - 1, WIDE), lax.rem(x + 1, WIDE)
    row_left, row_right = in_row(place, left), in_row(place, right)
    second_to = (lax.rem(place // WIDE * WIDE + right + 2, count), member)
    second_from = in_row(lax.rem(place + count - 2, count), lax.rem(x + 2 * WIDE - 3, WIDE))

    def remote(source, target, send_sem, recv_sem, device):
        return pltpu.make_async_remote_copy(
            src_ref=source,
            dst_ref=target,
            send_sem=send_sem,
            recv_sem=recv_sem,
            device_id=device,
            device_id_type=MESH_IDS,
        )

    load_tokens = pltpu.make_async_copy(tokens_hbm, tokens_ref, weight_sem.at[2])
    load_tokens.start()
    load_raw = pltpu.make_async_copy(raw_hbm, raw_ref, weight_sem.at[3])
    load_raw.start()
    loads = [
        pltpu.make_async_copy(w_key_ref, weights.at[:, pl.ds(0, cols)], weight_sem.at[0]),
        pltpu.make_async_copy(w_value_ref, weights.at[:, pl.ds(cols, cols)], weight_sem.at[1]),
    ]
    for one in loads:
        one.start()
    barrier = pltpu.get_barrier_semaphore()
    for other in [z_up, z_down, partner, later, earlier, second_to, second_from, row_left, row_right]:
        pl.semaphore_signal(barrier, inc=1, device_id=other, device_id_type=MESH_IDS)

    own = pl.multiple_of(member * rows, rows)
    beside = pl.multiple_of((upper * 2 + 1 - core) * rows, rows)
    across = pl.multiple_of(((1 - upper) * 2 + core) * rows, rows)
    corner = pl.multiple_of(((1 - upper) * 2 + 1 - core) * rows, rows)

    def norm_rows(step, carry):
        at = pl.ds(pl.multiple_of(step * 16, 16), 16)
        values = tokens_ref[at, :].astype(jnp.float32)
        scale = lax.rsqrt(jnp.mean(values * values, axis=1, keepdims=True) + EPSILON)
        held[pl.ds(pl.multiple_of(own + step * 16, 16), 16), :] = (
            values * scale * gain_ref[...]
        ).astype(jnp.bfloat16)
        return carry

    load_tokens.wait()
    lax.fori_loop(0, rows // 16, norm_rows, 0)
    pl.semaphore_wait(barrier, 9)

    to_partner = remote(
        held.at[pl.ds(own, rows)], held.at[pl.ds(own, rows)], pair_send.at[0], pair_recv.at[0], partner
    )
    to_partner.start()

    def first_up(step):
        return remote(
            held.at[pl.ds(pl.multiple_of(own + step * piece, piece), piece)],
            relay_up.at[pl.ds(pl.multiple_of(step * piece, piece), piece)],
            relay_send.at[0, step], relay_recv.at[0, step], z_up,
        )

    def first_down(step):
        return remote(
            held.at[pl.ds(pl.multiple_of(own + half + step * piece, piece), piece)],
            relay_down.at[pl.ds(pl.multiple_of(step * piece, piece), piece)],
            relay_send.at[1, step], relay_recv.at[1, step], z_down,
        )

    def second_up(step):
        target = pl.multiple_of(((1 - lax.rem(z + 2, 8) // 4) * 2 + core) * rows + step * piece, piece)
        return remote(
            relay_up.at[pl.ds(pl.multiple_of(step * piece, piece), piece)],
            held.at[pl.ds(target, piece)],
            cross_send.at[0, step], cross_recv.at[0, step], z_up,
        )

    def second_down(step):
        target = pl.multiple_of(
            ((1 - lax.rem(z + 6, 8) // 4) * 2 + core) * rows + half + step * piece, piece
        )
        return remote(
            relay_down.at[pl.ds(pl.multiple_of(step * piece, piece), piece)],
            held.at[pl.ds(target, piece)],
            cross_send.at[1, step], cross_recv.at[1, step], z_down,
        )

    def pass_on(side, step):
        at = pl.ds(pl.multiple_of(across + side * half + step * piece, piece), piece)
        return remote(held.at[at], held.at[at], chunk_send.at[side, step], chunk_recv.at[side, step], partner)

    for step in range(2):
        first_up(step).start()
        first_down(step).start()

    def halo(by, index, begin, size):
        at = pl.ds(begin, size)
        return remote(
            window.at[2, at] if by == 1 else passing.at[at],
            window.at[2 - by, at],
            halo_send.at[by - 1, index], halo_recv.at[by - 1, index], later if by == 1 else second_to,
        )

    def middle(index, begin, size):
        at = pl.ds(begin, size)
        return remote(
            window.at[2, at], passing.at[at], middle_send.at[index], middle_recv.at[index], row_left
        )

    def hand_on(index, begin, size):
        middle(index, begin, size).wait_recv()
        halo(2, index, begin, size).start()

    def project(parts):
        block = [held[pl.ds(begin, size), :] for begin, size in parts]
        block = block[0] if len(block) == 1 else jnp.concatenate(block, axis=0)
        result = jnp.dot(block, weights[...], preferred_element_type=jnp.float32)
        at = 0
        for begin, size in parts:
            mine = result[at : at + size]
            at += size
            where = pl.ds(begin, size)
            raw_key_ref[where, :] = mine[:, :cols]
            window[2, where, cols:] = mine[:, cols:].astype(jnp.bfloat16)
            for head in range(cols // head_size):
                lanes = slice(head * head_size, (head + 1) * head_size)
                values = mine[:, lanes]
                scale = lax.rsqrt(jnp.mean(values * values, axis=1, keepdims=True) + EPSILON)
                values = values * scale * k_gain_ref[...]
                window[2, where, lanes] = turn(values, cos_ref[where, :], sin_ref[where, :]).astype(
                    jnp.bfloat16
                )

    out_own = pltpu.make_async_copy(
        held.at[pl.ds(own, rows)], gathered_ref.at[pl.ds(own, rows)], out_sem.at[0]
    )
    out_own.start()
    for one in loads:
        one.wait()
    project([(own, rows)])
    halo(1, 0, own, rows).start()
    middle(0, own, rows).start()
    to_partner.wait_recv()
    out_beside = pltpu.make_async_copy(
        held.at[pl.ds(beside, rows)], gathered_ref.at[pl.ds(beside, rows)], out_sem.at[1]
    )
    out_beside.start()
    project([(beside, rows)])
    halo(1, 1, beside, rows).start()
    middle(1, beside, rows).start()
    for step in range(2, 4):
        first_up(step).start()
        first_down(step).start()

    load_raw.wait()
    for head in range(raw_ref.shape[1] // head_size):
        lanes = slice(head * head_size, (head + 1) * head_size)
        values = raw_ref[:, lanes].astype(jnp.float32)
        scale = lax.rsqrt(jnp.mean(values * values, axis=1, keepdims=True) + EPSILON)
        values = values * scale * q_gain_ref[...]
        query_ref[:, lanes] = (turn(values, cos_ref[...], sin_ref[...]) * QUERY_SCALE).astype(
            jnp.bfloat16
        )

    for step in range(4):
        first_up(step).wait_recv()
        second_up(step).start()
        first_down(step).wait_recv()
        second_down(step).start()
        if step == 0:
            hand_on(0, own, rows)
            hand_on(1, beside, rows)

    def groups(step):
        return [
            (pl.multiple_of(base + side * half + step * piece, piece), piece)
            for base in (across, corner)
            for side in (0, 1)
        ]

    def arrive(step, carry):
        for side, copy in ((0, second_up(step)), (1, second_down(step))):
            copy.wait_recv()
            pass_on(side, step).start()

        @pl.when(step > 0)
        def before():
            for index, (begin, size) in enumerate(groups(step - 1)):
                hand_on(2 + (step - 1) * 4 + index, begin, size)

        for side in (0, 1):
            pass_on(side, step).wait_recv()
        project(groups(step))
        for index, (begin, size) in enumerate(groups(step)):
            halo(1, 2 + step * 4 + index, begin, size).start()
            middle(2 + step * 4 + index, begin, size).start()
        return carry

    lax.fori_loop(0, 4, arrive, 0)
    for index, (begin, size) in enumerate(groups(3)):
        hand_on(14 + index, begin, size)
    out_across = pltpu.make_async_copy(
        held.at[pl.ds(across, rows)], gathered_ref.at[pl.ds(across, rows)], out_sem.at[2]
    )
    out_corner = pltpu.make_async_copy(
        held.at[pl.ds(corner, rows)], gathered_ref.at[pl.ds(corner, rows)], out_sem.at[3]
    )
    out_across.start()
    out_corner.start()

    def each_halo(kinds, act):
        for kind in kinds:
            act(kind(0, own, rows))
            act(kind(1, beside, rows))

            def inner(step, carry):
                for index, (begin, size) in enumerate(groups(step)):
                    act(kind(2 + step * 4 + index, begin, size))
                return carry

            lax.fori_loop(0, 4, inner, 0)

    halos = [functools.partial(halo, 1), functools.partial(halo, 2)]
    each_halo(halos, lambda copy: copy.wait_recv())
    out_window = pltpu.make_async_copy(window, window_ref, window_sem.at[0])
    out_window.start()
    each_halo(halos + [middle], lambda copy: copy.wait_send())
    to_partner.wait_send()
    for step in range(4):
        first_up(step).wait_send()
        first_down(step).wait_send()
        second_up(step).wait_send()
        second_down(step).wait_send()
        pass_on(0, step).wait_send()
        pass_on(1, step).wait_send()
    for one in (out_own, out_beside, out_across, out_corner, out_window):
        one.wait()


def gather_and_project(tokens, in_gain, raw_queries, w_key, w_value, q_gain, k_gain, cosine, sine):
    rows, depth = tokens.shape
    shard = rows * 4
    cols = w_key.shape[1]
    bf = jnp.bfloat16
    vmem = pl.BlockSpec(memory_space=pltpu.VMEM)
    anywhere = pl.BlockSpec(memory_space=pl.ANY)
    outside = pl.BlockSpec(memory_space=pltpu.HBM)
    dma = pltpu.SemaphoreType.DMA
    return pl.pallas_call(
        gather_kernel,
        out_shape=[
            jax.ShapeDtypeStruct((shard, depth), bf),
            jax.ShapeDtypeStruct(raw_queries.shape, bf),
            jax.ShapeDtypeStruct((shard, cols), jnp.float32),
            jax.ShapeDtypeStruct((3, shard, 2 * cols), bf),
        ],
        in_specs=[outside, vmem, outside] + [vmem] * 4 + [outside] * 2,
        out_specs=[anywhere, vmem, vmem, anywhere],
        scratch_shapes=[
            pltpu.VMEM((shard, depth), bf),
            pltpu.VMEM((rows // 2, depth), bf),
            pltpu.VMEM((rows // 2, depth), bf),
            pltpu.VMEM((depth, 2 * cols), bf),
            pltpu.VMEM((3, shard, 2 * cols), bf),
            pltpu.VMEM((rows, depth), bf),
            pltpu.VMEM(raw_queries.shape, bf),
            pltpu.VMEM((shard, 2 * cols), bf),
            dma((4,)),
            dma((4,)),
            dma((1,)),
            dma((2, 4)),
            dma((2, 4)),
            dma((2, 4)),
            dma((2, 4)),
            dma((1,)),
            dma((1,)),
            dma((2, 4)),
            dma((2, 4)),
            dma((2, 18)),
            dma((2, 18)),
            dma((18,)),
            dma((18,)),
        ],
        compiler_params=pltpu.CompilerParams(
            collective_id=2, has_side_effects=True, vmem_limit_bytes=60 * 1024 * 1024
        ),
        cost_estimate=pl.CostEstimate(
            flops=3_000_000_000, bytes_accessed=150_000_000, transcendentals=0
        ),
        name="gather_and_project",
    )(tokens, in_gain[None, :], raw_queries, q_gain[None, :], k_gain[None, :], cosine, sine, w_key, w_value)


def unturn(values, cosine, sine):
    return values * cosine - pltpu.roll(values, values.shape[-1] // 2, 1) * sine


def norm_back(grad, values, gain):
    scale = lax.rsqrt(jnp.mean(values * values, axis=1, keepdims=True) + EPSILON)
    unit = values * scale
    inner = grad * gain
    return scale * (inner - unit * jnp.mean(inner * unit, axis=1, keepdims=True))


def attend_kernel(
    query_ref, window_ref, out_grad_hbm, low_ref, raw_hbm, raw_key_ref, cos_ref, sin_ref, q_gain_ref, k_gain_ref,
    grad_query_ref, grad_kv_ref,
    exps, along, totals, query_total, parts, returned, out_grad_ref, raw_ref, passing,
    send_sem, recv_sem, middle_send, middle_recv, load_sem,
):
    shard = query_ref.shape[0]
    head_size = q_gain_ref.shape[1]
    kv_heads = raw_key_ref.shape[1] // head_size
    group_size = query_ref.shape[1] // raw_key_ref.shape[1]
    tile = shard // 2
    reach = 2 * shard
    place = lax.axis_index("seq")
    member = lax.axis_index("tp")
    count = lax.axis_size("seq")
    x = lax.rem(place, WIDE)

    def in_row(of, xs):
        return (of // WIDE * WIDE + xs, member)

    left, right = lax.rem(x + WIDE - 1, WIDE), lax.rem(x + 1, WIDE)
    later = (lax.rem(place + 1, count), member)
    earlier = (lax.rem(place + count - 1, count), member)
    middle_to = in_row(lax.rem(place + count - 2, count), right)
    middle_from = (lax.rem(place // WIDE * WIDE + right + 2, count), member)
    row_left, row_right = in_row(place, left), in_row(place, right)
    load_grads = pltpu.make_async_copy(out_grad_hbm, out_grad_ref, load_sem.at[0])
    load_grads.start()
    load_raw = pltpu.make_async_copy(raw_hbm, raw_ref, load_sem.at[1])
    load_raw.start()
    barrier = pltpu.get_barrier_semaphore()
    for other in [later, earlier, middle_to, middle_from, row_left, row_right]:
        pl.semaphore_signal(barrier, inc=1, device_id=other, device_id_type=MESH_IDS)

    totals[...] = jnp.zeros_like(totals)

    def across(left, right):
        return lax.dot_general(left, right, (((1,), (1,)), ((), ())), preferred_element_type=jnp.float32)

    def back(window, head):
        return pltpu.make_async_remote_copy(
            src_ref=parts.at[window, head] if window == 1 else passing.at[head],
            dst_ref=returned.at[window, head],
            send_sem=send_sem.at[window, head],
            recv_sem=recv_sem.at[window, head],
            device_id=earlier if window == 1 else row_right,
            device_id_type=MESH_IDS,
        )

    def middle(head):
        return pltpu.make_async_remote_copy(
            src_ref=parts.at[0, head],
            dst_ref=passing.at[head],
            send_sem=middle_send.at[head],
            recv_sem=middle_recv.at[head],
            device_id=middle_to,
            device_id_type=MESH_IDS,
        )

    load_grads.wait()
    load_raw.wait()
    for head in range(kv_heads):
        key_lanes = slice(head * head_size, (head + 1) * head_size)
        value_lanes = slice((kv_heads + head) * head_size, (kv_heads + head + 1) * head_size)
        lanes = [
            slice((head * group_size + member_of) * head_size, (head * group_size + member_of + 1) * head_size)
            for member_of in range(group_size)
        ]

        def half(step, carry):
            begin = pl.multiple_of(step * tile, tile)
            rows = pl.ds(begin, tile)
            queries = jnp.concatenate([query_ref[rows, at] for at in lanes], axis=0)
            grads = jnp.concatenate([out_grad_ref[rows, at] for at in lanes], axis=0)
            low = low_ref[step]
            low = jnp.concatenate([low] * group_size, axis=1)
            width = group_size * tile
            high = lax.broadcasted_iota(jnp.int32, (1, tile), 1) + (reach + begin)
            high = jnp.concatenate([high] * group_size, axis=1)

            def scores(index, stats):
                total, delta = stats
                first = pl.multiple_of(begin + index * tile, tile)
                key_rows = pl.ds(first, tile)
                score = across(window_ref[key_rows, key_lanes], queries)
                partial = across(window_ref[key_rows, value_lanes], grads)
                key = lax.broadcasted_iota(jnp.int32, (tile, width), 0) + first
                value = jnp.where((key >= low) & (key <= high), jnp.exp(score), 0.0)
                at = pl.ds(pl.multiple_of(index * tile, tile), tile)
                exps[at, :] = value
                along[at, :] = partial
                total = total + jnp.sum(value, axis=0, keepdims=True)
                delta = delta + jnp.sum(value * partial, axis=0, keepdims=True)
                return total, delta

            nothing = jnp.zeros((1, width), jnp.float32)
            total, delta = lax.fori_loop(0, reach // tile + 1, scores, (nothing, nothing))
            inverse = 1.0 / total
            delta = delta * inverse
            query_total[...] = jnp.zeros_like(query_total)

            def slopes(index, carry):
                key_rows = pl.ds(pl.multiple_of(begin + index * tile, tile), tile)
                at = pl.ds(pl.multiple_of(index * tile, tile), tile)
                probs = exps[at, :] * inverse
                slope = (probs * (along[at, :] - delta)).astype(jnp.bfloat16)
                query_total[...] += contract_first(window_ref[key_rows, key_lanes], slope)
                totals[key_rows, key_lanes] += jnp.dot(slope, queries, preferred_element_type=jnp.float32)
                totals[key_rows, value_lanes] += jnp.dot(
                    probs.astype(jnp.bfloat16), grads, preferred_element_type=jnp.float32
                )
                return carry

            lax.fori_loop(0, reach // tile + 1, slopes, 0)
            flipped = query_total[...].T
            for member_of, at in enumerate(lanes):
                grad = flipped[member_of * tile : (member_of + 1) * tile] * QUERY_SCALE
                grad = unturn(grad, cos_ref[rows, :], sin_ref[rows, :])
                values = raw_ref[rows, at].astype(jnp.float32)
                grad_query_ref[rows, at] = norm_back(grad, values, q_gain_ref[...]).astype(jnp.bfloat16)
            return carry

        lax.fori_loop(0, 2, half, 0)
        for window in range(2):
            rows = slice(window * shard, (window + 1) * shard)
            parts[window, head, :, :head_size] = totals[rows, key_lanes].astype(jnp.bfloat16)
            parts[window, head, :, head_size:] = totals[rows, value_lanes].astype(jnp.bfloat16)
        if head == 0:
            pl.semaphore_wait(barrier, 6)
        middle(head).start()
        back(1, head).start()

    for head in range(kv_heads):
        middle(head).wait_recv()
        back(0, head).start()
    own = slice(reach, reach + shard)
    for head in range(kv_heads):
        key_lanes = slice(head * head_size, (head + 1) * head_size)
        value_lanes = slice((kv_heads + head) * head_size, (kv_heads + head + 1) * head_size)
        for window in range(2):
            back(window, head).wait_recv()
        key_grad = totals[own, key_lanes]
        value_grad = totals[own, value_lanes]
        for window in (1, 0):
            key_grad = key_grad + returned[window, head, :, :head_size].astype(jnp.float32)
            value_grad = value_grad + returned[window, head, :, head_size:].astype(jnp.float32)
        grad_kv_ref[:, value_lanes] = value_grad.astype(jnp.bfloat16)
        key_grad = unturn(key_grad, cos_ref[...], sin_ref[...])
        grad_kv_ref[:, key_lanes] = norm_back(key_grad, raw_key_ref[:, key_lanes], k_gain_ref[...]).astype(
            jnp.bfloat16
        )
    for head in range(kv_heads):
        middle(head).wait_send()
        for window in range(2):
            back(window, head).wait_send()


def attend_back(query_rot, window, out_grad, low, raw_queries, raw_keys, cosine, sine, q_gain, k_gain):
    shard = query_rot.shape[0]
    head_size = q_gain.shape[0]
    kv_heads = raw_keys.shape[1] // head_size
    group_size = query_rot.shape[1] // raw_keys.shape[1]
    tile = shard // 2
    width = group_size * tile
    vmem = pl.BlockSpec(memory_space=pltpu.VMEM)
    outside = pl.BlockSpec(memory_space=pltpu.HBM)
    return pl.pallas_call(
        attend_kernel,
        out_shape=[
            jax.ShapeDtypeStruct(query_rot.shape, jnp.bfloat16),
            jax.ShapeDtypeStruct((shard, 2 * raw_keys.shape[1]), jnp.bfloat16),
        ],
        in_specs=[vmem, vmem, outside, vmem, outside] + [vmem] * 5,
        out_specs=[vmem] * 2,
        scratch_shapes=[
            pltpu.VMEM((2 * shard + tile, width), jnp.float32),
            pltpu.VMEM((2 * shard + tile, width), jnp.float32),
            pltpu.VMEM((3 * shard, 2 * raw_keys.shape[1]), jnp.float32),
            pltpu.VMEM((head_size, width), jnp.float32),
            pltpu.VMEM((2, kv_heads, shard, 2 * head_size), jnp.bfloat16),
            pltpu.VMEM((2, kv_heads, shard, 2 * head_size), jnp.bfloat16),
            pltpu.VMEM(query_rot.shape, jnp.bfloat16),
            pltpu.VMEM(query_rot.shape, jnp.bfloat16),
            pltpu.VMEM((kv_heads, shard, 2 * head_size), jnp.bfloat16),
            pltpu.SemaphoreType.DMA((2, kv_heads)),
            pltpu.SemaphoreType.DMA((2, kv_heads)),
            pltpu.SemaphoreType.DMA((kv_heads,)),
            pltpu.SemaphoreType.DMA((kv_heads,)),
            pltpu.SemaphoreType.DMA((2,)),
        ],
        compiler_params=pltpu.CompilerParams(
            collective_id=3, has_side_effects=True, vmem_limit_bytes=60 * 1024 * 1024
        ),
        cost_estimate=pl.CostEstimate(
            flops=8_000_000_000, bytes_accessed=100_000_000, transcendentals=3_000_000
        ),
        name="attend_back",
    )(
        query_rot, window.reshape(3 * shard, window.shape[2]), out_grad, low, raw_queries, raw_keys,
        cosine, sine, q_gain[None, :], k_gain[None, :],
    )


def finish_kernel(
    gathered_ref, grad_ref, w_key_ref, w_value_ref, tokens_ref, gain_ref,
    key_out, value_out, grad_x_ref,
    held, weights, tokens, total_own, corner_out, corner_in, beside_out, beside_in, cross_out, cross_in,
    relay_up, relay_down,
    key_term, value_term, key_send, order, value_total, key_next, value_next, last_send, last_recv,
    *rest,
):
    bufs_a, bufs_b, bufs_c, bufs_d = rest[0:6], rest[6:12], rest[12:18], rest[18:24]
    sems = rest[24:34]
    load_sem, weight_sem, pair_send, pair_recv, relay_send, relay_recv, cross_send, cross_recv = rest[34:]
    depth = gain_ref.shape[1]
    block = tokens_ref.shape[0]
    rows = key_out.shape[0]
    cols = key_out.shape[1]
    half = block // 2
    piece = half // 4
    big, mid = 16 * rows, 4 * rows
    split_big = big // 2
    split_mid = mid // 2 + mid // 2 % 16
    slab = 768 if depth % 768 == 0 else 128
    strip = 384 if depth % 384 == 0 else 128
    place = lax.axis_index("seq")
    member = lax.axis_index("tp")
    core = lax.rem(member, 2)
    upper = member // 2
    x = lax.rem(place, 4)
    z = lax.rem(place // 4, 4)
    y = place // 16
    height = upper * 4 + z

    def device(ys, zs, xs):
        return ((ys * 4 + zs) * 4 + xs, member)

    def along_z(by):
        other = lax.rem(height + by, 8)
        return ((y * 4 + lax.rem(other, 4)) * 4 + x, other // 4 * 2 + core)

    def remote(source, target, send_sem, recv_sem, to):
        return pltpu.make_async_remote_copy(
            src_ref=source,
            dst_ref=target,
            send_sem=send_sem,
            recv_sem=recv_sem,
            device_id=to,
            device_id_type=MESH_IDS,
        )

    def weight_load(step):
        at = pl.ds(pl.multiple_of(step * slab, slab), slab)
        return (
            pltpu.make_async_copy(w_key_ref.at[at], weights.at[at, pl.ds(0, cols)], weight_sem.at[0, step]),
            pltpu.make_async_copy(w_value_ref.at[at], weights.at[at, pl.ds(cols, cols)], weight_sem.at[1, step]),
        )

    for step in range(depth // slab):
        for one in weight_load(step):
            one.start()
    load_held = pltpu.make_async_copy(gathered_ref, held, load_sem.at[0])
    load_held.start()
    load_tokens = pltpu.make_async_copy(tokens_ref, tokens, load_sem.at[1])
    load_tokens.start()

    z_up, z_down = along_z(2), along_z(6)
    partner = (place, upper * 2 + 1 - core)
    x_up, x_down = device(y, z, lax.rem(x + 1, 4)), device(y, z, lax.rem(x + 3, 4))
    y_up, y_down = device(lax.rem(y + 1, 4), z, x), device(lax.rem(y + 3, 4), z, x)
    z_others = [device(y, lax.rem(z + d, 4), x) for d in (1, 2, 3)]
    barrier = pltpu.get_barrier_semaphore()
    for other in [z_up, z_down, partner, x_up, x_down, y_up, y_down] + z_others:
        pl.semaphore_signal(barrier, inc=1, device_id=other, device_id_type=MESH_IDS)

    own = pl.multiple_of(member * block, block)
    beside = pl.multiple_of((upper * 2 + 1 - core) * block, block)
    across = pl.multiple_of(((1 - upper) * 2 + core) * block, block)
    corner = pl.multiple_of(((1 - upper) * 2 + 1 - core) * block, block)

    def part(begin, store, first=False):
        grads = grad_ref[pl.ds(begin, block), :]

        def one_slab(step, carry):
            if first:
                for one in weight_load(step):
                    one.wait()
            at = pl.ds(pl.multiple_of(step * slab, slab), slab)
            store(at, contract_last(grads, weights[at, :]))
            return carry

        lax.fori_loop(0, depth // slab, one_slab, 0)

    def store_corner(at, value):
        corner_out[:, at] = value.astype(jnp.bfloat16)

    part(corner, store_corner, first=True)
    pl.semaphore_wait(barrier, 10)
    send_corner = remote(corner_out, corner_in, pair_send.at[0], pair_recv.at[0], partner)
    send_corner.start()

    def store_total(at, value):
        total_own[:, at] = value

    part(across, store_total)
    send_corner.wait_recv()

    def join(step, carry):
        at = pl.ds(pl.multiple_of(step * 16, 16), 16)
        cross_out[at, :] = (total_own[at, :] + corner_in[at, :].astype(jnp.float32)).astype(jnp.bfloat16)
        return carry

    lax.fori_loop(0, block // 16, join, 0)

    def rows_at(side, step):
        return pl.ds(side * half + step * piece, piece)

    def small(step):
        return pl.ds(step * piece, piece)

    first = [
        [
            remote(cross_out.at[rows_at(0, step)], relay_up.at[small(step)], relay_send.at[0, step], relay_recv.at[0, step], z_up),
            remote(cross_out.at[rows_at(1, step)], relay_down.at[small(step)], relay_send.at[1, step], relay_recv.at[1, step], z_down),
        ]
        for step in range(4)
    ]
    second = [
        [
            remote(relay_up.at[small(step)], cross_in.at[rows_at(0, step)], cross_send.at[0, step], cross_recv.at[0, step], z_up),
            remote(relay_down.at[small(step)], cross_in.at[rows_at(1, step)], cross_send.at[1, step], cross_recv.at[1, step], z_down),
        ]
        for step in range(4)
    ]
    for pair in first:
        for one in pair:
            one.start()

    def relay(step):
        for side in (0, 1):
            first[step][side].wait_recv()
            second[step][side].start()

    load_held.wait()

    def strips(step, carry):
        at = pl.ds(pl.multiple_of(step * strip, strip), strip)
        result = contract_first(held[:, at], grad_ref[...])
        key_term[at, :] = result[:, :cols]
        value_term[at, :] = result[:, cols:].astype(jnp.bfloat16)
        return carry

    lax.fori_loop(0, depth // strip, strips, 0)

    def finish_b1(total):
        for quarter in range(4):
            at = pl.ds(quarter * mid, mid)
            value_total[at, :] = total(at)
        for xs in range(4):
            for zs in range(4):
                order[zs * rows : zs * rows + rows, :] = value_total[
                    zs * mid + xs * rows : zs * mid + xs * rows + rows, :
                ]
            value_next[xs] = order[...].astype(jnp.bfloat16)

    second_b = ring_sum(
        lambda t: value_term.at[pl.ds(pl.multiple_of(t * big, 16), big)],
        big, split_big, y, y_up, y_down, bufs_b, sems[2:4], finish_b1,
    )

    for ys in range(4):
        for xs in range(4):
            for zs in range(4):
                begin = ((ys * 4 + zs) * 4 + xs) * rows
                order[zs * rows : zs * rows + rows, :] = key_term[begin : begin + rows, :]
            key_send[xs, ys * mid : ys * mid + mid, :] = order[...].astype(jnp.bfloat16)

    def finish_a1(total):
        for quarter in range(4):
            at = pl.ds(quarter * mid, mid)
            key_next[quarter] = total(at).astype(jnp.bfloat16)

    second_a = ring_sum(
        lambda t: key_send.at[t],
        big, split_big, x, x_up, x_down, bufs_a, sems[0:2], finish_a1,
    )
    relay(0)

    def store_beside(at, value):
        beside_out[:, at] = value.astype(jnp.bfloat16)

    part(beside, store_beside)
    send_beside = remote(beside_out, beside_in, pair_send.at[1], pair_recv.at[1], partner)
    send_beside.start()
    part(own, store_total)
    relay(1)
    third_b = second_b()
    third_a = second_a()
    relay(2)
    drain_b = third_b()

    def finish_last(at):
        def finish(total):
            order[...] = total(pl.ds(0, mid))
            for zs in range(4):
                last_send[zs, 0:rows, at : at + cols] = order[
                    zs * rows : zs * rows + rows, :
                ].astype(jnp.bfloat16)
                last_send[zs, rows:, at : at + cols] = jnp.zeros(
                    (last_send.shape[1] - rows, cols), jnp.bfloat16
                )

        return finish

    second_d = ring_sum(
        lambda t: value_next.at[t],
        mid, split_mid, x, x_up, x_down, bufs_d, sems[6:8], finish_last(cols),
    )
    relay(3)
    drain_a = third_a()
    second_c = ring_sum(
        lambda t: key_next.at[t],
        mid, split_mid, y, y_up, y_down, bufs_c, sems[4:6], finish_last(0),
    )
    third_d = second_d()
    third_c = second_c()
    drain_d = third_d()
    drain_c = third_c()
    copies = []
    for d in (1, 2, 3):
        one = remote(
            last_send.at[lax.rem(z + d, 4)], last_recv.at[d - 1], sems[8].at[d - 1], sems[9].at[d - 1], z_others[d - 1]
        )
        one.start()
        copies.append(one)

    load_tokens.wait()
    send_beside.wait_recv()
    for step in range(4):
        for side in (0, 1):
            second[step][side].wait_recv()
            at = rows_at(side, step)
            grad = (
                total_own[at, :] + beside_in[at, :].astype(jnp.float32) + cross_in[at, :].astype(jnp.float32)
            )
            grad_x_ref[at, :] = norm_back(grad, tokens[at, :].astype(jnp.float32), gain_ref[...]).astype(
                jnp.bfloat16
            )

    for one in copies:
        one.wait_recv()
    total = last_send[z, 0:rows, :].astype(jnp.float32)
    for d in range(3):
        total = total + last_recv[d, 0:rows, :].astype(jnp.float32)
    key_out[...] = total[:, 0:cols]
    value_out[...] = total[:, cols:]
    for one in copies:
        one.wait_send()
    for drain in (drain_a, drain_b, drain_c, drain_d):
        drain()
    send_corner.wait_send()
    send_beside.wait_send()
    for pair in first + second:
        for one in pair:
            one.wait_send()


def finish(gathered, grad_kv, w_key, w_value, tokens, in_gain):
    shard, depth = gathered.shape
    block = tokens.shape[0]
    cols = w_key.shape[1]
    rows = depth // 64
    big, mid = 16 * rows, 4 * rows
    split_big = big // 2
    split_mid = mid // 2 + mid // 2 % 16
    padded = (rows + 15) // 16 * 16
    slabs = depth // (768 if depth % 768 == 0 else 128)
    bf = jnp.bfloat16
    dma = pltpu.SemaphoreType.DMA
    vmem = pl.BlockSpec(memory_space=pltpu.VMEM)
    outside = pl.BlockSpec(memory_space=pltpu.HBM)

    def bufs(size, split):
        return [
            pltpu.VMEM((split, cols), bf),
            pltpu.VMEM((size - split, cols), bf),
            pltpu.VMEM((split, cols), bf),
            pltpu.VMEM((size - split, cols), bf),
            pltpu.VMEM((size, cols), bf),
            pltpu.VMEM((size, cols), bf),
        ]

    return pl.pallas_call(
        finish_kernel,
        out_shape=[
            jax.ShapeDtypeStruct((rows, cols), jnp.float32),
            jax.ShapeDtypeStruct((rows, cols), jnp.float32),
            jax.ShapeDtypeStruct((block, depth), bf),
        ],
        in_specs=[outside, vmem, outside, outside, outside, vmem],
        out_specs=[vmem] * 3,
        scratch_shapes=[
            pltpu.VMEM((shard, depth), bf),
            pltpu.VMEM((depth, 2 * cols), bf),
            pltpu.VMEM((block, depth), bf),
            pltpu.VMEM((block, depth), jnp.float32),
        ]
        + [pltpu.VMEM((block, depth), bf)] * 6
        + [pltpu.VMEM((block // 2, depth), bf)] * 2
        + [
            pltpu.VMEM((depth, cols), jnp.float32),
            pltpu.VMEM((depth, cols), bf),
            pltpu.VMEM((4, big, cols), bf),
            pltpu.VMEM((mid, cols), jnp.float32),
            pltpu.VMEM((big, cols), jnp.float32),
            pltpu.VMEM((4, mid, cols), bf),
            pltpu.VMEM((4, mid, cols), bf),
            pltpu.VMEM((4, padded, 2 * cols), bf),
            pltpu.VMEM((3, padded, 2 * cols), bf),
        ]
        + bufs(big, split_big)
        + bufs(big, split_big)
        + bufs(mid, split_mid)
        + bufs(mid, split_mid)
        + [dma((6,))] * 8
        + [dma((3,))] * 2
        + [dma((2,)), dma((2, slabs)), dma((2,)), dma((2,))]
        + [dma((2, 4))] * 4,
        compiler_params=pltpu.CompilerParams(
            collective_id=1, has_side_effects=True, vmem_limit_bytes=51 * 1024 * 1024
        ),
        cost_estimate=pl.CostEstimate(
            flops=6_000_000_000, bytes_accessed=150_000_000, transcendentals=0
        ),
        name="finish",
    )(gathered, grad_kv, w_key, w_value, tokens, in_gain[None, :])


def shards(tokens, in_gain, raw_queries, w_key, w_value, q_gain, k_gain, doc_lengths, out_grad):
    head_size = q_gain.shape[0]
    shard_rows = tokens.shape[0] * lax.axis_size("tp")
    reach = 2 * shard_rows
    first_row = lax.axis_index("seq") * shard_rows
    positions = first_row + jnp.arange(shard_rows, dtype=jnp.int32)
    begins = doc_begin(doc_lengths, positions)
    lowest = jnp.maximum(begins, positions - (WINDOW - 1))
    low = (lowest - (first_row - reach)).reshape(2, 1, shard_rows // 2)
    cosine, sine = angle_tables(positions - begins, head_size)
    gathered, query_rot, raw_keys, window = gather_and_project(
        tokens, in_gain, raw_queries, w_key, w_value, q_gain, k_gain, cosine, sine
    )
    grad_queries, grad_kv = attend_back(
        query_rot, window, out_grad, low, raw_queries, raw_keys, cosine, sine, q_gain, k_gain
    )
    grad_wk, grad_wv, grad_x = finish(gathered, grad_kv, w_key, w_value, tokens, in_gain)
    return (grad_x, grad_queries, grad_wk, grad_wv)


def solution(mesh):
    placed = (
        P(("seq", "tp"), None),
        P(),
        P("seq", "tp"),
        P(None, "tp"),
        P(None, "tp"),
        P(),
        P(),
        P(),
        P("seq", "tp"),
    )
    return jax.shard_map(
        shards,
        mesh=mesh,
        in_specs=placed,
        out_specs=(P(("seq", "tp"), None), P("seq", "tp"), P("seq", "tp"), P("seq", "tp")),
        check_vma=False,
    )
```

```python
import functools

import jax
import jax.numpy as jnp
from jax import lax
from jax.experimental import pallas as pl
from jax.experimental.pallas import tpu as pltpu
from jax.sharding import PartitionSpec as P

WINDOW = 1024
WIDE = 4


EPSILON = 1e-06
QUERY_SCALE = 168.0 ** (-0.5)
ROPE_BASE = 10000.0


def doc_begin(doc_lengths, positions):
    endings = jnp.cumsum(doc_lengths, dtype=jnp.int32)
    starts = endings - doc_lengths
    inside = starts[None, :] <= positions[:, None]
    return jnp.max(jnp.where(inside, starts[None, :], jnp.zeros_like(starts)[None, :]), axis=1)


def angle_tables(positions, head_size):
    half_size = head_size // 2
    lane = jnp.arange(head_size, dtype=jnp.int32)
    powers = (lane % half_size).astype(jnp.float32) * (2.0 / head_size)
    frequency = ROPE_BASE ** (-powers)
    angles = positions.astype(jnp.float32)[:, None] * frequency[None, :]
    sign = jnp.where(lane < half_size, -1.0, 1.0)
    return jnp.cos(angles), jnp.sin(angles) * sign[None, :]


def one_row(blocks_ref, row_ref):
    for index in range(blocks_ref.shape[0]):
        row_ref[:, index * 128 : (index + 1) * 128] = blocks_ref[index : index + 1, :]


def contract_last(left, right):
    return lax.dot_general(
        left, right, (((1,), (1,)), ((), ())), preferred_element_type=jnp.float32
    )


def contract_first(left, right):
    return lax.dot_general(
        left, right, (((0,), (0,)), ((), ())), preferred_element_type=jnp.float32
    )


MESH_IDS = pl.DeviceIdType.MESH


def ring_sum(piece, size, split, pos, up, down, bufs, sems, finish):
    half_up, half_down, mixed_up, mixed_down, full_up, full_down = bufs
    send_sem, recv_sem = sems
    far = lax.rem(pos + 2, 4)
    after = lax.rem(pos + 1, 4)
    before = lax.rem(pos + 3, 4)
    low = pl.ds(0, split)
    high = pl.ds(split, size - split)

    def copy(index, source, target, device):
        return pltpu.make_async_remote_copy(
            src_ref=source,
            dst_ref=target,
            send_sem=send_sem.at[index],
            recv_sem=recv_sem.at[index],
            device_id=device,
            device_id_type=MESH_IDS,
        )

    first = [
        copy(0, piece(far).at[low], half_up, up),
        copy(1, piece(far).at[high], half_down, down),
        copy(2, piece(after).at[high], full_up.at[high], up),
        copy(3, piece(before).at[low], full_down.at[low], down),
    ]
    for one in first:
        one.start()

    def second():
        first[0].wait_recv()
        mixed_up[...] = (
            piece(after)[low, :].astype(jnp.float32) + half_up[...].astype(jnp.float32)
        ).astype(jnp.bfloat16)
        last_up = copy(4, mixed_up, full_up.at[low], up)
        last_up.start()
        first[1].wait_recv()
        mixed_down[...] = (
            piece(before)[high, :].astype(jnp.float32) + half_down[...].astype(jnp.float32)
        ).astype(jnp.bfloat16)
        last_down = copy(5, mixed_down, full_down.at[high], down)
        last_down.start()

        def third():
            first[2].wait_recv()
            first[3].wait_recv()
            last_up.wait_recv()
            last_down.wait_recv()
            finish(
                lambda rows: piece(pos)[rows, :].astype(jnp.float32)
                + full_up[rows, :].astype(jnp.float32)
                + full_down[rows, :].astype(jnp.float32)
            )

            def drain():
                for one in first + [last_up, last_down]:
                    one.wait_send()

            return drain

        return third

    return second


def turn(values, cosine, sine):
    return values * cosine + pltpu.roll(values, values.shape[-1] // 2, 1) * sine


def gather_kernel(
    tokens_hbm, gain_blocks, raw_hbm, q_gain_ref, k_gain_ref, cos_ref, sin_ref, w_key_ref, w_value_ref,
    gathered_ref, query_ref, raw_key_ref, window_ref,
    held, relay_up, relay_down, weights, window, tokens_ref, raw_ref, passing, gain_ref,
    weight_sem, out_sem, window_sem, relay_send, relay_recv, cross_send, cross_recv,
    pair_send, pair_recv, chunk_send, chunk_recv, halo_send, halo_recv, middle_send, middle_recv,
):
    rows = tokens_ref.shape[0]
    half = rows // 2
    piece = half // 4
    cols = w_key_ref.shape[1]
    head_size = k_gain_ref.shape[1]
    place = lax.axis_index("seq")
    member = lax.axis_index("tp")
    count = lax.axis_size("seq")
    core = lax.rem(member, 2)
    upper = member // 2
    x = lax.rem(place, WIDE)
    z = upper * 4 + lax.rem(place // WIDE, 4)
    y = place // (4 * WIDE)

    def along_z(by):
        other = lax.rem(z + by, 8)
        return ((y * 4 + lax.rem(other, 4)) * WIDE + x, other // 4 * 2 + core)

    z_up, z_down = along_z(2), along_z(6)
    partner = (place, upper * 2 + 1 - core)
    later = (lax.rem(place + 1, count), member)
    earlier = (lax.rem(place + count - 1, count), member)

    def in_row(of, xs):
        return (of // WIDE * WIDE + xs, member)

    left, right = lax.rem(x + WIDE - 1, WIDE), lax.rem(x + 1, WIDE)
    row_left, row_right = in_row(place, left), in_row(place, right)
    second_to = (lax.rem(place // WIDE * WIDE + right + 2, count), member)
    second_from = in_row(lax.rem(place + count - 2, count), lax.rem(x + 2 * WIDE - 3, WIDE))

    def remote(source, target, send_sem, recv_sem, device):
        return pltpu.make_async_remote_copy(
            src_ref=source,
            dst_ref=target,
            send_sem=send_sem,
            recv_sem=recv_sem,
            device_id=device,
            device_id_type=MESH_IDS,
        )

    load_tokens = pltpu.make_async_copy(tokens_hbm, tokens_ref, weight_sem.at[2])
    load_tokens.start()
    load_raw = pltpu.make_async_copy(raw_hbm, raw_ref, weight_sem.at[3])
    load_raw.start()
    loads = [
        pltpu.make_async_copy(w_key_ref, weights.at[:, pl.ds(0, cols)], weight_sem.at[0]),
        pltpu.make_async_copy(w_value_ref, weights.at[:, pl.ds(cols, cols)], weight_sem.at[1]),
    ]
    for one in loads:
        one.start()
    barrier = pltpu.get_barrier_semaphore()
    for other in [z_up, z_down, partner, later, earlier, second_to, second_from, row_left, row_right]:
        pl.semaphore_signal(barrier, inc=1, device_id=other, device_id_type=MESH_IDS)

    own = pl.multiple_of(member * rows, rows)
    beside = pl.multiple_of((upper * 2 + 1 - core) * rows, rows)
    across = pl.multiple_of(((1 - upper) * 2 + core) * rows, rows)
    corner = pl.multiple_of(((1 - upper) * 2 + 1 - core) * rows, rows)

    def norm_rows(step, carry):
        at = pl.ds(pl.multiple_of(step * 16, 16), 16)
        values = tokens_ref[at, :].astype(jnp.float32)
        scale = lax.rsqrt(jnp.mean(values * values, axis=1, keepdims=True) + EPSILON)
        held[pl.ds(pl.multiple_of(own + step * 16, 16), 16), :] = (
            values * scale * gain_ref[...]
        ).astype(jnp.bfloat16)
        return carry

    one_row(gain_blocks, gain_ref)
    load_tokens.wait()
    lax.fori_loop(0, rows // 16, norm_rows, 0)
    pl.semaphore_wait(barrier, 9)

    to_partner = remote(
        held.at[pl.ds(own, rows)], held.at[pl.ds(own, rows)], pair_send.at[0], pair_recv.at[0], partner
    )
    to_partner.start()

    def first_up(step):
        return remote(
            held.at[pl.ds(pl.multiple_of(own + step * piece, piece), piece)],
            relay_up.at[pl.ds(pl.multiple_of(step * piece, piece), piece)],
            relay_send.at[0, step], relay_recv.at[0, step], z_up,
        )

    def first_down(step):
        return remote(
            held.at[pl.ds(pl.multiple_of(own + half + step * piece, piece), piece)],
            relay_down.at[pl.ds(pl.multiple_of(step * piece, piece), piece)],
            relay_send.at[1, step], relay_recv.at[1, step], z_down,
        )

    def second_up(step):
        target = pl.multiple_of(((1 - lax.rem(z + 2, 8) // 4) * 2 + core) * rows + step * piece, piece)
        return remote(
            relay_up.at[pl.ds(pl.multiple_of(step * piece, piece), piece)],
            held.at[pl.ds(target, piece)],
            cross_send.at[0, step], cross_recv.at[0, step], z_up,
        )

    def second_down(step):
        target = pl.multiple_of(
            ((1 - lax.rem(z + 6, 8) // 4) * 2 + core) * rows + half + step * piece, piece
        )
        return remote(
            relay_down.at[pl.ds(pl.multiple_of(step * piece, piece), piece)],
            held.at[pl.ds(target, piece)],
            cross_send.at[1, step], cross_recv.at[1, step], z_down,
        )

    def pass_on(side, step):
        at = pl.ds(pl.multiple_of(across + side * half + step * piece, piece), piece)
        return remote(held.at[at], held.at[at], chunk_send.at[side, step], chunk_recv.at[side, step], partner)

    for step in range(2):
        first_up(step).start()
        first_down(step).start()

    def halo(by, index, begin, size):
        at = pl.ds(begin, size)
        return remote(
            window.at[2, at] if by == 1 else passing.at[at],
            window.at[2 - by, at],
            halo_send.at[by - 1, index], halo_recv.at[by - 1, index], later if by == 1 else second_to,
        )

    def middle(index, begin, size):
        at = pl.ds(begin, size)
        return remote(
            window.at[2, at], passing.at[at], middle_send.at[index], middle_recv.at[index], row_left
        )

    def hand_on(index, begin, size):
        middle(index, begin, size).wait_recv()
        halo(2, index, begin, size).start()

    def project(parts):
        block = [held[pl.ds(begin, size), :] for begin, size in parts]
        block = block[0] if len(block) == 1 else jnp.concatenate(block, axis=0)
        result = jnp.dot(block, weights[...], preferred_element_type=jnp.float32)
        at = 0
        for begin, size in parts:
            mine = result[at : at + size]
            at += size
            where = pl.ds(begin, size)
            raw_key_ref[where, :] = mine[:, :cols]
            window[2, where, cols:] = mine[:, cols:].astype(jnp.bfloat16)
            for head in range(cols // head_size):
                lanes = slice(head * head_size, (head + 1) * head_size)
                values = mine[:, lanes]
                scale = lax.rsqrt(jnp.mean(values * values, axis=1, keepdims=True) + EPSILON)
                values = values * scale * k_gain_ref[...]
                window[2, where, lanes] = turn(values, cos_ref[where, :], sin_ref[where, :]).astype(
                    jnp.bfloat16
                )

    out_own = pltpu.make_async_copy(
        held.at[pl.ds(own, rows)], gathered_ref.at[pl.ds(own, rows)], out_sem.at[0]
    )
    out_own.start()
    for one in loads:
        one.wait()
    project([(own, rows)])
    halo(1, 0, own, rows).start()
    middle(0, own, rows).start()
    to_partner.wait_recv()
    out_beside = pltpu.make_async_copy(
        held.at[pl.ds(beside, rows)], gathered_ref.at[pl.ds(beside, rows)], out_sem.at[1]
    )
    out_beside.start()
    project([(beside, rows)])
    halo(1, 1, beside, rows).start()
    middle(1, beside, rows).start()
    for step in range(2, 4):
        first_up(step).start()
        first_down(step).start()

    load_raw.wait()
    for head in range(raw_ref.shape[1] // head_size):
        lanes = slice(head * head_size, (head + 1) * head_size)
        values = raw_ref[:, lanes].astype(jnp.float32)
        scale = lax.rsqrt(jnp.mean(values * values, axis=1, keepdims=True) + EPSILON)
        values = values * scale * q_gain_ref[...]
        query_ref[:, lanes] = (turn(values, cos_ref[...], sin_ref[...]) * QUERY_SCALE).astype(
            jnp.bfloat16
        )

    for step in range(4):
        first_up(step).wait_recv()
        second_up(step).start()
        first_down(step).wait_recv()
        second_down(step).start()
        if step == 0:
            hand_on(0, own, rows)
            hand_on(1, beside, rows)

    def groups(step):
        return [
            (pl.multiple_of(base + side * half + step * piece, piece), piece)
            for base in (across, corner)
            for side in (0, 1)
        ]

    def arrive(step, carry):
        for side, copy in ((0, second_up(step)), (1, second_down(step))):
            copy.wait_recv()
            pass_on(side, step).start()

        @pl.when(step > 0)
        def before():
            for index, (begin, size) in enumerate(groups(step - 1)):
                hand_on(2 + (step - 1) * 4 + index, begin, size)

        for side in (0, 1):
            pass_on(side, step).wait_recv()
        project(groups(step))
        for index, (begin, size) in enumerate(groups(step)):
            halo(1, 2 + step * 4 + index, begin, size).start()
            middle(2 + step * 4 + index, begin, size).start()
        return carry

    lax.fori_loop(0, 4, arrive, 0)
    for index, (begin, size) in enumerate(groups(3)):
        hand_on(14 + index, begin, size)
    out_across = pltpu.make_async_copy(
        held.at[pl.ds(across, rows)], gathered_ref.at[pl.ds(across, rows)], out_sem.at[2]
    )
    out_corner = pltpu.make_async_copy(
        held.at[pl.ds(corner, rows)], gathered_ref.at[pl.ds(corner, rows)], out_sem.at[3]
    )
    out_across.start()
    out_corner.start()

    def each_halo(kinds, act):
        for kind in kinds:
            act(kind(0, own, rows))
            act(kind(1, beside, rows))

            def inner(step, carry):
                for index, (begin, size) in enumerate(groups(step)):
                    act(kind(2 + step * 4 + index, begin, size))
                return carry

            lax.fori_loop(0, 4, inner, 0)

    halos = [functools.partial(halo, 1), functools.partial(halo, 2)]
    each_halo(halos, lambda copy: copy.wait_recv())
    out_window = pltpu.make_async_copy(window, window_ref, window_sem.at[0])
    out_window.start()
    each_halo(halos + [middle], lambda copy: copy.wait_send())
    to_partner.wait_send()
    for step in range(4):
        first_up(step).wait_send()
        first_down(step).wait_send()
        second_up(step).wait_send()
        second_down(step).wait_send()
        pass_on(0, step).wait_send()
        pass_on(1, step).wait_send()
    for one in (out_own, out_beside, out_across, out_corner, out_window):
        one.wait()


def gather_and_project(tokens, in_gain, raw_queries, w_key, w_value, q_gain, k_gain, cosine, sine):
    rows, depth = tokens.shape
    shard = rows * 4
    cols = w_key.shape[1]
    bf = jnp.bfloat16
    vmem = pl.BlockSpec(memory_space=pltpu.VMEM)
    anywhere = pl.BlockSpec(memory_space=pl.ANY)
    outside = pl.BlockSpec(memory_space=pltpu.HBM)
    dma = pltpu.SemaphoreType.DMA
    return pl.pallas_call(
        gather_kernel,
        out_shape=[
            jax.ShapeDtypeStruct((shard, depth), bf),
            jax.ShapeDtypeStruct(raw_queries.shape, bf),
            jax.ShapeDtypeStruct((shard, cols), jnp.float32),
            jax.ShapeDtypeStruct((3, shard, 2 * cols), bf),
        ],
        in_specs=[outside, vmem, outside] + [vmem] * 4 + [outside] * 2,
        out_specs=[anywhere, vmem, vmem, anywhere],
        scratch_shapes=[
            pltpu.VMEM((shard, depth), bf),
            pltpu.VMEM((rows // 2, depth), bf),
            pltpu.VMEM((rows // 2, depth), bf),
            pltpu.VMEM((depth, 2 * cols), bf),
            pltpu.VMEM((3, shard, 2 * cols), bf),
            pltpu.VMEM((rows, depth), bf),
            pltpu.VMEM(raw_queries.shape, bf),
            pltpu.VMEM((shard, 2 * cols), bf),
            pltpu.VMEM((1, depth), jnp.float32),
            dma((4,)),
            dma((4,)),
            dma((1,)),
            dma((2, 4)),
            dma((2, 4)),
            dma((2, 4)),
            dma((2, 4)),
            dma((1,)),
            dma((1,)),
            dma((2, 4)),
            dma((2, 4)),
            dma((2, 18)),
            dma((2, 18)),
            dma((18,)),
            dma((18,)),
        ],
        compiler_params=pltpu.CompilerParams(
            collective_id=2, has_side_effects=True, vmem_limit_bytes=60 * 1024 * 1024
        ),
        cost_estimate=pl.CostEstimate(
            flops=3_000_000_000, bytes_accessed=150_000_000, transcendentals=0
        ),
        name="gather_and_project",
    )(tokens, in_gain.reshape(depth // 128, 128), raw_queries, q_gain[None, :], k_gain[None, :], cosine, sine, w_key, w_value)


def unturn(values, cosine, sine):
    return values * cosine - pltpu.roll(values, values.shape[-1] // 2, 1) * sine


def norm_back(grad, values, gain):
    scale = lax.rsqrt(jnp.mean(values * values, axis=1, keepdims=True) + EPSILON)
    unit = values * scale
    inner = grad * gain
    return scale * (inner - unit * jnp.mean(inner * unit, axis=1, keepdims=True))


def attend_kernel(
    query_ref, window_ref, out_grad_hbm, low_ref, raw_hbm, raw_key_ref, cos_ref, sin_ref, q_gain_ref, k_gain_ref,
    grad_query_ref, grad_kv_ref,
    exps, along, totals, query_total, parts, returned, out_grad_ref, raw_ref, passing,
    send_sem, recv_sem, middle_send, middle_recv, load_sem, chain_send, chain_recv, sum_send, sum_recv,
):
    shard = query_ref.shape[0]
    head_size = q_gain_ref.shape[1]
    kv_heads = raw_key_ref.shape[1] // head_size
    group_size = query_ref.shape[1] // raw_key_ref.shape[1]
    tile = shard // 2
    reach = 2 * shard
    place = lax.axis_index("seq")
    member = lax.axis_index("tp")
    count = lax.axis_size("seq")
    x = lax.rem(place, WIDE)

    def in_row(of, xs):
        return (of // WIDE * WIDE + xs, member)

    left, right = lax.rem(x + WIDE - 1, WIDE), lax.rem(x + 1, WIDE)
    later = (lax.rem(place + 1, count), member)
    earlier = (lax.rem(place + count - 1, count), member)
    middle_to = in_row(lax.rem(place + count - 2, count), right)
    middle_from = (lax.rem(place // WIDE * WIDE + right + 2, count), member)
    row_left, row_right = in_row(place, left), in_row(place, right)
    load_grads = pltpu.make_async_copy(out_grad_hbm, out_grad_ref, load_sem.at[0])
    load_grads.start()
    load_raw = pltpu.make_async_copy(raw_hbm, raw_ref, load_sem.at[1])
    load_raw.start()
    barrier = pltpu.get_barrier_semaphore()
    for other in [later, earlier, middle_to, middle_from, row_left, row_right]:
        pl.semaphore_signal(barrier, inc=1, device_id=other, device_id_type=MESH_IDS)

    totals[...] = jnp.zeros_like(totals)

    def across(left, right):
        return lax.dot_general(left, right, (((1,), (1,)), ((), ())), preferred_element_type=jnp.float32)

    def back(window, head):
        return pltpu.make_async_remote_copy(
            src_ref=parts.at[window, head] if window == 1 else passing.at[head],
            dst_ref=returned.at[window, head],
            send_sem=send_sem.at[window, head],
            recv_sem=recv_sem.at[window, head],
            device_id=earlier if window == 1 else row_right,
            device_id_type=MESH_IDS,
        )

    def middle(head):
        return pltpu.make_async_remote_copy(
            src_ref=parts.at[0, head],
            dst_ref=passing.at[head],
            send_sem=middle_send.at[head],
            recv_sem=middle_recv.at[head],
            device_id=middle_to,
            device_id_type=MESH_IDS,
        )

    last = kv_heads - 1

    def chain(piece):
        at = pl.ds(piece * tile, tile)
        return pltpu.make_async_remote_copy(
            src_ref=parts.at[0, last, at],
            dst_ref=passing.at[last, at],
            send_sem=chain_send.at[piece],
            recv_sem=chain_recv.at[piece],
            device_id=earlier,
            device_id_type=MESH_IDS,
        )

    def summed(piece):
        at = pl.ds(piece * tile, tile)
        return pltpu.make_async_remote_copy(
            src_ref=parts.at[1, last, at],
            dst_ref=returned.at[1, last, at],
            send_sem=sum_send.at[piece],
            recv_sem=sum_recv.at[piece],
            device_id=earlier,
            device_id_type=MESH_IDS,
        )

    load_grads.wait()
    load_raw.wait()
    for head in range(kv_heads):
        key_lanes = slice(head * head_size, (head + 1) * head_size)
        value_lanes = slice((kv_heads + head) * head_size, (kv_heads + head + 1) * head_size)
        lanes = [
            slice((head * group_size + member_of) * head_size, (head * group_size + member_of + 1) * head_size)
            for member_of in range(group_size)
        ]

        def half(step, carry):
            begin = pl.multiple_of(step * tile, tile)
            rows = pl.ds(begin, tile)
            queries = jnp.concatenate([query_ref[rows, at] for at in lanes], axis=0)
            grads = jnp.concatenate([out_grad_ref[rows, at] for at in lanes], axis=0)
            low = low_ref[step]
            low = jnp.concatenate([low] * group_size, axis=1)
            width = group_size * tile
            high = lax.broadcasted_iota(jnp.int32, (1, tile), 1) + (reach + begin)
            high = jnp.concatenate([high] * group_size, axis=1)

            def scores(index, stats):
                total, delta = stats
                first = pl.multiple_of(begin + index * tile, tile)
                key_rows = pl.ds(first, tile)
                score = across(window_ref[key_rows, key_lanes], queries)
                partial = across(window_ref[key_rows, value_lanes], grads)
                key = lax.broadcasted_iota(jnp.int32, (tile, width), 0) + first
                value = jnp.where((key >= low) & (key <= high), jnp.exp(score), 0.0)
                at = pl.ds(pl.multiple_of(index * tile, tile), tile)
                exps[at, :] = value
                along[at, :] = partial
                total = total + jnp.sum(value, axis=0, keepdims=True)
                delta = delta + jnp.sum(value * partial, axis=0, keepdims=True)
                return total, delta

            nothing = jnp.zeros((1, width), jnp.float32)
            total, delta = lax.fori_loop(0, reach // tile + 1, scores, (nothing, nothing))
            inverse = 1.0 / total
            delta = delta * inverse
            query_total[...] = jnp.zeros_like(query_total)

            def slopes(index, carry):
                key_rows = pl.ds(pl.multiple_of(begin + index * tile, tile), tile)
                at = pl.ds(pl.multiple_of(index * tile, tile), tile)
                probs = exps[at, :] * inverse
                slope = (probs * (along[at, :] - delta)).astype(jnp.bfloat16)
                query_total[...] += contract_first(window_ref[key_rows, key_lanes], slope)
                totals[key_rows, key_lanes] += jnp.dot(slope, queries, preferred_element_type=jnp.float32)
                totals[key_rows, value_lanes] += jnp.dot(
                    probs.astype(jnp.bfloat16), grads, preferred_element_type=jnp.float32
                )
                return carry

            lax.fori_loop(0, reach // tile + 1, slopes, 0)
            flipped = query_total[...].T
            for member_of, at in enumerate(lanes):
                grad = flipped[member_of * tile : (member_of + 1) * tile] * QUERY_SCALE
                grad = unturn(grad, cos_ref[rows, :], sin_ref[rows, :])
                values = raw_ref[rows, at].astype(jnp.float32)
                grad_query_ref[rows, at] = norm_back(grad, values, q_gain_ref[...]).astype(jnp.bfloat16)
            return carry

        lax.fori_loop(0, 2, half, 0)
        for window in range(2 if head < last else 1):
            rows = slice(window * shard, (window + 1) * shard)
            parts[window, head, :, :head_size] = totals[rows, key_lanes].astype(jnp.bfloat16)
            parts[window, head, :, head_size:] = totals[rows, value_lanes].astype(jnp.bfloat16)
        if head == 0:
            pl.semaphore_wait(barrier, 6)
        if head < last:
            middle(head).start()
            back(1, head).start()
        else:
            chain(0).start()
            chain(1).start()

    for head in range(last):
        middle(head).wait_recv()
        back(0, head).start()
    for piece in range(2):
        chain(piece).wait_recv()
        here = slice(piece * tile, (piece + 1) * tile)
        rows = slice(shard + piece * tile, shard + (piece + 1) * tile)
        lanes = slice(last * head_size, (last + 1) * head_size)
        parts[1, last, here, :head_size] = (
            totals[rows, lanes] + passing[last, here, :head_size].astype(jnp.float32)
        ).astype(jnp.bfloat16)
        lanes = slice((kv_heads + last) * head_size, (kv_heads + last + 1) * head_size)
        parts[1, last, here, head_size:] = (
            totals[rows, lanes] + passing[last, here, head_size:].astype(jnp.float32)
        ).astype(jnp.bfloat16)
        summed(piece).start()
    own = slice(reach, reach + shard)
    for head in range(kv_heads):
        key_lanes = slice(head * head_size, (head + 1) * head_size)
        value_lanes = slice((kv_heads + head) * head_size, (kv_heads + head + 1) * head_size)
        if head < last:
            for window in range(2):
                back(window, head).wait_recv()
        else:
            summed(0).wait_recv()
            summed(1).wait_recv()
        key_grad = totals[own, key_lanes]
        value_grad = totals[own, value_lanes]
        for window in (1, 0) if head < last else (1,):
            key_grad = key_grad + returned[window, head, :, :head_size].astype(jnp.float32)
            value_grad = value_grad + returned[window, head, :, head_size:].astype(jnp.float32)
        grad_kv_ref[:, value_lanes] = value_grad.astype(jnp.bfloat16)
        key_grad = unturn(key_grad, cos_ref[...], sin_ref[...])
        grad_kv_ref[:, key_lanes] = norm_back(key_grad, raw_key_ref[:, key_lanes], k_gain_ref[...]).astype(
            jnp.bfloat16
        )
    for head in range(last):
        middle(head).wait_send()
        for window in range(2):
            back(window, head).wait_send()
    for piece in range(2):
        chain(piece).wait_send()
        summed(piece).wait_send()


def attend_back(query_rot, window, out_grad, low, raw_queries, raw_keys, cosine, sine, q_gain, k_gain):
    shard = query_rot.shape[0]
    head_size = q_gain.shape[0]
    kv_heads = raw_keys.shape[1] // head_size
    group_size = query_rot.shape[1] // raw_keys.shape[1]
    tile = shard // 2
    width = group_size * tile
    vmem = pl.BlockSpec(memory_space=pltpu.VMEM)
    outside = pl.BlockSpec(memory_space=pltpu.HBM)
    return pl.pallas_call(
        attend_kernel,
        out_shape=[
            jax.ShapeDtypeStruct(query_rot.shape, jnp.bfloat16),
            jax.ShapeDtypeStruct((shard, 2 * raw_keys.shape[1]), jnp.bfloat16),
        ],
        in_specs=[vmem, vmem, outside, vmem, outside] + [vmem] * 5,
        out_specs=[vmem] * 2,
        scratch_shapes=[
            pltpu.VMEM((2 * shard + tile, width), jnp.float32),
            pltpu.VMEM((2 * shard + tile, width), jnp.float32),
            pltpu.VMEM((3 * shard, 2 * raw_keys.shape[1]), jnp.float32),
            pltpu.VMEM((head_size, width), jnp.float32),
            pltpu.VMEM((2, kv_heads, shard, 2 * head_size), jnp.bfloat16),
            pltpu.VMEM((2, kv_heads, shard, 2 * head_size), jnp.bfloat16),
            pltpu.VMEM(query_rot.shape, jnp.bfloat16),
            pltpu.VMEM(query_rot.shape, jnp.bfloat16),
            pltpu.VMEM((kv_heads, shard, 2 * head_size), jnp.bfloat16),
            pltpu.SemaphoreType.DMA((2, kv_heads)),
            pltpu.SemaphoreType.DMA((2, kv_heads)),
            pltpu.SemaphoreType.DMA((kv_heads,)),
            pltpu.SemaphoreType.DMA((kv_heads,)),
            pltpu.SemaphoreType.DMA((2,)),
            pltpu.SemaphoreType.DMA((2,)),
            pltpu.SemaphoreType.DMA((2,)),
            pltpu.SemaphoreType.DMA((2,)),
            pltpu.SemaphoreType.DMA((2,)),
        ],
        compiler_params=pltpu.CompilerParams(
            collective_id=3, has_side_effects=True, vmem_limit_bytes=60 * 1024 * 1024
        ),
        cost_estimate=pl.CostEstimate(
            flops=8_000_000_000, bytes_accessed=100_000_000, transcendentals=3_000_000
        ),
        name="attend_back",
    )(
        query_rot, window.reshape(3 * shard, window.shape[2]), out_grad, low, raw_queries, raw_keys,
        cosine, sine, q_gain[None, :], k_gain[None, :],
    )


def finish_kernel(
    gathered_ref, grad_ref, w_key_ref, w_value_ref, tokens_ref, gain_blocks,
    key_out, value_out, grad_x_ref,
    held, weights, tokens, gain_ref, total_own, corner_out, corner_in, beside_out, beside_in, cross_out, cross_in,
    relay_up, relay_down,
    key_term, value_term, key_send, order, value_total, key_next, value_next, last_send, last_recv,
    *rest,
):
    bufs_a, bufs_b, bufs_c, bufs_d = rest[0:6], rest[6:12], rest[12:18], rest[18:24]
    sems = rest[24:34]
    load_sem, weight_sem, pair_send, pair_recv, relay_send, relay_recv, cross_send, cross_recv = rest[34:42]
    corner_send, corner_recv = rest[42:]
    depth = gain_ref.shape[1]
    block = tokens_ref.shape[0]
    rows = key_out.shape[0]
    cols = key_out.shape[1]
    half = block // 2
    piece = half // 4
    big, mid = 16 * rows, 4 * rows
    split_big = big // 2
    split_mid = mid // 2 + mid // 2 % 16
    slab = 768 if depth % 768 == 0 else 128
    strip = 384 if depth % 384 == 0 else 128
    place = lax.axis_index("seq")
    member = lax.axis_index("tp")
    core = lax.rem(member, 2)
    upper = member // 2
    x = lax.rem(place, 4)
    z = lax.rem(place // 4, 4)
    y = place // 16
    height = upper * 4 + z

    def device(ys, zs, xs):
        return ((ys * 4 + zs) * 4 + xs, member)

    def along_z(by):
        other = lax.rem(height + by, 8)
        return ((y * 4 + lax.rem(other, 4)) * 4 + x, other // 4 * 2 + core)

    def remote(source, target, send_sem, recv_sem, to):
        return pltpu.make_async_remote_copy(
            src_ref=source,
            dst_ref=target,
            send_sem=send_sem,
            recv_sem=recv_sem,
            device_id=to,
            device_id_type=MESH_IDS,
        )

    def weight_load(step):
        at = pl.ds(pl.multiple_of(step * slab, slab), slab)
        return (
            pltpu.make_async_copy(w_key_ref.at[at], weights.at[at, pl.ds(0, cols)], weight_sem.at[0, step]),
            pltpu.make_async_copy(w_value_ref.at[at], weights.at[at, pl.ds(cols, cols)], weight_sem.at[1, step]),
        )

    for step in range(depth // slab):
        for one in weight_load(step):
            one.start()
    load_held = pltpu.make_async_copy(gathered_ref, held, load_sem.at[0])
    load_held.start()
    load_tokens = pltpu.make_async_copy(tokens_ref, tokens, load_sem.at[1])
    load_tokens.start()

    z_up, z_down = along_z(2), along_z(6)
    partner = (place, upper * 2 + 1 - core)
    x_up, x_down = device(y, z, lax.rem(x + 1, 4)), device(y, z, lax.rem(x + 3, 4))
    y_up, y_down = device(lax.rem(y + 1, 4), z, x), device(lax.rem(y + 3, 4), z, x)
    z_others = [device(y, lax.rem(z + d, 4), x) for d in (1, 2, 3)]
    barrier = pltpu.get_barrier_semaphore()
    for other in [z_up, z_down, partner, x_up, x_down, y_up, y_down] + z_others:
        pl.semaphore_signal(barrier, inc=1, device_id=other, device_id_type=MESH_IDS)

    own = pl.multiple_of(member * block, block)
    beside = pl.multiple_of((upper * 2 + 1 - core) * block, block)
    across = pl.multiple_of(((1 - upper) * 2 + core) * block, block)
    corner = pl.multiple_of(((1 - upper) * 2 + 1 - core) * block, block)

    def part(begin, store, first=False):
        grads = grad_ref[pl.ds(begin, block), :]

        def one_slab(step, carry):
            if first:
                for one in weight_load(step):
                    one.wait()
            at = pl.ds(pl.multiple_of(step * slab, slab), slab)
            store(at, contract_last(grads, weights[at, :]))
            return carry

        lax.fori_loop(0, depth // slab, one_slab, 0)

    def store_corner(at, value):
        corner_out[:, at] = value.astype(jnp.bfloat16)

    part(corner, store_corner, first=True)
    pl.semaphore_wait(barrier, 10)

    def rows_at(side, step):
        return pl.ds(side * half + step * piece, piece)

    pieces = [(side, step) for step in range(4) for side in (0, 1)]
    send_corner = {
        (side, step): remote(
            corner_out.at[rows_at(side, step)], corner_in.at[rows_at(side, step)],
            corner_send.at[side, step], corner_recv.at[side, step], partner,
        )
        for side, step in pieces
    }
    for one in pieces:
        send_corner[one].start()

    def store_total(at, value):
        total_own[:, at] = value

    part(across, store_total)
    def small(step):
        return pl.ds(step * piece, piece)

    first = [
        [
            remote(cross_out.at[rows_at(0, step)], relay_up.at[small(step)], relay_send.at[0, step], relay_recv.at[0, step], z_up),
            remote(cross_out.at[rows_at(1, step)], relay_down.at[small(step)], relay_send.at[1, step], relay_recv.at[1, step], z_down),
        ]
        for step in range(4)
    ]
    second = [
        [
            remote(relay_up.at[small(step)], cross_in.at[rows_at(0, step)], cross_send.at[0, step], cross_recv.at[0, step], z_up),
            remote(relay_down.at[small(step)], cross_in.at[rows_at(1, step)], cross_send.at[1, step], cross_recv.at[1, step], z_down),
        ]
        for step in range(4)
    ]
    for side, step in pieces:
        send_corner[side, step].wait_recv()
        at = rows_at(side, step)
        cross_out[at, :] = (total_own[at, :] + corner_in[at, :].astype(jnp.float32)).astype(jnp.bfloat16)
        first[step][side].start()

    def relay(step):
        for side in (0, 1):
            first[step][side].wait_recv()
            second[step][side].start()

    load_held.wait()

    def strips(step, carry):
        at = pl.ds(pl.multiple_of(step * strip, strip), strip)
        result = contract_first(held[:, at], grad_ref[...])
        key_term[at, :] = result[:, :cols]
        value_term[at, :] = result[:, cols:].astype(jnp.bfloat16)
        return carry

    lax.fori_loop(0, depth // strip, strips, 0)

    def finish_b1(total):
        for quarter in range(4):
            at = pl.ds(quarter * mid, mid)
            value_total[at, :] = total(at)
        for xs in range(4):
            for zs in range(4):
                order[zs * rows : zs * rows + rows, :] = value_total[
                    zs * mid + xs * rows : zs * mid + xs * rows + rows, :
                ]
            value_next[xs] = order[...].astype(jnp.bfloat16)

    second_b = ring_sum(
        lambda t: value_term.at[pl.ds(pl.multiple_of(t * big, 16), big)],
        big, split_big, y, y_up, y_down, bufs_b, sems[2:4], finish_b1,
    )

    for ys in range(4):
        for xs in range(4):
            for zs in range(4):
                begin = ((ys * 4 + zs) * 4 + xs) * rows
                order[zs * rows : zs * rows + rows, :] = key_term[begin : begin + rows, :]
            key_send[xs, ys * mid : ys * mid + mid, :] = order[...].astype(jnp.bfloat16)

    def finish_a1(total):
        for quarter in range(4):
            at = pl.ds(quarter * mid, mid)
            key_next[quarter] = total(at).astype(jnp.bfloat16)

    second_a = ring_sum(
        lambda t: key_send.at[t],
        big, split_big, x, x_up, x_down, bufs_a, sems[0:2], finish_a1,
    )
    relay(0)

    def store_beside(at, value):
        beside_out[:, at] = value.astype(jnp.bfloat16)

    part(beside, store_beside)
    send_beside = remote(beside_out, beside_in, pair_send.at[1], pair_recv.at[1], partner)
    send_beside.start()
    part(own, store_total)
    relay(1)
    third_b = second_b()
    third_a = second_a()
    relay(2)
    drain_b = third_b()

    def finish_last(at):
        def finish(total):
            order[...] = total(pl.ds(0, mid))
            for zs in range(4):
                last_send[zs, 0:rows, at : at + cols] = order[
                    zs * rows : zs * rows + rows, :
                ].astype(jnp.bfloat16)
                last_send[zs, rows:, at : at + cols] = jnp.zeros(
                    (last_send.shape[1] - rows, cols), jnp.bfloat16
                )

        return finish

    second_d = ring_sum(
        lambda t: value_next.at[t],
        mid, split_mid, x, x_up, x_down, bufs_d, sems[6:8], finish_last(cols),
    )
    relay(3)
    drain_a = third_a()
    second_c = ring_sum(
        lambda t: key_next.at[t],
        mid, split_mid, y, y_up, y_down, bufs_c, sems[4:6], finish_last(0),
    )
    third_d = second_d()
    third_c = second_c()
    drain_d = third_d()
    drain_c = third_c()
    copies = []
    for d in (1, 2, 3):
        one = remote(
            last_send.at[lax.rem(z + d, 4)], last_recv.at[d - 1], sems[8].at[d - 1], sems[9].at[d - 1], z_others[d - 1]
        )
        one.start()
        copies.append(one)

    one_row(gain_blocks, gain_ref)
    load_tokens.wait()
    send_beside.wait_recv()
    for step in range(4):
        for side in (0, 1):
            second[step][side].wait_recv()
            at = rows_at(side, step)
            grad = (
                total_own[at, :] + beside_in[at, :].astype(jnp.float32) + cross_in[at, :].astype(jnp.float32)
            )
            grad_x_ref[at, :] = norm_back(grad, tokens[at, :].astype(jnp.float32), gain_ref[...]).astype(
                jnp.bfloat16
            )

    for one in copies:
        one.wait_recv()
    total = last_send[z, 0:rows, :].astype(jnp.float32)
    for d in range(3):
        total = total + last_recv[d, 0:rows, :].astype(jnp.float32)
    key_out[...] = total[:, 0:cols]
    value_out[...] = total[:, cols:]
    for one in copies:
        one.wait_send()
    for drain in (drain_a, drain_b, drain_c, drain_d):
        drain()
    for one in pieces:
        send_corner[one].wait_send()
    send_beside.wait_send()
    for pair in first + second:
        for one in pair:
            one.wait_send()


def finish(gathered, grad_kv, w_key, w_value, tokens, in_gain):
    shard, depth = gathered.shape
    block = tokens.shape[0]
    cols = w_key.shape[1]
    rows = depth // 64
    big, mid = 16 * rows, 4 * rows
    split_big = big // 2
    split_mid = mid // 2 + mid // 2 % 16
    padded = (rows + 15) // 16 * 16
    slabs = depth // (768 if depth % 768 == 0 else 128)
    bf = jnp.bfloat16
    dma = pltpu.SemaphoreType.DMA
    vmem = pl.BlockSpec(memory_space=pltpu.VMEM)
    outside = pl.BlockSpec(memory_space=pltpu.HBM)

    def bufs(size, split):
        return [
            pltpu.VMEM((split, cols), bf),
            pltpu.VMEM((size - split, cols), bf),
            pltpu.VMEM((split, cols), bf),
            pltpu.VMEM((size - split, cols), bf),
            pltpu.VMEM((size, cols), bf),
            pltpu.VMEM((size, cols), bf),
        ]

    return pl.pallas_call(
        finish_kernel,
        out_shape=[
            jax.ShapeDtypeStruct((rows, cols), jnp.float32),
            jax.ShapeDtypeStruct((rows, cols), jnp.float32),
            jax.ShapeDtypeStruct((block, depth), bf),
        ],
        in_specs=[outside, vmem, outside, outside, outside, vmem],
        out_specs=[vmem] * 3,
        scratch_shapes=[
            pltpu.VMEM((shard, depth), bf),
            pltpu.VMEM((depth, 2 * cols), bf),
            pltpu.VMEM((block, depth), bf),
            pltpu.VMEM((1, depth), jnp.float32),
            pltpu.VMEM((block, depth), jnp.float32),
        ]
        + [pltpu.VMEM((block, depth), bf)] * 6
        + [pltpu.VMEM((block // 2, depth), bf)] * 2
        + [
            pltpu.VMEM((depth, cols), jnp.float32),
            pltpu.VMEM((depth, cols), bf),
            pltpu.VMEM((4, big, cols), bf),
            pltpu.VMEM((mid, cols), jnp.float32),
            pltpu.VMEM((big, cols), jnp.float32),
            pltpu.VMEM((4, mid, cols), bf),
            pltpu.VMEM((4, mid, cols), bf),
            pltpu.VMEM((4, padded, 2 * cols), bf),
            pltpu.VMEM((3, padded, 2 * cols), bf),
        ]
        + bufs(big, split_big)
        + bufs(big, split_big)
        + bufs(mid, split_mid)
        + bufs(mid, split_mid)
        + [dma((6,))] * 8
        + [dma((3,))] * 2
        + [dma((2,)), dma((2, slabs)), dma((2,)), dma((2,))]
        + [dma((2, 4))] * 6,
        compiler_params=pltpu.CompilerParams(
            collective_id=1, has_side_effects=True, vmem_limit_bytes=51 * 1024 * 1024
        ),
        cost_estimate=pl.CostEstimate(
            flops=6_000_000_000, bytes_accessed=150_000_000, transcendentals=0
        ),
        name="finish",
    )(gathered, grad_kv, w_key, w_value, tokens, in_gain.reshape(depth // 128, 128))


def shards(tokens, in_gain, raw_queries, w_key, w_value, q_gain, k_gain, doc_lengths, out_grad):
    head_size = q_gain.shape[0]
    shard_rows = tokens.shape[0] * lax.axis_size("tp")
    reach = 2 * shard_rows
    first_row = lax.axis_index("seq") * shard_rows
    positions = first_row + jnp.arange(shard_rows, dtype=jnp.int32)
    begins = doc_begin(doc_lengths, positions)
    lowest = jnp.maximum(begins, positions - (WINDOW - 1))
    low = (lowest - (first_row - reach)).reshape(2, 1, shard_rows // 2)
    cosine, sine = angle_tables(positions - begins, head_size)
    gathered, query_rot, raw_keys, window = gather_and_project(
        tokens, in_gain, raw_queries, w_key, w_value, q_gain, k_gain, cosine, sine
    )
    grad_queries, grad_kv = attend_back(
        query_rot, window, out_grad, low, raw_queries, raw_keys, cosine, sine, q_gain, k_gain
    )
    grad_wk, grad_wv, grad_x = finish(gathered, grad_kv, w_key, w_value, tokens, in_gain)
    return (grad_x, grad_queries, grad_wk, grad_wv)


def solution(mesh):
    placed = (
        P(("seq", "tp"), None),
        P(),
        P("seq", "tp"),
        P(None, "tp"),
        P(None, "tp"),
        P(),
        P(),
        P(),
        P("seq", "tp"),
    )
    return jax.shard_map(
        shards,
        mesh=mesh,
        in_specs=placed,
        out_specs=(P(("seq", "tp"), None), P("seq", "tp"), P("seq", "tp"), P("seq", "tp")),
        check_vma=False,
    )
```

```python
import functools

import jax
import jax.numpy as jnp
from jax import lax
from jax.experimental import pallas as pl
from jax.experimental.pallas import tpu as pltpu
from jax.sharding import PartitionSpec as P

WINDOW = 1024
WIDE = 4


EPSILON = 1e-06
QUERY_SCALE = 168.0 ** (-0.5)
ROPE_BASE = 10000.0


def doc_begin(doc_lengths, positions):
    endings = jnp.cumsum(doc_lengths, dtype=jnp.int32)
    starts = endings - doc_lengths
    inside = starts[None, :] <= positions[:, None]
    return jnp.max(jnp.where(inside, starts[None, :], jnp.zeros_like(starts)[None, :]), axis=1)


def angle_tables(positions, head_size):
    half_size = head_size // 2
    lane = jnp.arange(head_size, dtype=jnp.int32)
    powers = (lane % half_size).astype(jnp.float32) * (2.0 / head_size)
    frequency = ROPE_BASE ** (-powers)
    angles = positions.astype(jnp.float32)[:, None] * frequency[None, :]
    sign = jnp.where(lane < half_size, -1.0, 1.0)
    return jnp.cos(angles), jnp.sin(angles) * sign[None, :]


def one_row(blocks_ref, row_ref):
    for index in range(blocks_ref.shape[0]):
        row_ref[:, index * 128 : (index + 1) * 128] = blocks_ref[index : index + 1, :]


def contract_last(left, right):
    return lax.dot_general(
        left, right, (((1,), (1,)), ((), ())), preferred_element_type=jnp.float32
    )


def contract_first(left, right):
    return lax.dot_general(
        left, right, (((0,), (0,)), ((), ())), preferred_element_type=jnp.float32
    )


MESH_IDS = pl.DeviceIdType.MESH


def ring_sum(piece, size, split, pos, up, down, bufs, sems, finish):
    half_up, half_down, mixed_up, mixed_down, full_up, full_down = bufs
    send_sem, recv_sem = sems
    far = lax.rem(pos + 2, 4)
    after = lax.rem(pos + 1, 4)
    before = lax.rem(pos + 3, 4)
    low = pl.ds(0, split)
    high = pl.ds(split, size - split)

    def copy(index, source, target, device):
        return pltpu.make_async_remote_copy(
            src_ref=source,
            dst_ref=target,
            send_sem=send_sem.at[index],
            recv_sem=recv_sem.at[index],
            device_id=device,
            device_id_type=MESH_IDS,
        )

    first = [
        copy(0, piece(far).at[low], half_up, up),
        copy(1, piece(far).at[high], half_down, down),
        copy(2, piece(after).at[high], full_up.at[high], up),
        copy(3, piece(before).at[low], full_down.at[low], down),
    ]
    for one in first:
        one.start()

    def second():
        first[0].wait_recv()
        mixed_up[...] = (
            piece(after)[low, :].astype(jnp.float32) + half_up[...].astype(jnp.float32)
        ).astype(jnp.bfloat16)
        last_up = copy(4, mixed_up, full_up.at[low], up)
        last_up.start()
        first[1].wait_recv()
        mixed_down[...] = (
            piece(before)[high, :].astype(jnp.float32) + half_down[...].astype(jnp.float32)
        ).astype(jnp.bfloat16)
        last_down = copy(5, mixed_down, full_down.at[high], down)
        last_down.start()

        def third():
            first[2].wait_recv()
            first[3].wait_recv()
            last_up.wait_recv()
            last_down.wait_recv()
            finish(
                lambda rows: piece(pos)[rows, :].astype(jnp.float32)
                + full_up[rows, :].astype(jnp.float32)
                + full_down[rows, :].astype(jnp.float32)
            )

            def drain():
                for one in first + [last_up, last_down]:
                    one.wait_send()

            return drain

        return third

    return second


def turn(values, cosine, sine):
    return values * cosine + pltpu.roll(values, values.shape[-1] // 2, 1) * sine


def gather_kernel(
    tokens_hbm, gain_blocks, raw_hbm, q_gain_ref, k_gain_ref, cos_ref, sin_ref, w_key_ref, w_value_ref,
    gathered_ref, query_ref, raw_key_ref, window_ref,
    held, relay_up, relay_down, weights, window, tokens_ref, raw_ref, passing, gain_ref,
    weight_sem, out_sem, window_sem, relay_send, relay_recv, cross_send, cross_recv,
    pair_send, pair_recv, chunk_send, chunk_recv, halo_send, halo_recv, middle_send, middle_recv,
):
    rows = tokens_ref.shape[0]
    half = rows // 2
    piece = half // 4
    cols = w_key_ref.shape[1]
    head_size = k_gain_ref.shape[1]
    place = lax.axis_index("seq")
    member = lax.axis_index("tp")
    count = lax.axis_size("seq")
    core = lax.rem(member, 2)
    upper = member // 2
    x = lax.rem(place, WIDE)
    z = upper * 4 + lax.rem(place // WIDE, 4)
    y = place // (4 * WIDE)

    def along_z(by):
        other = lax.rem(z + by, 8)
        return ((y * 4 + lax.rem(other, 4)) * WIDE + x, other // 4 * 2 + core)

    z_up, z_down = along_z(2), along_z(6)
    partner = (place, upper * 2 + 1 - core)
    later = (lax.rem(place + 1, count), member)
    earlier = (lax.rem(place + count - 1, count), member)

    def in_row(of, xs):
        return (of // WIDE * WIDE + xs, member)

    left, right = lax.rem(x + WIDE - 1, WIDE), lax.rem(x + 1, WIDE)
    row_left, row_right = in_row(place, left), in_row(place, right)
    direct_to = (lax.rem(place + 2, count), member)
    direct_from = (lax.rem(place + count - 2, count), member)
    second_to = (lax.rem(place // WIDE * WIDE + right + 2, count), member)
    second_from = in_row(lax.rem(place + count - 2, count), lax.rem(x + 2 * WIDE - 3, WIDE))

    def remote(source, target, send_sem, recv_sem, device):
        return pltpu.make_async_remote_copy(
            src_ref=source,
            dst_ref=target,
            send_sem=send_sem,
            recv_sem=recv_sem,
            device_id=device,
            device_id_type=MESH_IDS,
        )

    load_tokens = pltpu.make_async_copy(tokens_hbm, tokens_ref, weight_sem.at[2])
    load_tokens.start()
    load_raw = pltpu.make_async_copy(raw_hbm, raw_ref, weight_sem.at[3])
    load_raw.start()
    loads = [
        pltpu.make_async_copy(w_key_ref, weights.at[:, pl.ds(0, cols)], weight_sem.at[0]),
        pltpu.make_async_copy(w_value_ref, weights.at[:, pl.ds(cols, cols)], weight_sem.at[1]),
    ]
    for one in loads:
        one.start()
    barrier = pltpu.get_barrier_semaphore()
    for other in [z_up, z_down, partner, later, earlier, direct_to, direct_from, second_to, second_from, row_left, row_right]:
        pl.semaphore_signal(barrier, inc=1, device_id=other, device_id_type=MESH_IDS)

    own = pl.multiple_of(member * rows, rows)
    beside = pl.multiple_of((upper * 2 + 1 - core) * rows, rows)
    across = pl.multiple_of(((1 - upper) * 2 + core) * rows, rows)
    corner = pl.multiple_of(((1 - upper) * 2 + 1 - core) * rows, rows)

    def norm_rows(step, carry):
        at = pl.ds(pl.multiple_of(step * 16, 16), 16)
        values = tokens_ref[at, :].astype(jnp.float32)
        scale = lax.rsqrt(jnp.mean(values * values, axis=1, keepdims=True) + EPSILON)
        held[pl.ds(pl.multiple_of(own + step * 16, 16), 16), :] = (
            values * scale * gain_ref[...]
        ).astype(jnp.bfloat16)
        return carry

    one_row(gain_blocks, gain_ref)
    load_tokens.wait()
    lax.fori_loop(0, rows // 16, norm_rows, 0)
    pl.semaphore_wait(barrier, 11)

    to_partner = remote(
        held.at[pl.ds(own, rows)], held.at[pl.ds(own, rows)], pair_send.at[0], pair_recv.at[0], partner
    )
    to_partner.start()

    def first_up(step):
        return remote(
            held.at[pl.ds(pl.multiple_of(own + step * piece, piece), piece)],
            relay_up.at[pl.ds(pl.multiple_of(step * piece, piece), piece)],
            relay_send.at[0, step], relay_recv.at[0, step], z_up,
        )

    def first_down(step):
        return remote(
            held.at[pl.ds(pl.multiple_of(own + half + step * piece, piece), piece)],
            relay_down.at[pl.ds(pl.multiple_of(step * piece, piece), piece)],
            relay_send.at[1, step], relay_recv.at[1, step], z_down,
        )

    def second_up(step):
        target = pl.multiple_of(((1 - lax.rem(z + 2, 8) // 4) * 2 + core) * rows + step * piece, piece)
        return remote(
            relay_up.at[pl.ds(pl.multiple_of(step * piece, piece), piece)],
            held.at[pl.ds(target, piece)],
            cross_send.at[0, step], cross_recv.at[0, step], z_up,
        )

    def second_down(step):
        target = pl.multiple_of(
            ((1 - lax.rem(z + 6, 8) // 4) * 2 + core) * rows + half + step * piece, piece
        )
        return remote(
            relay_down.at[pl.ds(pl.multiple_of(step * piece, piece), piece)],
            held.at[pl.ds(target, piece)],
            cross_send.at[1, step], cross_recv.at[1, step], z_down,
        )

    def pass_on(side, step):
        at = pl.ds(pl.multiple_of(across + side * half + step * piece, piece), piece)
        return remote(held.at[at], held.at[at], chunk_send.at[side, step], chunk_recv.at[side, step], partner)

    for step in range(2):
        first_up(step).start()
        first_down(step).start()

    def halo(by, index, begin, size):
        at = pl.ds(begin, size)
        return remote(
            window.at[2, at] if by == 1 else passing.at[at],
            window.at[2 - by, at],
            halo_send.at[by - 1, index], halo_recv.at[by - 1, index], later if by == 1 else second_to,
        )

    def middle(index, begin, size):
        at = pl.ds(begin, size)
        return remote(
            window.at[2, at], passing.at[at], middle_send.at[index], middle_recv.at[index], row_left
        )

    def direct(index, begin, size):
        at = pl.ds(begin, size)
        return remote(
            window.at[2, at], window.at[0, at], halo_send.at[1, index], halo_recv.at[1, index], direct_to
        )

    def hand_on(index, begin, size):
        middle(index, begin, size).wait_recv()
        halo(2, index, begin, size).start()

    def project(parts):
        block = [held[pl.ds(begin, size), :] for begin, size in parts]
        block = block[0] if len(block) == 1 else jnp.concatenate(block, axis=0)
        result = jnp.dot(block, weights[...], preferred_element_type=jnp.float32)
        at = 0
        for begin, size in parts:
            mine = result[at : at + size]
            at += size
            where = pl.ds(begin, size)
            raw_key_ref[where, :] = mine[:, :cols]
            window[2, where, cols:] = mine[:, cols:].astype(jnp.bfloat16)
            for head in range(cols // head_size):
                lanes = slice(head * head_size, (head + 1) * head_size)
                values = mine[:, lanes]
                scale = lax.rsqrt(jnp.mean(values * values, axis=1, keepdims=True) + EPSILON)
                values = values * scale * k_gain_ref[...]
                window[2, where, lanes] = turn(values, cos_ref[where, :], sin_ref[where, :]).astype(
                    jnp.bfloat16
                )

    out_own = pltpu.make_async_copy(
        held.at[pl.ds(own, rows)], gathered_ref.at[pl.ds(own, rows)], out_sem.at[0]
    )
    out_own.start()
    for one in loads:
        one.wait()
    project([(own, rows)])
    halo(1, 0, own, rows).start()
    middle(0, own, rows).start()
    to_partner.wait_recv()
    out_beside = pltpu.make_async_copy(
        held.at[pl.ds(beside, rows)], gathered_ref.at[pl.ds(beside, rows)], out_sem.at[1]
    )
    out_beside.start()
    project([(beside, rows)])
    halo(1, 1, beside, rows).start()
    middle(1, beside, rows).start()
    for step in range(2, 4):
        first_up(step).start()
        first_down(step).start()

    load_raw.wait()
    for head in range(raw_ref.shape[1] // head_size):
        lanes = slice(head * head_size, (head + 1) * head_size)
        values = raw_ref[:, lanes].astype(jnp.float32)
        scale = lax.rsqrt(jnp.mean(values * values, axis=1, keepdims=True) + EPSILON)
        values = values * scale * q_gain_ref[...]
        query_ref[:, lanes] = (turn(values, cos_ref[...], sin_ref[...]) * QUERY_SCALE).astype(
            jnp.bfloat16
        )

    for step in range(4):
        first_up(step).wait_recv()
        second_up(step).start()
        first_down(step).wait_recv()
        second_down(step).start()
        if step == 0:
            hand_on(0, own, rows)
            hand_on(1, beside, rows)

    def groups(step):
        return [
            (pl.multiple_of(base + side * half + step * piece, piece), piece)
            for base in (across, corner)
            for side in (0, 1)
        ]

    def arrive(step, carry):
        for side, copy in ((0, second_up(step)), (1, second_down(step))):
            copy.wait_recv()
            pass_on(side, step).start()

        @pl.when(step > 0)
        def before():
            for index, (begin, size) in enumerate(groups(step - 1)):
                hand_on(2 + (step - 1) * 4 + index, begin, size)

        for side in (0, 1):
            pass_on(side, step).wait_recv()
        project(groups(step))
        for index, (begin, size) in enumerate(groups(step)):
            halo(1, 2 + step * 4 + index, begin, size).start()

        @pl.when(step < 3)
        def over_middle():
            for index, (begin, size) in enumerate(groups(step)):
                middle(2 + step * 4 + index, begin, size).start()

        @pl.when(step == 3)
        def at_last():
            for index, (begin, size) in enumerate(groups(step)):
                direct(2 + step * 4 + index, begin, size).start()

        return carry

    lax.fori_loop(0, 4, arrive, 0)
    out_mine = pltpu.make_async_copy(window.at[2], window_ref.at[2], window_sem.at[0])
    out_mine.start()
    out_across = pltpu.make_async_copy(
        held.at[pl.ds(across, rows)], gathered_ref.at[pl.ds(across, rows)], out_sem.at[2]
    )
    out_corner = pltpu.make_async_copy(
        held.at[pl.ds(corner, rows)], gathered_ref.at[pl.ds(corner, rows)], out_sem.at[3]
    )
    out_across.start()
    out_corner.start()

    def each_halo(kind, steps, act):
        act(kind(0, own, rows))
        act(kind(1, beside, rows))

        def inner(step, carry):
            for index, (begin, size) in enumerate(groups(step)):
                act(kind(2 + step * 4 + index, begin, size))
            return carry

        lax.fori_loop(0, steps, inner, 0)

    def last_direct(act):
        for index, (begin, size) in enumerate(groups(3)):
            act(direct(14 + index, begin, size))

    one_on, two_on = functools.partial(halo, 1), functools.partial(halo, 2)
    each_halo(one_on, 4, lambda copy: copy.wait_recv())
    each_halo(two_on, 3, lambda copy: copy.wait_recv())
    last_direct(lambda copy: copy.wait_recv())
    out_window = pltpu.make_async_copy(
        window.at[pl.ds(0, 2)], window_ref.at[pl.ds(0, 2)], window_sem.at[1]
    )
    out_window.start()
    each_halo(one_on, 4, lambda copy: copy.wait_send())
    each_halo(two_on, 3, lambda copy: copy.wait_send())
    each_halo(middle, 3, lambda copy: copy.wait_send())
    last_direct(lambda copy: copy.wait_send())
    to_partner.wait_send()
    for step in range(4):
        first_up(step).wait_send()
        first_down(step).wait_send()
        second_up(step).wait_send()
        second_down(step).wait_send()
        pass_on(0, step).wait_send()
        pass_on(1, step).wait_send()
    for one in (out_own, out_beside, out_across, out_corner, out_mine, out_window):
        one.wait()


def gather_and_project(tokens, in_gain, raw_queries, w_key, w_value, q_gain, k_gain, cosine, sine):
    rows, depth = tokens.shape
    shard = rows * 4
    cols = w_key.shape[1]
    bf = jnp.bfloat16
    vmem = pl.BlockSpec(memory_space=pltpu.VMEM)
    anywhere = pl.BlockSpec(memory_space=pl.ANY)
    outside = pl.BlockSpec(memory_space=pltpu.HBM)
    dma = pltpu.SemaphoreType.DMA
    return pl.pallas_call(
        gather_kernel,
        out_shape=[
            jax.ShapeDtypeStruct((shard, depth), bf),
            jax.ShapeDtypeStruct(raw_queries.shape, bf),
            jax.ShapeDtypeStruct((shard, cols), jnp.float32),
            jax.ShapeDtypeStruct((3, shard, 2 * cols), bf),
        ],
        in_specs=[outside, vmem, outside] + [vmem] * 4 + [outside] * 2,
        out_specs=[anywhere, vmem, vmem, anywhere],
        scratch_shapes=[
            pltpu.VMEM((shard, depth), bf),
            pltpu.VMEM((rows // 2, depth), bf),
            pltpu.VMEM((rows // 2, depth), bf),
            pltpu.VMEM((depth, 2 * cols), bf),
            pltpu.VMEM((3, shard, 2 * cols), bf),
            pltpu.VMEM((rows, depth), bf),
            pltpu.VMEM(raw_queries.shape, bf),
            pltpu.VMEM((shard, 2 * cols), bf),
            pltpu.VMEM((1, depth), jnp.float32),
            dma((4,)),
            dma((4,)),
            dma((2,)),
            dma((2, 4)),
            dma((2, 4)),
            dma((2, 4)),
            dma((2, 4)),
            dma((1,)),
            dma((1,)),
            dma((2, 4)),
            dma((2, 4)),
            dma((2, 18)),
            dma((2, 18)),
            dma((18,)),
            dma((18,)),
        ],
        compiler_params=pltpu.CompilerParams(
            collective_id=2, has_side_effects=True, vmem_limit_bytes=60 * 1024 * 1024
        ),
        cost_estimate=pl.CostEstimate(
            flops=3_000_000_000, bytes_accessed=150_000_000, transcendentals=0
        ),
        name="gather_and_project",
    )(tokens, in_gain.reshape(depth // 128, 128), raw_queries, q_gain[None, :], k_gain[None, :], cosine, sine, w_key, w_value)


def unturn(values, cosine, sine):
    return values * cosine - pltpu.roll(values, values.shape[-1] // 2, 1) * sine


def norm_back(grad, values, gain):
    scale = lax.rsqrt(jnp.mean(values * values, axis=1, keepdims=True) + EPSILON)
    unit = values * scale
    inner = grad * gain
    return scale * (inner - unit * jnp.mean(inner * unit, axis=1, keepdims=True))


def attend_kernel(
    query_ref, window_ref, out_grad_hbm, low_ref, raw_hbm, raw_key_ref, cos_ref, sin_ref, q_gain_ref, k_gain_ref,
    grad_query_ref, grad_kv_ref,
    exps, along, totals, query_total, parts, returned, out_grad_ref, raw_ref, passing,
    send_sem, recv_sem, middle_send, middle_recv, load_sem, chain_send, chain_recv, sum_send, sum_recv,
):
    shard = query_ref.shape[0]
    head_size = q_gain_ref.shape[1]
    kv_heads = raw_key_ref.shape[1] // head_size
    group_size = query_ref.shape[1] // raw_key_ref.shape[1]
    tile = shard // 2
    reach = 2 * shard
    place = lax.axis_index("seq")
    member = lax.axis_index("tp")
    count = lax.axis_size("seq")
    x = lax.rem(place, WIDE)

    def in_row(of, xs):
        return (of // WIDE * WIDE + xs, member)

    left, right = lax.rem(x + WIDE - 1, WIDE), lax.rem(x + 1, WIDE)
    later = (lax.rem(place + 1, count), member)
    earlier = (lax.rem(place + count - 1, count), member)
    middle_to = in_row(lax.rem(place + count - 2, count), right)
    middle_from = (lax.rem(place // WIDE * WIDE + right + 2, count), member)
    row_left, row_right = in_row(place, left), in_row(place, right)
    load_grads = pltpu.make_async_copy(out_grad_hbm, out_grad_ref, load_sem.at[0])
    load_grads.start()
    load_raw = pltpu.make_async_copy(raw_hbm, raw_ref, load_sem.at[1])
    load_raw.start()
    barrier = pltpu.get_barrier_semaphore()
    for other in [later, earlier, middle_to, middle_from, row_left, row_right]:
        pl.semaphore_signal(barrier, inc=1, device_id=other, device_id_type=MESH_IDS)

    totals[...] = jnp.zeros_like(totals)

    def across(left, right):
        return lax.dot_general(left, right, (((1,), (1,)), ((), ())), preferred_element_type=jnp.float32)

    def back(window, head):
        return pltpu.make_async_remote_copy(
            src_ref=parts.at[window, head] if window == 1 else passing.at[head],
            dst_ref=returned.at[window, head],
            send_sem=send_sem.at[window, head],
            recv_sem=recv_sem.at[window, head],
            device_id=earlier if window == 1 else row_right,
            device_id_type=MESH_IDS,
        )

    def middle(head):
        return pltpu.make_async_remote_copy(
            src_ref=parts.at[0, head],
            dst_ref=passing.at[head],
            send_sem=middle_send.at[head],
            recv_sem=middle_recv.at[head],
            device_id=middle_to,
            device_id_type=MESH_IDS,
        )

    last = kv_heads - 1

    def chain(piece):
        at = pl.ds(piece * tile, tile)
        return pltpu.make_async_remote_copy(
            src_ref=parts.at[0, last, at],
            dst_ref=passing.at[last, at],
            send_sem=chain_send.at[piece],
            recv_sem=chain_recv.at[piece],
            device_id=earlier,
            device_id_type=MESH_IDS,
        )

    def summed(piece):
        at = pl.ds(piece * tile, tile)
        return pltpu.make_async_remote_copy(
            src_ref=parts.at[1, last, at],
            dst_ref=returned.at[1, last, at],
            send_sem=sum_send.at[piece],
            recv_sem=sum_recv.at[piece],
            device_id=earlier,
            device_id_type=MESH_IDS,
        )

    load_grads.wait()
    load_raw.wait()
    for head in range(kv_heads):
        key_lanes = slice(head * head_size, (head + 1) * head_size)
        value_lanes = slice((kv_heads + head) * head_size, (kv_heads + head + 1) * head_size)
        lanes = [
            slice((head * group_size + member_of) * head_size, (head * group_size + member_of + 1) * head_size)
            for member_of in range(group_size)
        ]

        def half(step, carry):
            begin = pl.multiple_of(step * tile, tile)
            rows = pl.ds(begin, tile)
            queries = jnp.concatenate([query_ref[rows, at] for at in lanes], axis=0)
            grads = jnp.concatenate([out_grad_ref[rows, at] for at in lanes], axis=0)
            low = low_ref[step]
            low = jnp.concatenate([low] * group_size, axis=1)
            width = group_size * tile
            high = lax.broadcasted_iota(jnp.int32, (1, tile), 1) + (reach + begin)
            high = jnp.concatenate([high] * group_size, axis=1)

            inner_key = lax.broadcasted_iota(jnp.int32, (tile, width), 0)

            def scores(index, stats, diagonal=False):
                total, delta = stats
                first = pl.multiple_of(begin + index * tile, tile)
                key_rows = pl.ds(first, tile)
                score = across(window_ref[key_rows, key_lanes], queries)
                partial = across(window_ref[key_rows, value_lanes], grads)
                allowed = inner_key >= low - first
                if diagonal:
                    allowed = allowed & (inner_key <= high - first)
                value = jnp.where(allowed, jnp.exp(score), 0.0)
                at = pl.ds(pl.multiple_of(index * tile, tile), tile)
                exps[at, :] = value
                along[at, :] = partial
                total = total + jnp.sum(value, axis=0, keepdims=True)
                delta = delta + jnp.sum(value * partial, axis=0, keepdims=True)
                return total, delta

            nothing = jnp.zeros((1, width), jnp.float32)
            stats = lax.fori_loop(0, reach // tile, scores, (nothing, nothing))
            total, delta = scores(reach // tile, stats, diagonal=True)
            inverse = 1.0 / total
            delta = delta * inverse
            query_total[...] = jnp.zeros_like(query_total)

            def slopes(index, carry):
                key_rows = pl.ds(pl.multiple_of(begin + index * tile, tile), tile)
                at = pl.ds(pl.multiple_of(index * tile, tile), tile)
                probs = exps[at, :] * inverse
                slope = (probs * (along[at, :] - delta)).astype(jnp.bfloat16)
                query_total[...] += contract_first(window_ref[key_rows, key_lanes], slope)
                totals[key_rows, key_lanes] += jnp.dot(slope, queries, preferred_element_type=jnp.float32)
                totals[key_rows, value_lanes] += jnp.dot(
                    probs.astype(jnp.bfloat16), grads, preferred_element_type=jnp.float32
                )
                return carry

            lax.fori_loop(0, reach // tile + 1, slopes, 0)
            flipped = query_total[...].T
            for member_of, at in enumerate(lanes):
                grad = flipped[member_of * tile : (member_of + 1) * tile] * QUERY_SCALE
                grad = unturn(grad, cos_ref[rows, :], sin_ref[rows, :])
                values = raw_ref[rows, at].astype(jnp.float32)
                grad_query_ref[rows, at] = norm_back(grad, values, q_gain_ref[...]).astype(jnp.bfloat16)
            return carry

        lax.fori_loop(0, 2, half, 0)
        for window in range(2 if head < last else 1):
            rows = slice(window * shard, (window + 1) * shard)
            parts[window, head, :, :head_size] = totals[rows, key_lanes].astype(jnp.bfloat16)
            parts[window, head, :, head_size:] = totals[rows, value_lanes].astype(jnp.bfloat16)
        if head == 0:
            pl.semaphore_wait(barrier, 6)
        if head < last:
            middle(head).start()
            back(1, head).start()
        else:
            chain(0).start()
            chain(1).start()

    for head in range(last):
        middle(head).wait_recv()
        back(0, head).start()
    for piece in range(2):
        chain(piece).wait_recv()
        here = slice(piece * tile, (piece + 1) * tile)
        rows = slice(shard + piece * tile, shard + (piece + 1) * tile)
        lanes = slice(last * head_size, (last + 1) * head_size)
        parts[1, last, here, :head_size] = (
            totals[rows, lanes] + passing[last, here, :head_size].astype(jnp.float32)
        ).astype(jnp.bfloat16)
        lanes = slice((kv_heads + last) * head_size, (kv_heads + last + 1) * head_size)
        parts[1, last, here, head_size:] = (
            totals[rows, lanes] + passing[last, here, head_size:].astype(jnp.float32)
        ).astype(jnp.bfloat16)
        summed(piece).start()
    own = slice(reach, reach + shard)
    for head in range(kv_heads):
        key_lanes = slice(head * head_size, (head + 1) * head_size)
        value_lanes = slice((kv_heads + head) * head_size, (kv_heads + head + 1) * head_size)
        if head < last:
            for window in range(2):
                back(window, head).wait_recv()
        else:
            summed(0).wait_recv()
            summed(1).wait_recv()
        key_grad = totals[own, key_lanes]
        value_grad = totals[own, value_lanes]
        for window in (1, 0) if head < last else (1,):
            key_grad = key_grad + returned[window, head, :, :head_size].astype(jnp.float32)
            value_grad = value_grad + returned[window, head, :, head_size:].astype(jnp.float32)
        grad_kv_ref[:, value_lanes] = value_grad.astype(jnp.bfloat16)
        key_grad = unturn(key_grad, cos_ref[...], sin_ref[...])
        grad_kv_ref[:, key_lanes] = norm_back(key_grad, raw_key_ref[:, key_lanes], k_gain_ref[...]).astype(
            jnp.bfloat16
        )
    for head in range(last):
        middle(head).wait_send()
        for window in range(2):
            back(window, head).wait_send()
    for piece in range(2):
        chain(piece).wait_send()
        summed(piece).wait_send()


def attend_back(query_rot, window, out_grad, low, raw_queries, raw_keys, cosine, sine, q_gain, k_gain):
    shard = query_rot.shape[0]
    head_size = q_gain.shape[0]
    kv_heads = raw_keys.shape[1] // head_size
    group_size = query_rot.shape[1] // raw_keys.shape[1]
    tile = shard // 2
    width = group_size * tile
    vmem = pl.BlockSpec(memory_space=pltpu.VMEM)
    outside = pl.BlockSpec(memory_space=pltpu.HBM)
    return pl.pallas_call(
        attend_kernel,
        out_shape=[
            jax.ShapeDtypeStruct(query_rot.shape, jnp.bfloat16),
            jax.ShapeDtypeStruct((shard, 2 * raw_keys.shape[1]), jnp.bfloat16),
        ],
        in_specs=[vmem, vmem, outside, vmem, outside] + [vmem] * 5,
        out_specs=[vmem] * 2,
        scratch_shapes=[
            pltpu.VMEM((2 * shard + tile, width), jnp.float32),
            pltpu.VMEM((2 * shard + tile, width), jnp.float32),
            pltpu.VMEM((3 * shard, 2 * raw_keys.shape[1]), jnp.float32),
            pltpu.VMEM((head_size, width), jnp.float32),
            pltpu.VMEM((2, kv_heads, shard, 2 * head_size), jnp.bfloat16),
            pltpu.VMEM((2, kv_heads, shard, 2 * head_size), jnp.bfloat16),
            pltpu.VMEM(query_rot.shape, jnp.bfloat16),
            pltpu.VMEM(query_rot.shape, jnp.bfloat16),
            pltpu.VMEM((kv_heads, shard, 2 * head_size), jnp.bfloat16),
            pltpu.SemaphoreType.DMA((2, kv_heads)),
            pltpu.SemaphoreType.DMA((2, kv_heads)),
            pltpu.SemaphoreType.DMA((kv_heads,)),
            pltpu.SemaphoreType.DMA((kv_heads,)),
            pltpu.SemaphoreType.DMA((2,)),
            pltpu.SemaphoreType.DMA((2,)),
            pltpu.SemaphoreType.DMA((2,)),
            pltpu.SemaphoreType.DMA((2,)),
            pltpu.SemaphoreType.DMA((2,)),
        ],
        compiler_params=pltpu.CompilerParams(
            collective_id=3, has_side_effects=True, vmem_limit_bytes=60 * 1024 * 1024
        ),
        cost_estimate=pl.CostEstimate(
            flops=8_000_000_000, bytes_accessed=100_000_000, transcendentals=3_000_000
        ),
        name="attend_back",
    )(
        query_rot, window.reshape(3 * shard, window.shape[2]), out_grad, low, raw_queries, raw_keys,
        cosine, sine, q_gain[None, :], k_gain[None, :],
    )


def finish_kernel(
    gathered_ref, grad_ref, w_key_ref, w_value_ref, tokens_ref, gain_blocks,
    key_out, value_out, grad_x_ref,
    held, weights, tokens, gain_ref, total_own, corner_out, corner_in, beside_out, beside_in, cross_out, cross_in,
    relay_up, relay_down,
    key_term, value_term, key_send, order, value_total, key_next, value_next, last_send, last_recv,
    *rest,
):
    bufs_a, bufs_b, bufs_c, bufs_d = rest[0:6], rest[6:12], rest[12:18], rest[18:24]
    sems = rest[24:34]
    load_sem, weight_sem, pair_send, pair_recv, relay_send, relay_recv, cross_send, cross_recv = rest[34:42]
    corner_send, corner_recv = rest[42:]
    depth = gain_ref.shape[1]
    block = tokens_ref.shape[0]
    rows = key_out.shape[0]
    cols = key_out.shape[1]
    half = block // 2
    piece = half // 4
    big, mid = 16 * rows, 4 * rows
    split_big = big // 2
    split_mid = mid // 2 + mid // 2 % 16
    slab = 768 if depth % 768 == 0 else 128
    strip = 384 if depth % 384 == 0 else 128
    place = lax.axis_index("seq")
    member = lax.axis_index("tp")
    core = lax.rem(member, 2)
    upper = member // 2
    x = lax.rem(place, 4)
    z = lax.rem(place // 4, 4)
    y = place // 16
    height = upper * 4 + z

    def device(ys, zs, xs):
        return ((ys * 4 + zs) * 4 + xs, member)

    def along_z(by):
        other = lax.rem(height + by, 8)
        return ((y * 4 + lax.rem(other, 4)) * 4 + x, other // 4 * 2 + core)

    def remote(source, target, send_sem, recv_sem, to):
        return pltpu.make_async_remote_copy(
            src_ref=source,
            dst_ref=target,
            send_sem=send_sem,
            recv_sem=recv_sem,
            device_id=to,
            device_id_type=MESH_IDS,
        )

    def weight_load(step):
        at = pl.ds(pl.multiple_of(step * slab, slab), slab)
        return (
            pltpu.make_async_copy(w_key_ref.at[at], weights.at[at, pl.ds(0, cols)], weight_sem.at[0, step]),
            pltpu.make_async_copy(w_value_ref.at[at], weights.at[at, pl.ds(cols, cols)], weight_sem.at[1, step]),
        )

    for step in range(depth // slab):
        for one in weight_load(step):
            one.start()
    load_held = pltpu.make_async_copy(gathered_ref, held, load_sem.at[0])
    load_held.start()
    load_tokens = pltpu.make_async_copy(tokens_ref, tokens, load_sem.at[1])
    load_tokens.start()

    z_up, z_down = along_z(2), along_z(6)
    partner = (place, upper * 2 + 1 - core)
    x_up, x_down = device(y, z, lax.rem(x + 1, 4)), device(y, z, lax.rem(x + 3, 4))
    y_up, y_down = device(lax.rem(y + 1, 4), z, x), device(lax.rem(y + 3, 4), z, x)
    z_others = [device(y, lax.rem(z + d, 4), x) for d in (1, 2, 3)]
    barrier = pltpu.get_barrier_semaphore()
    for other in [z_up, z_down, partner, x_up, x_down, y_up, y_down] + z_others:
        pl.semaphore_signal(barrier, inc=1, device_id=other, device_id_type=MESH_IDS)

    own = pl.multiple_of(member * block, block)
    beside = pl.multiple_of((upper * 2 + 1 - core) * block, block)
    across = pl.multiple_of(((1 - upper) * 2 + core) * block, block)
    corner = pl.multiple_of(((1 - upper) * 2 + 1 - core) * block, block)

    def part(begin, store, first=False):
        grads = grad_ref[pl.ds(begin, block), :]

        def one_slab(step, carry):
            if first:
                for one in weight_load(step):
                    one.wait()
            at = pl.ds(pl.multiple_of(step * slab, slab), slab)
            store(at, contract_last(grads, weights[at, :]))
            return carry

        lax.fori_loop(0, depth // slab, one_slab, 0)

    def store_corner(at, value):
        corner_out[:, at] = value.astype(jnp.bfloat16)

    part(corner, store_corner, first=True)
    pl.semaphore_wait(barrier, 10)

    def rows_at(side, step):
        return pl.ds(side * half + step * piece, piece)

    pieces = [(side, step) for step in range(4) for side in (0, 1)]
    send_corner = {
        (side, step): remote(
            corner_out.at[rows_at(side, step)], corner_in.at[rows_at(side, step)],
            corner_send.at[side, step], corner_recv.at[side, step], partner,
        )
        for side, step in pieces
    }
    for one in pieces:
        send_corner[one].start()

    def store_total(at, value):
        total_own[:, at] = value

    part(across, store_total)
    def small(step):
        return pl.ds(step * piece, piece)

    first = [
        [
            remote(cross_out.at[rows_at(0, step)], relay_up.at[small(step)], relay_send.at[0, step], relay_recv.at[0, step], z_up),
            remote(cross_out.at[rows_at(1, step)], relay_down.at[small(step)], relay_send.at[1, step], relay_recv.at[1, step], z_down),
        ]
        for step in range(4)
    ]
    second = [
        [
            remote(relay_up.at[small(step)], cross_in.at[rows_at(0, step)], cross_send.at[0, step], cross_recv.at[0, step], z_up),
            remote(relay_down.at[small(step)], cross_in.at[rows_at(1, step)], cross_send.at[1, step], cross_recv.at[1, step], z_down),
        ]
        for step in range(4)
    ]
    for side, step in pieces:
        send_corner[side, step].wait_recv()
        at = rows_at(side, step)
        cross_out[at, :] = (total_own[at, :] + corner_in[at, :].astype(jnp.float32)).astype(jnp.bfloat16)
        first[step][side].start()

    def relay(step):
        for side in (0, 1):
            first[step][side].wait_recv()
            second[step][side].start()

    load_held.wait()

    def strips(step, carry):
        at = pl.ds(pl.multiple_of(step * strip, strip), strip)
        result = contract_first(held[:, at], grad_ref[...])
        key_term[at, :] = result[:, :cols]
        value_term[at, :] = result[:, cols:].astype(jnp.bfloat16)
        return carry

    lax.fori_loop(0, depth // strip, strips, 0)

    def finish_b1(total):
        for quarter in range(4):
            at = pl.ds(quarter * mid, mid)
            value_total[at, :] = total(at)
        for xs in range(4):
            for zs in range(4):
                order[zs * rows : zs * rows + rows, :] = value_total[
                    zs * mid + xs * rows : zs * mid + xs * rows + rows, :
                ]
            value_next[xs] = order[...].astype(jnp.bfloat16)

    second_b = ring_sum(
        lambda t: value_term.at[pl.ds(pl.multiple_of(t * big, 16), big)],
        big, split_big, y, y_up, y_down, bufs_b, sems[2:4], finish_b1,
    )

    for ys in range(4):
        for xs in range(4):
            for zs in range(4):
                begin = ((ys * 4 + zs) * 4 + xs) * rows
                order[zs * rows : zs * rows + rows, :] = key_term[begin : begin + rows, :]
            key_send[xs, ys * mid : ys * mid + mid, :] = order[...].astype(jnp.bfloat16)

    def finish_a1(total):
        for quarter in range(4):
            at = pl.ds(quarter * mid, mid)
            key_next[quarter] = total(at).astype(jnp.bfloat16)

    second_a = ring_sum(
        lambda t: key_send.at[t],
        big, split_big, x, x_up, x_down, bufs_a, sems[0:2], finish_a1,
    )
    relay(0)

    def store_beside(at, value):
        beside_out[:, at] = value.astype(jnp.bfloat16)

    part(beside, store_beside)
    send_beside = remote(beside_out, beside_in, pair_send.at[1], pair_recv.at[1], partner)
    send_beside.start()
    part(own, store_total)
    relay(1)
    third_b = second_b()
    third_a = second_a()
    relay(2)
    drain_b = third_b()

    def finish_last(at):
        def finish(total):
            order[...] = total(pl.ds(0, mid))
            for zs in range(4):
                last_send[zs, 0:rows, at : at + cols] = order[
                    zs * rows : zs * rows + rows, :
                ].astype(jnp.bfloat16)
                last_send[zs, rows:, at : at + cols] = jnp.zeros(
                    (last_send.shape[1] - rows, cols), jnp.bfloat16
                )

        return finish

    second_d = ring_sum(
        lambda t: value_next.at[t],
        mid, split_mid, x, x_up, x_down, bufs_d, sems[6:8], finish_last(cols),
    )
    relay(3)
    drain_a = third_a()
    second_c = ring_sum(
        lambda t: key_next.at[t],
        mid, split_mid, y, y_up, y_down, bufs_c, sems[4:6], finish_last(0),
    )
    third_d = second_d()
    third_c = second_c()
    drain_d = third_d()
    drain_c = third_c()
    copies = []
    for d in (1, 2, 3):
        one = remote(
            last_send.at[lax.rem(z + d, 4)], last_recv.at[d - 1], sems[8].at[d - 1], sems[9].at[d - 1], z_others[d - 1]
        )
        one.start()
        copies.append(one)

    one_row(gain_blocks, gain_ref)
    load_tokens.wait()
    send_beside.wait_recv()
    for step in range(4):
        for side in (0, 1):
            second[step][side].wait_recv()
            at = rows_at(side, step)
            grad = (
                total_own[at, :] + beside_in[at, :].astype(jnp.float32) + cross_in[at, :].astype(jnp.float32)
            )
            grad_x_ref[at, :] = norm_back(grad, tokens[at, :].astype(jnp.float32), gain_ref[...]).astype(
                jnp.bfloat16
            )

    for one in copies:
        one.wait_recv()
    total = last_send[z, 0:rows, :].astype(jnp.float32)
    for d in range(3):
        total = total + last_recv[d, 0:rows, :].astype(jnp.float32)
    key_out[...] = total[:, 0:cols]
    value_out[...] = total[:, cols:]
    for one in copies:
        one.wait_send()
    for drain in (drain_a, drain_b, drain_c, drain_d):
        drain()
    for one in pieces:
        send_corner[one].wait_send()
    send_beside.wait_send()
    for pair in first + second:
        for one in pair:
            one.wait_send()


def finish(gathered, grad_kv, w_key, w_value, tokens, in_gain):
    shard, depth = gathered.shape
    block = tokens.shape[0]
    cols = w_key.shape[1]
    rows = depth // 64
    big, mid = 16 * rows, 4 * rows
    split_big = big // 2
    split_mid = mid // 2 + mid // 2 % 16
    padded = (rows + 15) // 16 * 16
    slabs = depth // (768 if depth % 768 == 0 else 128)
    bf = jnp.bfloat16
    dma = pltpu.SemaphoreType.DMA
    vmem = pl.BlockSpec(memory_space=pltpu.VMEM)
    outside = pl.BlockSpec(memory_space=pltpu.HBM)

    def bufs(size, split):
        return [
            pltpu.VMEM((split, cols), bf),
            pltpu.VMEM((size - split, cols), bf),
            pltpu.VMEM((split, cols), bf),
            pltpu.VMEM((size - split, cols), bf),
            pltpu.VMEM((size, cols), bf),
            pltpu.VMEM((size, cols), bf),
        ]

    return pl.pallas_call(
        finish_kernel,
        out_shape=[
            jax.ShapeDtypeStruct((rows, cols), jnp.float32),
            jax.ShapeDtypeStruct((rows, cols), jnp.float32),
            jax.ShapeDtypeStruct((block, depth), bf),
        ],
        in_specs=[outside, vmem, outside, outside, outside, vmem],
        out_specs=[vmem] * 3,
        scratch_shapes=[
            pltpu.VMEM((shard, depth), bf),
            pltpu.VMEM((depth, 2 * cols), bf),
            pltpu.VMEM((block, depth), bf),
            pltpu.VMEM((1, depth), jnp.float32),
            pltpu.VMEM((block, depth), jnp.float32),
        ]
        + [pltpu.VMEM((block, depth), bf)] * 6
        + [pltpu.VMEM((block // 2, depth), bf)] * 2
        + [
            pltpu.VMEM((depth, cols), jnp.float32),
            pltpu.VMEM((depth, cols), bf),
            pltpu.VMEM((4, big, cols), bf),
            pltpu.VMEM((mid, cols), jnp.float32),
            pltpu.VMEM((big, cols), jnp.float32),
            pltpu.VMEM((4, mid, cols), bf),
            pltpu.VMEM((4, mid, cols), bf),
            pltpu.VMEM((4, padded, 2 * cols), bf),
            pltpu.VMEM((3, padded, 2 * cols), bf),
        ]
        + bufs(big, split_big)
        + bufs(big, split_big)
        + bufs(mid, split_mid)
        + bufs(mid, split_mid)
        + [dma((6,))] * 8
        + [dma((3,))] * 2
        + [dma((2,)), dma((2, slabs)), dma((2,)), dma((2,))]
        + [dma((2, 4))] * 6,
        compiler_params=pltpu.CompilerParams(
            collective_id=1, has_side_effects=True, vmem_limit_bytes=51 * 1024 * 1024
        ),
        cost_estimate=pl.CostEstimate(
            flops=6_000_000_000, bytes_accessed=150_000_000, transcendentals=0
        ),
        name="finish",
    )(gathered, grad_kv, w_key, w_value, tokens, in_gain.reshape(depth // 128, 128))


def shards(tokens, in_gain, raw_queries, w_key, w_value, q_gain, k_gain, doc_lengths, out_grad):
    head_size = q_gain.shape[0]
    shard_rows = tokens.shape[0] * lax.axis_size("tp")
    reach = 2 * shard_rows
    first_row = lax.axis_index("seq") * shard_rows
    positions = first_row + jnp.arange(shard_rows, dtype=jnp.int32)
    begins = doc_begin(doc_lengths, positions)
    lowest = jnp.maximum(begins, positions - (WINDOW - 1))
    low = (lowest - (first_row - reach)).reshape(2, 1, shard_rows // 2)
    cosine, sine = angle_tables(positions - begins, head_size)
    gathered, query_rot, raw_keys, window = gather_and_project(
        tokens, in_gain, raw_queries, w_key, w_value, q_gain, k_gain, cosine, sine
    )
    grad_queries, grad_kv = attend_back(
        query_rot, window, out_grad, low, raw_queries, raw_keys, cosine, sine, q_gain, k_gain
    )
    grad_wk, grad_wv, grad_x = finish(gathered, grad_kv, w_key, w_value, tokens, in_gain)
    return (grad_x, grad_queries, grad_wk, grad_wv)


def solution(mesh):
    placed = (
        P(("seq", "tp"), None),
        P(),
        P("seq", "tp"),
        P(None, "tp"),
        P(None, "tp"),
        P(),
        P(),
        P(),
        P("seq", "tp"),
    )
    return jax.shard_map(
        shards,
        mesh=mesh,
        in_specs=placed,
        out_specs=(P(("seq", "tp"), None), P("seq", "tp"), P("seq", "tp"), P("seq", "tp")),
        check_vma=False,
    )
```

```python
import functools

import jax
import jax.numpy as jnp
from jax import lax
from jax.experimental import pallas as pl
from jax.experimental.pallas import tpu as pltpu
from jax.sharding import PartitionSpec as P

WINDOW = 1024
WIDE = 4


EPSILON = 1e-06
QUERY_SCALE = 168.0 ** (-0.5)
ROPE_BASE = 10000.0


def doc_begin(doc_lengths, positions):
    endings = jnp.cumsum(doc_lengths, dtype=jnp.int32)
    starts = endings - doc_lengths
    inside = starts[None, :] <= positions[:, None]
    return jnp.max(jnp.where(inside, starts[None, :], jnp.zeros_like(starts)[None, :]), axis=1)


def angle_tables(positions, head_size):
    half_size = head_size // 2
    lane = jnp.arange(head_size, dtype=jnp.int32)
    powers = (lane % half_size).astype(jnp.float32) * (2.0 / head_size)
    frequency = ROPE_BASE ** (-powers)
    angles = positions.astype(jnp.float32)[:, None] * frequency[None, :]
    sign = jnp.where(lane < half_size, -1.0, 1.0)
    return jnp.cos(angles), jnp.sin(angles) * sign[None, :]


def one_row(blocks_ref, row_ref):
    for index in range(blocks_ref.shape[0]):
        row_ref[:, index * 128 : (index + 1) * 128] = blocks_ref[index : index + 1, :]


def contract_last(left, right):
    return lax.dot_general(
        left, right, (((1,), (1,)), ((), ())), preferred_element_type=jnp.float32
    )


def contract_first(left, right):
    return lax.dot_general(
        left, right, (((0,), (0,)), ((), ())), preferred_element_type=jnp.float32
    )


MESH_IDS = pl.DeviceIdType.MESH


def ring_sum(piece, size, split, pos, up, down, bufs, sems, finish):
    half_up, half_down, mixed_up, mixed_down, full_up, full_down = bufs
    send_sem, recv_sem = sems
    far = lax.rem(pos + 2, 4)
    after = lax.rem(pos + 1, 4)
    before = lax.rem(pos + 3, 4)
    low = pl.ds(0, split)
    high = pl.ds(split, size - split)

    def copy(index, source, target, device):
        return pltpu.make_async_remote_copy(
            src_ref=source,
            dst_ref=target,
            send_sem=send_sem.at[index],
            recv_sem=recv_sem.at[index],
            device_id=device,
            device_id_type=MESH_IDS,
        )

    first = [
        copy(0, piece(far).at[low], half_up, up),
        copy(1, piece(far).at[high], half_down, down),
        copy(2, piece(after).at[high], full_up.at[high], up),
        copy(3, piece(before).at[low], full_down.at[low], down),
    ]
    for one in first:
        one.start()

    def second():
        first[0].wait_recv()
        mixed_up[...] = (
            piece(after)[low, :].astype(jnp.float32) + half_up[...].astype(jnp.float32)
        ).astype(jnp.bfloat16)
        last_up = copy(4, mixed_up, full_up.at[low], up)
        last_up.start()
        first[1].wait_recv()
        mixed_down[...] = (
            piece(before)[high, :].astype(jnp.float32) + half_down[...].astype(jnp.float32)
        ).astype(jnp.bfloat16)
        last_down = copy(5, mixed_down, full_down.at[high], down)
        last_down.start()

        def third():
            first[2].wait_recv()
            first[3].wait_recv()
            last_up.wait_recv()
            last_down.wait_recv()
            finish(
                lambda rows: piece(pos)[rows, :].astype(jnp.float32)
                + full_up[rows, :].astype(jnp.float32)
                + full_down[rows, :].astype(jnp.float32)
            )

            def drain():
                for one in first + [last_up, last_down]:
                    one.wait_send()

            return drain

        return third

    return second


def turn(values, cosine, sine):
    return values * cosine + pltpu.roll(values, values.shape[-1] // 2, 1) * sine


def gather_kernel(
    tokens_hbm, gain_blocks, raw_hbm, q_gain_ref, k_gain_ref, cos_ref, sin_ref, w_key_ref, w_value_ref,
    gathered_ref, query_ref, raw_key_ref, window_ref,
    held, relay_up, relay_down, weights, window, tokens_ref, raw_ref, passing, gain_ref,
    weight_sem, out_sem, window_sem, relay_send, relay_recv, cross_send, cross_recv,
    pair_send, pair_recv, chunk_send, chunk_recv, halo_send, halo_recv, middle_send, middle_recv,
):
    rows = tokens_ref.shape[0]
    half = rows // 2
    piece = half // 4
    cols = w_key_ref.shape[1]
    head_size = k_gain_ref.shape[1]
    place = lax.axis_index("seq")
    member = lax.axis_index("tp")
    count = lax.axis_size("seq")
    core = lax.rem(member, 2)
    upper = member // 2
    x = lax.rem(place, WIDE)
    z = upper * 4 + lax.rem(place // WIDE, 4)
    y = place // (4 * WIDE)

    def along_z(by):
        other = lax.rem(z + by, 8)
        return ((y * 4 + lax.rem(other, 4)) * WIDE + x, other // 4 * 2 + core)

    z_up, z_down = along_z(2), along_z(6)
    partner = (place, upper * 2 + 1 - core)
    later = (lax.rem(place + 1, count), member)
    earlier = (lax.rem(place + count - 1, count), member)

    def in_row(of, xs):
        return (of // WIDE * WIDE + xs, member)

    left, right = lax.rem(x + WIDE - 1, WIDE), lax.rem(x + 1, WIDE)
    row_left, row_right = in_row(place, left), in_row(place, right)
    direct_to = (lax.rem(place + 2, count), member)
    direct_from = (lax.rem(place + count - 2, count), member)
    second_to = (lax.rem(place // WIDE * WIDE + right + 2, count), member)
    second_from = in_row(lax.rem(place + count - 2, count), lax.rem(x + 2 * WIDE - 3, WIDE))

    def remote(source, target, send_sem, recv_sem, device):
        return pltpu.make_async_remote_copy(
            src_ref=source,
            dst_ref=target,
            send_sem=send_sem,
            recv_sem=recv_sem,
            device_id=device,
            device_id_type=MESH_IDS,
        )

    load_tokens = pltpu.make_async_copy(tokens_hbm, tokens_ref, weight_sem.at[2])
    load_tokens.start()
    load_raw = pltpu.make_async_copy(raw_hbm, raw_ref, weight_sem.at[3])
    load_raw.start()
    loads = [
        pltpu.make_async_copy(w_key_ref, weights.at[:, pl.ds(0, cols)], weight_sem.at[0]),
        pltpu.make_async_copy(w_value_ref, weights.at[:, pl.ds(cols, cols)], weight_sem.at[1]),
    ]
    for one in loads:
        one.start()
    barrier = pltpu.get_barrier_semaphore()
    for other in [z_up, z_down, partner, later, earlier, direct_to, direct_from, second_to, second_from, row_left, row_right]:
        pl.semaphore_signal(barrier, inc=1, device_id=other, device_id_type=MESH_IDS)

    own = pl.multiple_of(member * rows, rows)
    beside = pl.multiple_of((upper * 2 + 1 - core) * rows, rows)
    across = pl.multiple_of(((1 - upper) * 2 + core) * rows, rows)
    corner = pl.multiple_of(((1 - upper) * 2 + 1 - core) * rows, rows)

    def norm_rows(step, carry):
        at = pl.ds(pl.multiple_of(step * 16, 16), 16)
        values = tokens_ref[at, :].astype(jnp.float32)
        scale = lax.rsqrt(jnp.mean(values * values, axis=1, keepdims=True) + EPSILON)
        held[pl.ds(pl.multiple_of(own + step * 16, 16), 16), :] = (
            values * scale * gain_ref[...]
        ).astype(jnp.bfloat16)
        return carry

    one_row(gain_blocks, gain_ref)
    load_tokens.wait()
    lax.fori_loop(0, rows // 16, norm_rows, 0)
    pl.semaphore_wait(barrier, 11)

    to_partner = remote(
        held.at[pl.ds(own, rows)], held.at[pl.ds(own, rows)], pair_send.at[0], pair_recv.at[0], partner
    )
    to_partner.start()

    def first_up(step):
        return remote(
            held.at[pl.ds(pl.multiple_of(own + step * piece, piece), piece)],
            relay_up.at[pl.ds(pl.multiple_of(step * piece, piece), piece)],
            relay_send.at[0, step], relay_recv.at[0, step], z_up,
        )

    def first_down(step):
        return remote(
            held.at[pl.ds(pl.multiple_of(own + half + step * piece, piece), piece)],
            relay_down.at[pl.ds(pl.multiple_of(step * piece, piece), piece)],
            relay_send.at[1, step], relay_recv.at[1, step], z_down,
        )

    def second_up(step):
        target = pl.multiple_of(((1 - lax.rem(z + 2, 8) // 4) * 2 + core) * rows + step * piece, piece)
        return remote(
            relay_up.at[pl.ds(pl.multiple_of(step * piece, piece), piece)],
            held.at[pl.ds(target, piece)],
            cross_send.at[0, step], cross_recv.at[0, step], z_up,
        )

    def second_down(step):
        target = pl.multiple_of(
            ((1 - lax.rem(z + 6, 8) // 4) * 2 + core) * rows + half + step * piece, piece
        )
        return remote(
            relay_down.at[pl.ds(pl.multiple_of(step * piece, piece), piece)],
            held.at[pl.ds(target, piece)],
            cross_send.at[1, step], cross_recv.at[1, step], z_down,
        )

    def pass_on(side, step):
        at = pl.ds(pl.multiple_of(across + side * half + step * piece, piece), piece)
        return remote(held.at[at], held.at[at], chunk_send.at[side, step], chunk_recv.at[side, step], partner)

    for step in range(2):
        first_up(step).start()
        first_down(step).start()

    def halo(by, index, begin, size):
        at = pl.ds(begin, size)
        return remote(
            window.at[2, at] if by == 1 else passing.at[at],
            window.at[2 - by, at],
            halo_send.at[by - 1, index], halo_recv.at[by - 1, index], later if by == 1 else second_to,
        )

    def middle(index, begin, size):
        at = pl.ds(begin, size)
        return remote(
            window.at[2, at], passing.at[at], middle_send.at[index], middle_recv.at[index], row_left
        )

    def direct(index, begin, size):
        at = pl.ds(begin, size)
        return remote(
            window.at[2, at], window.at[0, at], halo_send.at[1, index], halo_recv.at[1, index], direct_to
        )

    def hand_on(index, begin, size):
        middle(index, begin, size).wait_recv()
        halo(2, index, begin, size).start()

    def project(parts):
        block = [held[pl.ds(begin, size), :] for begin, size in parts]
        block = block[0] if len(block) == 1 else jnp.concatenate(block, axis=0)
        result = jnp.dot(block, weights[...], preferred_element_type=jnp.float32)
        at = 0
        for begin, size in parts:
            mine = result[at : at + size]
            at += size
            where = pl.ds(begin, size)
            raw_key_ref[where, :] = mine[:, :cols]
            window[2, where, cols:] = mine[:, cols:].astype(jnp.bfloat16)
            for head in range(cols // head_size):
                lanes = slice(head * head_size, (head + 1) * head_size)
                values = mine[:, lanes]
                scale = lax.rsqrt(jnp.mean(values * values, axis=1, keepdims=True) + EPSILON)
                values = values * scale * k_gain_ref[...]
                window[2, where, lanes] = turn(values, cos_ref[where, :], sin_ref[where, :]).astype(
                    jnp.bfloat16
                )

    out_own = pltpu.make_async_copy(
        held.at[pl.ds(own, rows)], gathered_ref.at[pl.ds(own, rows)], out_sem.at[0]
    )
    out_own.start()
    for one in loads:
        one.wait()
    project([(own, rows)])
    halo(1, 0, own, rows).start()
    middle(0, own, rows).start()
    to_partner.wait_recv()
    out_beside = pltpu.make_async_copy(
        held.at[pl.ds(beside, rows)], gathered_ref.at[pl.ds(beside, rows)], out_sem.at[1]
    )
    out_beside.start()
    project([(beside, rows)])
    halo(1, 1, beside, rows).start()
    middle(1, beside, rows).start()
    for step in range(2, 4):
        first_up(step).start()
        first_down(step).start()

    load_raw.wait()
    for head in range(raw_ref.shape[1] // head_size):
        lanes = slice(head * head_size, (head + 1) * head_size)
        values = raw_ref[:, lanes].astype(jnp.float32)
        scale = lax.rsqrt(jnp.mean(values * values, axis=1, keepdims=True) + EPSILON)
        values = values * scale * q_gain_ref[...]
        query_ref[:, lanes] = (turn(values, cos_ref[...], sin_ref[...]) * QUERY_SCALE).astype(
            jnp.bfloat16
        )

    for step in range(4):
        first_up(step).wait_recv()
        second_up(step).start()
        first_down(step).wait_recv()
        second_down(step).start()
        if step == 0:
            hand_on(0, own, rows)
            hand_on(1, beside, rows)

    def groups(step):
        return [
            (pl.multiple_of(base + side * half + step * piece, piece), piece)
            for base in (across, corner)
            for side in (0, 1)
        ]

    def arrive(step, carry):
        for side, copy in ((0, second_up(step)), (1, second_down(step))):
            copy.wait_recv()
            pass_on(side, step).start()

        @pl.when(step > 0)
        def before():
            for index, (begin, size) in enumerate(groups(step - 1)):
                hand_on(2 + (step - 1) * 4 + index, begin, size)

        for side in (0, 1):
            pass_on(side, step).wait_recv()
        project(groups(step))
        for index, (begin, size) in enumerate(groups(step)):
            halo(1, 2 + step * 4 + index, begin, size).start()

        @pl.when(step < 3)
        def over_middle():
            for index, (begin, size) in enumerate(groups(step)):
                middle(2 + step * 4 + index, begin, size).start()

        @pl.when(step == 3)
        def at_last():
            for index, (begin, size) in enumerate(groups(step)):
                direct(2 + step * 4 + index, begin, size).start()

        return carry

    lax.fori_loop(0, 4, arrive, 0)
    out_mine = pltpu.make_async_copy(window.at[2], window_ref.at[2], window_sem.at[0])
    out_mine.start()
    out_across = pltpu.make_async_copy(
        held.at[pl.ds(across, rows)], gathered_ref.at[pl.ds(across, rows)], out_sem.at[2]
    )
    out_corner = pltpu.make_async_copy(
        held.at[pl.ds(corner, rows)], gathered_ref.at[pl.ds(corner, rows)], out_sem.at[3]
    )
    out_across.start()
    out_corner.start()

    def each_halo(kind, steps, act):
        act(kind(0, own, rows))
        act(kind(1, beside, rows))

        def inner(step, carry):
            for index, (begin, size) in enumerate(groups(step)):
                act(kind(2 + step * 4 + index, begin, size))
            return carry

        lax.fori_loop(0, steps, inner, 0)

    def last_direct(act):
        for index, (begin, size) in enumerate(groups(3)):
            act(direct(14 + index, begin, size))

    one_on, two_on = functools.partial(halo, 1), functools.partial(halo, 2)
    each_halo(one_on, 4, lambda copy: copy.wait_recv())
    each_halo(two_on, 3, lambda copy: copy.wait_recv())
    last_direct(lambda copy: copy.wait_recv())
    out_window = pltpu.make_async_copy(
        window.at[pl.ds(0, 2)], window_ref.at[pl.ds(0, 2)], window_sem.at[1]
    )
    out_window.start()
    each_halo(one_on, 4, lambda copy: copy.wait_send())
    each_halo(two_on, 3, lambda copy: copy.wait_send())
    each_halo(middle, 3, lambda copy: copy.wait_send())
    last_direct(lambda copy: copy.wait_send())
    to_partner.wait_send()
    for step in range(4):
        first_up(step).wait_send()
        first_down(step).wait_send()
        second_up(step).wait_send()
        second_down(step).wait_send()
        pass_on(0, step).wait_send()
        pass_on(1, step).wait_send()
    for one in (out_own, out_beside, out_across, out_corner, out_mine, out_window):
        one.wait()


def gather_and_project(tokens, in_gain, raw_queries, w_key, w_value, q_gain, k_gain, cosine, sine):
    rows, depth = tokens.shape
    shard = rows * 4
    cols = w_key.shape[1]
    bf = jnp.bfloat16
    vmem = pl.BlockSpec(memory_space=pltpu.VMEM)
    anywhere = pl.BlockSpec(memory_space=pl.ANY)
    outside = pl.BlockSpec(memory_space=pltpu.HBM)
    dma = pltpu.SemaphoreType.DMA
    return pl.pallas_call(
        gather_kernel,
        out_shape=[
            jax.ShapeDtypeStruct((shard, depth), bf),
            jax.ShapeDtypeStruct(raw_queries.shape, bf),
            jax.ShapeDtypeStruct((shard, cols), jnp.float32),
            jax.ShapeDtypeStruct((3, shard, 2 * cols), bf),
        ],
        in_specs=[outside, vmem, outside] + [vmem] * 4 + [outside] * 2,
        out_specs=[anywhere, vmem, vmem, anywhere],
        scratch_shapes=[
            pltpu.VMEM((shard, depth), bf),
            pltpu.VMEM((rows // 2, depth), bf),
            pltpu.VMEM((rows // 2, depth), bf),
            pltpu.VMEM((depth, 2 * cols), bf),
            pltpu.VMEM((3, shard, 2 * cols), bf),
            pltpu.VMEM((rows, depth), bf),
            pltpu.VMEM(raw_queries.shape, bf),
            pltpu.VMEM((shard, 2 * cols), bf),
            pltpu.VMEM((1, depth), jnp.float32),
            dma((4,)),
            dma((4,)),
            dma((2,)),
            dma((2, 4)),
            dma((2, 4)),
            dma((2, 4)),
            dma((2, 4)),
            dma((1,)),
            dma((1,)),
            dma((2, 4)),
            dma((2, 4)),
            dma((2, 18)),
            dma((2, 18)),
            dma((18,)),
            dma((18,)),
        ],
        compiler_params=pltpu.CompilerParams(
            collective_id=2, has_side_effects=True, vmem_limit_bytes=57 * 1024 * 1024
        ),
        cost_estimate=pl.CostEstimate(
            flops=3_000_000_000, bytes_accessed=150_000_000, transcendentals=0
        ),
        name="gather_and_project",
    )(tokens, in_gain.reshape(depth // 128, 128), raw_queries, q_gain[None, :], k_gain[None, :], cosine, sine, w_key, w_value)


def unturn(values, cosine, sine):
    return values * cosine - pltpu.roll(values, values.shape[-1] // 2, 1) * sine


def norm_back(grad, values, gain):
    scale = lax.rsqrt(jnp.mean(values * values, axis=1, keepdims=True) + EPSILON)
    unit = values * scale
    inner = grad * gain
    return scale * (inner - unit * jnp.mean(inner * unit, axis=1, keepdims=True))


def attend_kernel(
    query_ref, window_ref, out_grad_hbm, low_ref, raw_hbm, raw_key_ref, cos_ref, sin_ref, q_gain_ref, k_gain_ref,
    grad_query_ref, grad_kv_ref,
    exps, along, totals, query_total, parts, returned, out_grad_ref, raw_ref, passing,
    send_sem, recv_sem, middle_send, middle_recv, load_sem, chain_send, chain_recv, sum_send, sum_recv,
):
    shard = query_ref.shape[0]
    head_size = q_gain_ref.shape[1]
    kv_heads = raw_key_ref.shape[1] // head_size
    group_size = query_ref.shape[1] // raw_key_ref.shape[1]
    tile = shard // 2
    reach = 2 * shard
    place = lax.axis_index("seq")
    member = lax.axis_index("tp")
    count = lax.axis_size("seq")
    x = lax.rem(place, WIDE)

    def in_row(of, xs):
        return (of // WIDE * WIDE + xs, member)

    left, right = lax.rem(x + WIDE - 1, WIDE), lax.rem(x + 1, WIDE)
    later = (lax.rem(place + 1, count), member)
    earlier = (lax.rem(place + count - 1, count), member)
    middle_to = in_row(lax.rem(place + count - 2, count), right)
    middle_from = (lax.rem(place // WIDE * WIDE + right + 2, count), member)
    row_left, row_right = in_row(place, left), in_row(place, right)
    load_grads = pltpu.make_async_copy(out_grad_hbm, out_grad_ref, load_sem.at[0])
    load_grads.start()
    load_raw = pltpu.make_async_copy(raw_hbm, raw_ref, load_sem.at[1])
    load_raw.start()
    barrier = pltpu.get_barrier_semaphore()
    for other in [later, earlier, middle_to, middle_from, row_left, row_right]:
        pl.semaphore_signal(barrier, inc=1, device_id=other, device_id_type=MESH_IDS)

    totals[...] = jnp.zeros_like(totals)

    def across(left, right):
        return lax.dot_general(left, right, (((1,), (1,)), ((), ())), preferred_element_type=jnp.float32)

    def back(window, head):
        return pltpu.make_async_remote_copy(
            src_ref=parts.at[window, head] if window == 1 else passing.at[head],
            dst_ref=returned.at[window, head],
            send_sem=send_sem.at[window, head],
            recv_sem=recv_sem.at[window, head],
            device_id=earlier if window == 1 else row_right,
            device_id_type=MESH_IDS,
        )

    def middle(head):
        return pltpu.make_async_remote_copy(
            src_ref=parts.at[0, head],
            dst_ref=passing.at[head],
            send_sem=middle_send.at[head],
            recv_sem=middle_recv.at[head],
            device_id=middle_to,
            device_id_type=MESH_IDS,
        )

    last = kv_heads - 1

    def chain(piece):
        at = pl.ds(piece * tile, tile)
        return pltpu.make_async_remote_copy(
            src_ref=parts.at[0, last, at],
            dst_ref=passing.at[last, at],
            send_sem=chain_send.at[piece],
            recv_sem=chain_recv.at[piece],
            device_id=earlier,
            device_id_type=MESH_IDS,
        )

    def summed(piece):
        at = pl.ds(piece * tile, tile)
        return pltpu.make_async_remote_copy(
            src_ref=parts.at[1, last, at],
            dst_ref=returned.at[1, last, at],
            send_sem=sum_send.at[piece],
            recv_sem=sum_recv.at[piece],
            device_id=earlier,
            device_id_type=MESH_IDS,
        )

    load_grads.wait()
    load_raw.wait()
    for head in range(kv_heads):
        key_lanes = slice(head * head_size, (head + 1) * head_size)
        value_lanes = slice((kv_heads + head) * head_size, (kv_heads + head + 1) * head_size)
        lanes = [
            slice((head * group_size + member_of) * head_size, (head * group_size + member_of + 1) * head_size)
            for member_of in range(group_size)
        ]

        def half(step, carry):
            begin = pl.multiple_of(step * tile, tile)
            rows = pl.ds(begin, tile)
            queries = jnp.concatenate([query_ref[rows, at] for at in lanes], axis=0)
            grads = jnp.concatenate([out_grad_ref[rows, at] for at in lanes], axis=0)
            low = low_ref[step]
            low = jnp.concatenate([low] * group_size, axis=1)
            width = group_size * tile
            high = lax.broadcasted_iota(jnp.int32, (1, tile), 1) + (reach + begin)
            high = jnp.concatenate([high] * group_size, axis=1)

            inner_key = lax.broadcasted_iota(jnp.int32, (tile, width), 0)

            def scores(index, stats, diagonal=False):
                total, delta = stats
                first = pl.multiple_of(begin + index * tile, tile)
                key_rows = pl.ds(first, tile)
                score = across(window_ref[key_rows, key_lanes], queries)
                partial = across(window_ref[key_rows, value_lanes], grads)
                allowed = inner_key >= low - first
                if diagonal:
                    allowed = allowed & (inner_key <= high - first)
                value = jnp.where(allowed, jnp.exp(score), 0.0)
                at = pl.ds(pl.multiple_of(index * tile, tile), tile)
                exps[at, :] = value
                along[at, :] = partial
                total = total + jnp.sum(value, axis=0, keepdims=True)
                delta = delta + jnp.sum(value * partial, axis=0, keepdims=True)
                return total, delta

            nothing = jnp.zeros((1, width), jnp.float32)
            stats = lax.fori_loop(0, reach // tile, scores, (nothing, nothing))
            total, delta = scores(reach // tile, stats, diagonal=True)
            inverse = 1.0 / total
            delta = delta * inverse
            query_total[...] = jnp.zeros_like(query_total)

            def slopes(index, carry):
                key_rows = pl.ds(pl.multiple_of(begin + index * tile, tile), tile)
                at = pl.ds(pl.multiple_of(index * tile, tile), tile)
                probs = exps[at, :] * inverse
                slope = (probs * (along[at, :] - delta)).astype(jnp.bfloat16)
                query_total[...] += contract_first(window_ref[key_rows, key_lanes], slope)
                totals[key_rows, key_lanes] += jnp.dot(slope, queries, preferred_element_type=jnp.float32)
                totals[key_rows, value_lanes] += jnp.dot(
                    probs.astype(jnp.bfloat16), grads, preferred_element_type=jnp.float32
                )
                return carry

            lax.fori_loop(0, reach // tile + 1, slopes, 0)
            flipped = query_total[...].T
            for member_of, at in enumerate(lanes):
                grad = flipped[member_of * tile : (member_of + 1) * tile] * QUERY_SCALE
                grad = unturn(grad, cos_ref[rows, :], sin_ref[rows, :])
                values = raw_ref[rows, at].astype(jnp.float32)
                grad_query_ref[rows, at] = norm_back(grad, values, q_gain_ref[...]).astype(jnp.bfloat16)
            return carry

        lax.fori_loop(0, 2, half, 0)
        for window in range(2 if head < last else 1):
            rows = slice(window * shard, (window + 1) * shard)
            parts[window, head, :, :head_size] = totals[rows, key_lanes].astype(jnp.bfloat16)
            parts[window, head, :, head_size:] = totals[rows, value_lanes].astype(jnp.bfloat16)
        if head == 0:
            pl.semaphore_wait(barrier, 6)
        if head < last:
            middle(head).start()
            back(1, head).start()
        else:
            chain(0).start()
            chain(1).start()

    for head in range(last):
        middle(head).wait_recv()
        back(0, head).start()
    for piece in range(2):
        chain(piece).wait_recv()
        here = slice(piece * tile, (piece + 1) * tile)
        rows = slice(shard + piece * tile, shard + (piece + 1) * tile)
        lanes = slice(last * head_size, (last + 1) * head_size)
        parts[1, last, here, :head_size] = (
            totals[rows, lanes] + passing[last, here, :head_size].astype(jnp.float32)
        ).astype(jnp.bfloat16)
        lanes = slice((kv_heads + last) * head_size, (kv_heads + last + 1) * head_size)
        parts[1, last, here, head_size:] = (
            totals[rows, lanes] + passing[last, here, head_size:].astype(jnp.float32)
        ).astype(jnp.bfloat16)
        summed(piece).start()
    own = slice(reach, reach + shard)
    for head in range(kv_heads):
        key_lanes = slice(head * head_size, (head + 1) * head_size)
        value_lanes = slice((kv_heads + head) * head_size, (kv_heads + head + 1) * head_size)
        if head < last:
            for window in range(2):
                back(window, head).wait_recv()
        else:
            summed(0).wait_recv()
            summed(1).wait_recv()
        key_grad = totals[own, key_lanes]
        value_grad = totals[own, value_lanes]
        for window in (1, 0) if head < last else (1,):
            key_grad = key_grad + returned[window, head, :, :head_size].astype(jnp.float32)
            value_grad = value_grad + returned[window, head, :, head_size:].astype(jnp.float32)
        grad_kv_ref[:, value_lanes] = value_grad.astype(jnp.bfloat16)
        key_grad = unturn(key_grad, cos_ref[...], sin_ref[...])
        grad_kv_ref[:, key_lanes] = norm_back(key_grad, raw_key_ref[:, key_lanes], k_gain_ref[...]).astype(
            jnp.bfloat16
        )
    for head in range(last):
        middle(head).wait_send()
        for window in range(2):
            back(window, head).wait_send()
    for piece in range(2):
        chain(piece).wait_send()
        summed(piece).wait_send()


def attend_back(query_rot, window, out_grad, low, raw_queries, raw_keys, cosine, sine, q_gain, k_gain):
    shard = query_rot.shape[0]
    head_size = q_gain.shape[0]
    kv_heads = raw_keys.shape[1] // head_size
    group_size = query_rot.shape[1] // raw_keys.shape[1]
    tile = shard // 2
    width = group_size * tile
    vmem = pl.BlockSpec(memory_space=pltpu.VMEM)
    outside = pl.BlockSpec(memory_space=pltpu.HBM)
    return pl.pallas_call(
        attend_kernel,
        out_shape=[
            jax.ShapeDtypeStruct(query_rot.shape, jnp.bfloat16),
            jax.ShapeDtypeStruct((shard, 2 * raw_keys.shape[1]), jnp.bfloat16),
        ],
        in_specs=[vmem, vmem, outside, vmem, outside] + [vmem] * 5,
        out_specs=[vmem] * 2,
        scratch_shapes=[
            pltpu.VMEM((2 * shard + tile, width), jnp.float32),
            pltpu.VMEM((2 * shard + tile, width), jnp.float32),
            pltpu.VMEM((3 * shard, 2 * raw_keys.shape[1]), jnp.float32),
            pltpu.VMEM((head_size, width), jnp.float32),
            pltpu.VMEM((2, kv_heads, shard, 2 * head_size), jnp.bfloat16),
            pltpu.VMEM((2, kv_heads, shard, 2 * head_size), jnp.bfloat16),
            pltpu.VMEM(query_rot.shape, jnp.bfloat16),
            pltpu.VMEM(query_rot.shape, jnp.bfloat16),
            pltpu.VMEM((kv_heads, shard, 2 * head_size), jnp.bfloat16),
            pltpu.SemaphoreType.DMA((2, kv_heads)),
            pltpu.SemaphoreType.DMA((2, kv_heads)),
            pltpu.SemaphoreType.DMA((kv_heads,)),
            pltpu.SemaphoreType.DMA((kv_heads,)),
            pltpu.SemaphoreType.DMA((2,)),
            pltpu.SemaphoreType.DMA((2,)),
            pltpu.SemaphoreType.DMA((2,)),
            pltpu.SemaphoreType.DMA((2,)),
            pltpu.SemaphoreType.DMA((2,)),
        ],
        compiler_params=pltpu.CompilerParams(
            collective_id=3, has_side_effects=True, vmem_limit_bytes=52 * 1024 * 1024
        ),
        cost_estimate=pl.CostEstimate(
            flops=8_000_000_000, bytes_accessed=100_000_000, transcendentals=3_000_000
        ),
        name="attend_back",
    )(
        query_rot, window.reshape(3 * shard, window.shape[2]), out_grad, low, raw_queries, raw_keys,
        cosine, sine, q_gain[None, :], k_gain[None, :],
    )


def finish_kernel(
    gathered_ref, grad_ref, w_key_ref, w_value_ref, tokens_ref, gain_blocks,
    key_out, value_out, grad_x_ref,
    held, weights, tokens, gain_ref, total_own, corner_out, corner_in, beside_out, beside_in, cross_out, cross_in,
    relay_up, relay_down,
    key_term, value_term, key_send, order, value_total, key_next, value_next, last_send, last_recv,
    *rest,
):
    bufs_a, bufs_b, bufs_c, bufs_d = rest[0:6], rest[6:12], rest[12:18], rest[18:24]
    sems = rest[24:34]
    load_sem, weight_sem, pair_send, pair_recv, relay_send, relay_recv, cross_send, cross_recv = rest[34:42]
    corner_send, corner_recv = rest[42:]
    depth = gain_ref.shape[1]
    block = tokens_ref.shape[0]
    rows = key_out.shape[0]
    cols = key_out.shape[1]
    half = block // 2
    piece = half // 4
    big, mid = 16 * rows, 4 * rows
    split_big = big // 2
    split_mid = mid // 2 + mid // 2 % 16
    slab = 768 if depth % 768 == 0 else 128
    strip = 384 if depth % 384 == 0 else 128
    place = lax.axis_index("seq")
    member = lax.axis_index("tp")
    core = lax.rem(member, 2)
    upper = member // 2
    x = lax.rem(place, 4)
    z = lax.rem(place // 4, 4)
    y = place // 16
    height = upper * 4 + z

    def device(ys, zs, xs):
        return ((ys * 4 + zs) * 4 + xs, member)

    def along_z(by):
        other = lax.rem(height + by, 8)
        return ((y * 4 + lax.rem(other, 4)) * 4 + x, other // 4 * 2 + core)

    def remote(source, target, send_sem, recv_sem, to):
        return pltpu.make_async_remote_copy(
            src_ref=source,
            dst_ref=target,
            send_sem=send_sem,
            recv_sem=recv_sem,
            device_id=to,
            device_id_type=MESH_IDS,
        )

    def weight_load(step):
        at = pl.ds(pl.multiple_of(step * slab, slab), slab)
        return (
            pltpu.make_async_copy(w_key_ref.at[at], weights.at[at, pl.ds(0, cols)], weight_sem.at[0, step]),
            pltpu.make_async_copy(w_value_ref.at[at], weights.at[at, pl.ds(cols, cols)], weight_sem.at[1, step]),
        )

    for step in range(depth // slab):
        for one in weight_load(step):
            one.start()
    load_held = pltpu.make_async_copy(gathered_ref, held, load_sem.at[0])
    load_held.start()
    load_tokens = pltpu.make_async_copy(tokens_ref, tokens, load_sem.at[1])
    load_tokens.start()

    z_up, z_down = along_z(2), along_z(6)
    partner = (place, upper * 2 + 1 - core)
    x_up, x_down = device(y, z, lax.rem(x + 1, 4)), device(y, z, lax.rem(x + 3, 4))
    y_up, y_down = device(lax.rem(y + 1, 4), z, x), device(lax.rem(y + 3, 4), z, x)
    z_others = [device(y, lax.rem(z + d, 4), x) for d in (1, 2, 3)]
    barrier = pltpu.get_barrier_semaphore()
    for other in [z_up, z_down, partner, x_up, x_down, y_up, y_down] + z_others:
        pl.semaphore_signal(barrier, inc=1, device_id=other, device_id_type=MESH_IDS)

    own = pl.multiple_of(member * block, block)
    beside = pl.multiple_of((upper * 2 + 1 - core) * block, block)
    across = pl.multiple_of(((1 - upper) * 2 + core) * block, block)
    corner = pl.multiple_of(((1 - upper) * 2 + 1 - core) * block, block)

    def part(begin, store, first=False):
        grads = grad_ref[pl.ds(begin, block), :]

        def one_slab(step, carry):
            if first:
                for one in weight_load(step):
                    one.wait()
            at = pl.ds(pl.multiple_of(step * slab, slab), slab)
            store(at, contract_last(grads, weights[at, :]))
            return carry

        lax.fori_loop(0, depth // slab, one_slab, 0)

    def store_corner(at, value):
        corner_out[:, at] = value.astype(jnp.bfloat16)

    part(corner, store_corner, first=True)
    pl.semaphore_wait(barrier, 10)

    def rows_at(side, step):
        return pl.ds(side * half + step * piece, piece)

    pieces = [(side, step) for step in range(4) for side in (0, 1)]
    send_corner = {
        (side, step): remote(
            corner_out.at[rows_at(side, step)], corner_in.at[rows_at(side, step)],
            corner_send.at[side, step], corner_recv.at[side, step], partner,
        )
        for side, step in pieces
    }
    for one in pieces:
        send_corner[one].start()

    def store_total(at, value):
        total_own[:, at] = value

    part(across, store_total)
    def small(step):
        return pl.ds(step * piece, piece)

    first = [
        [
            remote(cross_out.at[rows_at(0, step)], relay_up.at[small(step)], relay_send.at[0, step], relay_recv.at[0, step], z_up),
            remote(cross_out.at[rows_at(1, step)], relay_down.at[small(step)], relay_send.at[1, step], relay_recv.at[1, step], z_down),
        ]
        for step in range(4)
    ]
    second = [
        [
            remote(relay_up.at[small(step)], cross_in.at[rows_at(0, step)], cross_send.at[0, step], cross_recv.at[0, step], z_up),
            remote(relay_down.at[small(step)], cross_in.at[rows_at(1, step)], cross_send.at[1, step], cross_recv.at[1, step], z_down),
        ]
        for step in range(4)
    ]
    for side, step in pieces:
        send_corner[side, step].wait_recv()
        at = rows_at(side, step)
        cross_out[at, :] = (total_own[at, :] + corner_in[at, :].astype(jnp.float32)).astype(jnp.bfloat16)
        first[step][side].start()

    def relay(step):
        for side in (0, 1):
            first[step][side].wait_recv()
            second[step][side].start()

    load_held.wait()

    def strips(step, carry):
        at = pl.ds(pl.multiple_of(step * strip, strip), strip)
        result = contract_first(held[:, at], grad_ref[...])
        key_term[at, :] = result[:, :cols]
        value_term[at, :] = result[:, cols:].astype(jnp.bfloat16)
        return carry

    lax.fori_loop(0, depth // strip, strips, 0)

    def finish_b1(total):
        for quarter in range(4):
            at = pl.ds(quarter * mid, mid)
            value_total[at, :] = total(at)
        for xs in range(4):
            for zs in range(4):
                order[zs * rows : zs * rows + rows, :] = value_total[
                    zs * mid + xs * rows : zs * mid + xs * rows + rows, :
                ]
            value_next[xs] = order[...].astype(jnp.bfloat16)

    second_b = ring_sum(
        lambda t: value_term.at[pl.ds(pl.multiple_of(t * big, 16), big)],
        big, split_big, y, y_up, y_down, bufs_b, sems[2:4], finish_b1,
    )

    for ys in range(4):
        for xs in range(4):
            for zs in range(4):
                begin = ((ys * 4 + zs) * 4 + xs) * rows
                order[zs * rows : zs * rows + rows, :] = key_term[begin : begin + rows, :]
            key_send[xs, ys * mid : ys * mid + mid, :] = order[...].astype(jnp.bfloat16)

    def finish_a1(total):
        for quarter in range(4):
            at = pl.ds(quarter * mid, mid)
            key_next[quarter] = total(at).astype(jnp.bfloat16)

    second_a = ring_sum(
        lambda t: key_send.at[t],
        big, split_big, x, x_up, x_down, bufs_a, sems[0:2], finish_a1,
    )
    relay(0)

    def store_beside(at, value):
        beside_out[:, at] = value.astype(jnp.bfloat16)

    part(beside, store_beside)
    send_beside = remote(beside_out, beside_in, pair_send.at[1], pair_recv.at[1], partner)
    send_beside.start()
    part(own, store_total)
    relay(1)
    third_b = second_b()
    third_a = second_a()
    relay(2)
    drain_b = third_b()

    def finish_last(at):
        def finish(total):
            order[...] = total(pl.ds(0, mid))
            for zs in range(4):
                last_send[zs, 0:rows, at : at + cols] = order[
                    zs * rows : zs * rows + rows, :
                ].astype(jnp.bfloat16)
                last_send[zs, rows:, at : at + cols] = jnp.zeros(
                    (last_send.shape[1] - rows, cols), jnp.bfloat16
                )

        return finish

    second_d = ring_sum(
        lambda t: value_next.at[t],
        mid, split_mid, x, x_up, x_down, bufs_d, sems[6:8], finish_last(cols),
    )
    relay(3)
    drain_a = third_a()
    second_c = ring_sum(
        lambda t: key_next.at[t],
        mid, split_mid, y, y_up, y_down, bufs_c, sems[4:6], finish_last(0),
    )
    third_d = second_d()
    third_c = second_c()
    drain_d = third_d()
    drain_c = third_c()
    copies = []
    for d in (1, 2, 3):
        one = remote(
            last_send.at[lax.rem(z + d, 4)], last_recv.at[d - 1], sems[8].at[d - 1], sems[9].at[d - 1], z_others[d - 1]
        )
        one.start()
        copies.append(one)

    one_row(gain_blocks, gain_ref)
    load_tokens.wait()
    send_beside.wait_recv()
    for step in range(4):
        for side in (0, 1):
            second[step][side].wait_recv()
            at = rows_at(side, step)
            grad = (
                total_own[at, :] + beside_in[at, :].astype(jnp.float32) + cross_in[at, :].astype(jnp.float32)
            )
            grad_x_ref[at, :] = norm_back(grad, tokens[at, :].astype(jnp.float32), gain_ref[...]).astype(
                jnp.bfloat16
            )

    for one in copies:
        one.wait_recv()
    total = last_send[z, 0:rows, :].astype(jnp.float32)
    for d in range(3):
        total = total + last_recv[d, 0:rows, :].astype(jnp.float32)
    key_out[...] = total[:, 0:cols]
    value_out[...] = total[:, cols:]
    for one in copies:
        one.wait_send()
    for drain in (drain_a, drain_b, drain_c, drain_d):
        drain()
    for one in pieces:
        send_corner[one].wait_send()
    send_beside.wait_send()
    for pair in first + second:
        for one in pair:
            one.wait_send()


def finish(gathered, grad_kv, w_key, w_value, tokens, in_gain):
    shard, depth = gathered.shape
    block = tokens.shape[0]
    cols = w_key.shape[1]
    rows = depth // 64
    big, mid = 16 * rows, 4 * rows
    split_big = big // 2
    split_mid = mid // 2 + mid // 2 % 16
    padded = (rows + 15) // 16 * 16
    slabs = depth // (768 if depth % 768 == 0 else 128)
    bf = jnp.bfloat16
    dma = pltpu.SemaphoreType.DMA
    vmem = pl.BlockSpec(memory_space=pltpu.VMEM)
    outside = pl.BlockSpec(memory_space=pltpu.HBM)

    def bufs(size, split):
        return [
            pltpu.VMEM((split, cols), bf),
            pltpu.VMEM((size - split, cols), bf),
            pltpu.VMEM((split, cols), bf),
            pltpu.VMEM((size - split, cols), bf),
            pltpu.VMEM((size, cols), bf),
            pltpu.VMEM((size, cols), bf),
        ]

    return pl.pallas_call(
        finish_kernel,
        out_shape=[
            jax.ShapeDtypeStruct((rows, cols), jnp.float32),
            jax.ShapeDtypeStruct((rows, cols), jnp.float32),
            jax.ShapeDtypeStruct((block, depth), bf),
        ],
        in_specs=[outside, vmem, outside, outside, outside, vmem],
        out_specs=[vmem] * 3,
        scratch_shapes=[
            pltpu.VMEM((shard, depth), bf),
            pltpu.VMEM((depth, 2 * cols), bf),
            pltpu.VMEM((block, depth), bf),
            pltpu.VMEM((1, depth), jnp.float32),
            pltpu.VMEM((block, depth), jnp.float32),
        ]
        + [pltpu.VMEM((block, depth), bf)] * 6
        + [pltpu.VMEM((block // 2, depth), bf)] * 2
        + [
            pltpu.VMEM((depth, cols), jnp.float32),
            pltpu.VMEM((depth, cols), bf),
            pltpu.VMEM((4, big, cols), bf),
            pltpu.VMEM((mid, cols), jnp.float32),
            pltpu.VMEM((big, cols), jnp.float32),
            pltpu.VMEM((4, mid, cols), bf),
            pltpu.VMEM((4, mid, cols), bf),
            pltpu.VMEM((4, padded, 2 * cols), bf),
            pltpu.VMEM((3, padded, 2 * cols), bf),
        ]
        + bufs(big, split_big)
        + bufs(big, split_big)
        + bufs(mid, split_mid)
        + bufs(mid, split_mid)
        + [dma((6,))] * 8
        + [dma((3,))] * 2
        + [dma((2,)), dma((2, slabs)), dma((2,)), dma((2,))]
        + [dma((2, 4))] * 6,
        compiler_params=pltpu.CompilerParams(
            collective_id=1, has_side_effects=True, vmem_limit_bytes=51 * 1024 * 1024
        ),
        cost_estimate=pl.CostEstimate(
            flops=6_000_000_000, bytes_accessed=150_000_000, transcendentals=0
        ),
        name="finish",
    )(gathered, grad_kv, w_key, w_value, tokens, in_gain.reshape(depth // 128, 128))


def shards(tokens, in_gain, raw_queries, w_key, w_value, q_gain, k_gain, doc_lengths, out_grad):
    head_size = q_gain.shape[0]
    shard_rows = tokens.shape[0] * lax.axis_size("tp")
    reach = 2 * shard_rows
    first_row = lax.axis_index("seq") * shard_rows
    positions = first_row + jnp.arange(shard_rows, dtype=jnp.int32)
    begins = doc_begin(doc_lengths, positions)
    lowest = jnp.maximum(begins, positions - (WINDOW - 1))
    low = (lowest - (first_row - reach)).reshape(2, 1, shard_rows // 2)
    cosine, sine = angle_tables(positions - begins, head_size)
    gathered, query_rot, raw_keys, window = gather_and_project(
        tokens, in_gain, raw_queries, w_key, w_value, q_gain, k_gain, cosine, sine
    )
    grad_queries, grad_kv = attend_back(
        query_rot, window, out_grad, low, raw_queries, raw_keys, cosine, sine, q_gain, k_gain
    )
    grad_wk, grad_wv, grad_x = finish(gathered, grad_kv, w_key, w_value, tokens, in_gain)
    return (grad_x, grad_queries, grad_wk, grad_wv)


def solution(mesh):
    placed = (
        P(("seq", "tp"), None),
        P(),
        P("seq", "tp"),
        P(None, "tp"),
        P(None, "tp"),
        P(),
        P(),
        P(),
        P("seq", "tp"),
    )
    return jax.shard_map(
        shards,
        mesh=mesh,
        in_specs=placed,
        out_specs=(P(("seq", "tp"), None), P("seq", "tp"), P("seq", "tp"), P("seq", "tp")),
        check_vma=False,
    )
```
